32 devices in a mesh: gx: 2 (over x), gy: 2 (over y), gz: 8 (over z, core).
Axes of the slice: x: 2, y: 2, z: 4, core: 2. Of those that a mesh axis runs over, the one named last changes fastest.
Arguments:
- corner_speed_prior: float32 [3, 16, 128, 128], P(None, 'gx', 'gz', 'gy'), may hold values from -6 to 6
- brick_stress_tensor_now: float32 [6, 16, 128, 128], P(None, 'gx', 'gz', 'gy'), may hold values from -4 to 4
- compact_onset_strength: float32 [16, 128, 128], P('gx', 'gz', 'gy'), may hold values from 0.3 to 3
- corner_weights_diagonal: float32 [16, 128, 128], P('gx', 'gz', 'gy'), may hold values from 0.5 to 4
- substance_labels: int32 [2, 16, 16], P('gx', None, 'gy'), may hold values from 0 to 2, as said below
- brick_warmth_prior: float32 [16, 128, 128], P('gx', ('gy', 'gz')), may hold values from -6 to 6
- caloric_capacity_per_timestep: float32 [16, 128, 128], P('gx', ('gy', 'gz')), may hold values from 0.5 to 4
Outputs:
- corner_speed_later: float32 [3, 16, 128, 128], P(None, 'gx', 'gz', 'gy')
- projected_brick_stress_tensor: float32 [6, 16, 128, 128], P(None, 'gx', 'gz', 'gy')
- diffused_kelvin_field: float32 [16, 128, 128], P('gx', ('gy', 'gz'))
The draws below stay inside these ranges and needn't reach their ends.
Inputs may be any that keep to these rules, and one draw needn't show every extreme that they name: `substance_labels`: among the 2 blocks of one mechanics device that share one second-dimension block index, at most 1 are powder (2), and in every draw some such group has exactly 1.
All inputs are finite; a program needn't handle non-finite values.
Results may differ from the reference program's by a relative error of at most 0.0003.
Values sent between devices are 32-bit elements; how exact they have to be, the bound alone decides.
No kernel may reach another device: no remote copies, remote signals or barrier semaphores. Data moves between devices by JAX's collectives and lax.ppermute only.
A program may use at most 64 MiB of HBM per device.

```python
import math
import jax
import jax.numpy as jnp
from jax import lax

BS = 8
XB = 1
ZB = 2
SWEEPS = 3
BRICKS_ALONG_ONE = 16
BRICKS_ALONG_TWO = 128
BRICKS_ALONG_RAM = 128
NXB = 2
NYB = 16
NZB = 16
PMAX = 1


def draw_substance_labels(key, part):
    group_x = NXB // XB
    group_z = NZB // ZB
    inner = XB * ZB
    key_count = jax.random.fold_in(key, 11)
    key_score = jax.random.fold_in(key, 12)
    key_other = jax.random.fold_in(key, 13)
    count = jax.random.randint(key_count, (group_x, NYB, group_z), 0, PMAX + 1)
    count = count.at[0, 0, 0].set(PMAX)
    scores = jax.random.randint(key_score, (group_x, NYB, group_z, inner), 0, 1 << 20) * inner
    scores = scores + jnp.arange(inner, dtype=jnp.int32)
    ranks = jnp.argsort(jnp.argsort(scores, axis=-1), axis=-1)
    powder = ranks < count[..., None]
    others = jax.random.randint(key_other, (group_x, NYB, group_z, inner), 0, 2)
    labels = jnp.where(powder, 2, others).astype(jnp.int32)
    labels = labels.reshape(group_x, NYB, group_z, XB, ZB)
    labels = jnp.transpose(labels, (0, 3, 2, 4, 1))
    return labels.reshape(NXB, NZB, NYB)


def steps_of(rng, dims, pieces, low, top_value):
    level = 1.0
    for axis_at, parts in pieces:
        steps = jax.random.uniform(jax.random.fold_in(jax.random.fold_in(rng, 6), axis_at), (parts,), jnp.float32, low / len(pieces), top_value / len(pieces))
        level = level * jnp.repeat(jnp.exp(steps), dims[axis_at] // parts).reshape((-1,) + (1,) * (len(dims) - 1 - axis_at))
    return level


def bell_draw(stream_key, shape, spread, most, pieces=(), kind=jnp.bfloat16):
    gain = steps_of(stream_key, shape, pieces, -0.22, 0.18) if pieces else 1.0
    entries = jax.random.normal(stream_key, shape, jnp.float32) * spread * gain
    return jnp.minimum(jnp.maximum(entries, -most), most).astype(kind)


def setup_inputs(seed: int = 0) -> dict:
    streams_of = jax.random.split(jax.random.key(seed), 8)
    corner_speed_prior = bell_draw(streams_of[0], (3, BRICKS_ALONG_ONE, BRICKS_ALONG_RAM, BRICKS_ALONG_TWO), 1.0, 6.0, ((1, 2), (2, 8), (3, 2)), jnp.float32)
    brick_stress_tensor_now = bell_draw(streams_of[1], (6, BRICKS_ALONG_ONE, BRICKS_ALONG_RAM, BRICKS_ALONG_TWO), 0.6, 4.0, ((1, 2), (2, 8), (3, 2)), jnp.float32)
    compact_onset_strength = jnp.clip(jnp.exp(math.log(3.0) - 2.3025851 * jax.random.uniform(streams_of[2], (BRICKS_ALONG_ONE, BRICKS_ALONG_RAM, BRICKS_ALONG_TWO), jnp.float32) ** steps_of(streams_of[2], (BRICKS_ALONG_ONE, BRICKS_ALONG_RAM, BRICKS_ALONG_TWO), ((0, 2), (1, 8), (2, 2)), -0.2, 0.2)), 0.3, 3.0)
    corner_weights_diagonal = jnp.clip(jnp.exp(math.log(4.0) - 2.0794415 * jax.random.uniform(streams_of[3], (BRICKS_ALONG_ONE, BRICKS_ALONG_RAM, BRICKS_ALONG_TWO), jnp.float32) ** steps_of(streams_of[3], (BRICKS_ALONG_ONE, BRICKS_ALONG_RAM, BRICKS_ALONG_TWO), ((0, 2), (1, 8), (2, 2)), -0.2, 0.2)), 0.5, 4.0)
    substance_labels = draw_substance_labels(jax.random.fold_in(streams_of[7], 71), 0)
    brick_warmth_prior = bell_draw(streams_of[5], (BRICKS_ALONG_ONE, BRICKS_ALONG_TWO, BRICKS_ALONG_RAM), 1.0, 6.0, ((0, 2), (1, 16)), jnp.float32)
    caloric_capacity_per_timestep = jnp.clip(jnp.exp(math.log(4.0) - 2.0794415 * jax.random.uniform(streams_of[6], (BRICKS_ALONG_ONE, BRICKS_ALONG_TWO, BRICKS_ALONG_RAM), jnp.float32) ** steps_of(streams_of[6], (BRICKS_ALONG_ONE, BRICKS_ALONG_TWO, BRICKS_ALONG_RAM), ((0, 2), (1, 16)), -0.2, 0.2)), 0.5, 4.0)
    return dict(corner_speed_prior=corner_speed_prior, brick_stress_tensor_now=brick_stress_tensor_now, compact_onset_strength=compact_onset_strength, corner_weights_diagonal=corner_weights_diagonal, substance_labels=substance_labels, brick_warmth_prior=brick_warmth_prior, caloric_capacity_per_timestep=caloric_capacity_per_timestep)


TIME_STEP = 0.2
VISCOSITY = 0.4
FRICTION = 0.5
TAYLOR_QUINNEY = 0.9
HEAT_SCALE = 5.0
ELASTIC_YIELD = 10000.0
LOWER_BOUND = 0.5
UPPER_BOUND = 16.0

def shifted_diff(values, axis_num):
    extent = values.shape[axis_num]
    return lax.slice_in_dim(values, 1, extent, axis=axis_num) - lax.slice_in_dim(values, 0, extent - 1, axis=axis_num)

def shifted_sum(values, axis_num):
    extent = values.shape[axis_num]
    return lax.slice_in_dim(values, 1, extent, axis=axis_num) + lax.slice_in_dim(values, 0, extent - 1, axis=axis_num)

def spread_blocks(values, width):
    extent_a, extent_b, extent_c = values.shape
    wide = jnp.broadcast_to(values[:, None, :, None, :, None], (extent_a, width, extent_b, width, extent_c, width))
    return wide.reshape(extent_a * width, extent_b * width, extent_c * width)

def moduli(substance_labels):
    shear_mod = jnp.where(substance_labels == 0, 3.0, jnp.where(substance_labels == 1, 2.0, 0.8)).astype(jnp.float32)
    bulk_mod = jnp.where(substance_labels == 0, 5.0, jnp.where(substance_labels == 1, 4.0, 1.2)).astype(jnp.float32)
    return (shear_mod, bulk_mod)

def face_term(element_values, axis_num):
    others = [other for other in (0, 1, 2) if other != axis_num]
    return shifted_diff(shifted_sum(shifted_sum(element_values, others[0]), others[1]), axis_num)

def mechanics(padded, corner_weights_diagonal):
    node_vel = padded[0:3]
    grad_x = 0.25 * shifted_diff(shifted_sum(shifted_sum(node_vel, 2), 3), 1)
    grad_y = 0.25 * shifted_diff(shifted_sum(shifted_sum(node_vel, 1), 3), 2)
    grad_z = 0.25 * shifted_diff(shifted_sum(shifted_sum(node_vel, 1), 2), 3)
    props = padded[3:, :-1, :-1, :-1]
    yield_eff = props[6]
    shear_mod = props[7]
    bulk_mod = props[8]
    strain_xx = TIME_STEP * grad_x[0]
    strain_yy = TIME_STEP * grad_y[1]
    strain_zz = TIME_STEP * grad_z[2]
    strain_xy = TIME_STEP * (0.5 * (grad_y[0] + grad_x[1]))
    strain_yz = TIME_STEP * (0.5 * (grad_z[1] + grad_y[2]))
    strain_xz = TIME_STEP * (0.5 * (grad_z[0] + grad_x[2]))
    volume = strain_xx + strain_yy + strain_zz
    vol_third = volume / 3.0
    trial_xx = props[0] + 2.0 * shear_mod * (strain_xx - vol_third) + bulk_mod * volume
    trial_yy = props[1] + 2.0 * shear_mod * (strain_yy - vol_third) + bulk_mod * volume
    trial_zz = props[2] + 2.0 * shear_mod * (strain_zz - vol_third) + bulk_mod * volume
    trial_xy = props[3] + 2.0 * shear_mod * strain_xy
    trial_yz = props[4] + 2.0 * shear_mod * strain_yz
    trial_xz = props[5] + 2.0 * shear_mod * strain_xz
    pressure = (trial_xx + trial_yy + trial_zz) / 3.0
    dev_xx = trial_xx - pressure
    dev_yy = trial_yy - pressure
    dev_zz = trial_zz - pressure
    second = dev_xx * dev_xx + dev_yy * dev_yy + dev_zz * dev_zz + 2.0 * (trial_xy * trial_xy + trial_yz * trial_yz + trial_xz * trial_xz)
    equivalent = jnp.sqrt(1.5 * second)
    flow_stress = yield_eff + FRICTION * jnp.maximum(-pressure, 0.0)
    excess = equivalent - flow_stress
    active = excess > 0.0
    plastic_rate = jnp.maximum(excess, 0.0) / (3.0 * shear_mod + VISCOSITY / TIME_STEP)
    scale_back = jnp.where(active, 1.0 - 3.0 * shear_mod * plastic_rate / jnp.where(active, equivalent, 1.0), 1.0)
    updated = jnp.stack([pressure + scale_back * dev_xx, pressure + scale_back * dev_yy, pressure + scale_back * dev_zz, scale_back * trial_xy, scale_back * trial_yz, scale_back * trial_xz])
    heat_local = HEAT_SCALE * TAYLOR_QUINNEY * (equivalent - 3.0 * shear_mod * plastic_rate) * plastic_rate
    force_x = face_term(updated[0], 0) + face_term(updated[3], 1) + face_term(updated[5], 2)
    force_y = face_term(updated[3], 0) + face_term(updated[1], 1) + face_term(updated[4], 2)
    force_z = face_term(updated[5], 0) + face_term(updated[4], 1) + face_term(updated[2], 2)
    force = -0.25 * jnp.stack([force_x, force_y, force_z])
    corner_speed_later = node_vel[:, 1:-1, 1:-1, 1:-1] - TIME_STEP * force / corner_weights_diagonal
    return (corner_speed_later, updated[:, 1:, 1:, 1:], heat_local[1:, 1:, 1:])

def stencil(values, padded, matrix_main_entries):
    beside = padded[2:, 1:-1, 1:-1] + padded[:-2, 1:-1, 1:-1]
    beside = beside + padded[1:-1, 2:, 1:-1] + padded[1:-1, :-2, 1:-1]
    beside = beside + padded[1:-1, 1:-1, 2:] + padded[1:-1, 1:-1, :-2]
    return matrix_main_entries * values - beside

def laplacian_action(values, matrix_main_entries):
    return stencil(values, jnp.pad(values, 1), matrix_main_entries)

def reference(corner_speed_prior, brick_stress_tensor_now, compact_onset_strength, corner_weights_diagonal, substance_labels, brick_warmth_prior, caloric_capacity_per_timestep):
    shear_blk, bulk_blk = moduli(substance_labels)
    powder_cells = spread_blocks(substance_labels, BS) == 2
    yield_eff = jnp.where(powder_cells, compact_onset_strength, ELASTIC_YIELD)
    stacked = jnp.concatenate([corner_speed_prior, brick_stress_tensor_now, yield_eff[None], spread_blocks(shear_blk, BS)[None], spread_blocks(bulk_blk, BS)[None]], axis=0)
    padded = jnp.pad(stacked, ((0, 0), (1, 1), (1, 1), (1, 1)))

    def slab(block_index):
        slab_piece = lax.dynamic_slice_in_dim(padded, block_index * BS, BS + 2, 1)
        mass_slab = lax.dynamic_slice_in_dim(corner_weights_diagonal, block_index * BS, BS, 0)
        return mechanics(slab_piece, mass_slab)
    speed_pieces, load_tensor_pieces, caloric_pieces = lax.map(slab, jnp.arange(BRICKS_ALONG_ONE // BS, dtype=jnp.int32))
    corner_speed_later = jnp.transpose(speed_pieces, (1, 0, 2, 3, 4)).reshape(3, BRICKS_ALONG_ONE, BRICKS_ALONG_RAM, BRICKS_ALONG_TWO)
    projected_brick_stress_tensor = jnp.transpose(load_tensor_pieces, (1, 0, 2, 3, 4)).reshape(6, BRICKS_ALONG_ONE, BRICKS_ALONG_RAM, BRICKS_ALONG_TWO)
    plastic_work_heating_rise = jnp.transpose(caloric_pieces.reshape(BRICKS_ALONG_ONE, BRICKS_ALONG_RAM, BRICKS_ALONG_TWO), (0, 2, 1))
    center_value = 0.5 * (UPPER_BOUND + LOWER_BOUND)
    half_width = 0.5 * (UPPER_BOUND - LOWER_BOUND)
    ratio_sig = center_value / half_width
    matrix_main_entries = 6.0 + caloric_capacity_per_timestep
    linear_system_target = caloric_capacity_per_timestep * brick_warmth_prior + plastic_work_heating_rise
    implicit_kelvin_result = brick_warmth_prior
    equation_misfit = linear_system_target - laplacian_action(implicit_kelvin_result, matrix_main_entries)
    weight_now = 1.0 / ratio_sig
    search_direction = equation_misfit / center_value
    for sweep_index in range(SWEEPS):
        implicit_kelvin_result = implicit_kelvin_result + search_direction
        if sweep_index + 1 < SWEEPS:
            equation_misfit = equation_misfit - laplacian_action(search_direction, matrix_main_entries)
            weight_next = 1.0 / (2.0 * ratio_sig - weight_now)
            search_direction = weight_next * weight_now * search_direction + 2.0 * weight_next / half_width * equation_misfit
            weight_now = weight_next
    return (corner_speed_later, projected_brick_stress_tensor, implicit_kelvin_result)
```

```python
import jax
import jax.numpy as jnp
from jax import lax
from jax.experimental import pallas as pl
from jax.experimental.pallas import tpu as pltpu
from jax.sharding import PartitionSpec as P

BS = 8
ZB = 2
SWEEPS = 3


TIME_STEP = 0.2
VISCOSITY = 0.4
FRICTION = 0.5
TAYLOR_QUINNEY = 0.9
HEAT_SCALE = 5.0
ELASTIC_YIELD = 10000.0
LOWER_BOUND = 0.5
UPPER_BOUND = 16.0


def extended(cells, sides, width):
    for axis, dim in sides:
        count = lax.axis_size(axis)
        ends = count - 1
        head = lax.slice_in_dim(cells, 0, width, axis=dim)
        tail = lax.slice_in_dim(cells, cells.shape[dim] - width, cells.shape[dim], axis=dim)
        cells = jnp.concatenate(
            [
                lax.ppermute(tail, axis, [(i, (i + 1) % count) for i in range(ends)]),
                cells,
                lax.ppermute(head, axis, [((i + 1) % count, i) for i in range(ends)]),
            ],
            axis=dim,
        )
    return cells


def shifted_diff(values, axis_num):
    extent = values.shape[axis_num]
    return lax.slice_in_dim(values, 1, extent, axis=axis_num) - lax.slice_in_dim(
        values, 0, extent - 1, axis=axis_num
    )


def shifted_sum(values, axis_num):
    extent = values.shape[axis_num]
    return lax.slice_in_dim(values, 1, extent, axis=axis_num) + lax.slice_in_dim(
        values, 0, extent - 1, axis=axis_num
    )


def spread_blocks(values, width):
    extent_a, extent_b, extent_c = values.shape
    wide = jnp.broadcast_to(
        values[:, None, :, None, :, None], (extent_a, width, extent_b, width, extent_c, width)
    )
    return wide.reshape(extent_a * width, extent_b * width, extent_c * width)


def moduli(substance_labels):
    shear_mod = jnp.where(
        substance_labels == 0, 3.0, jnp.where(substance_labels == 1, 2.0, 0.8)
    ).astype(jnp.float32)
    bulk_mod = jnp.where(
        substance_labels == 0, 5.0, jnp.where(substance_labels == 1, 4.0, 1.2)
    ).astype(jnp.float32)
    return (shear_mod, bulk_mod)


def face_term(element_values, axis_num):
    others = [other for other in (0, 1, 2) if other != axis_num]
    return shifted_diff(shifted_sum(shifted_sum(element_values, others[0]), others[1]), axis_num)


def element_state(node_vel, props):
    grad_x = 0.25 * shifted_diff(shifted_sum(shifted_sum(node_vel, 2), 3), 1)
    grad_y = 0.25 * shifted_diff(shifted_sum(shifted_sum(node_vel, 1), 3), 2)
    grad_z = 0.25 * shifted_diff(shifted_sum(shifted_sum(node_vel, 1), 2), 3)
    yield_eff = props[6]
    shear_mod = props[7]
    bulk_mod = props[8]
    strain_xx = TIME_STEP * grad_x[0]
    strain_yy = TIME_STEP * grad_y[1]
    strain_zz = TIME_STEP * grad_z[2]
    strain_xy = TIME_STEP * (0.5 * (grad_y[0] + grad_x[1]))
    strain_yz = TIME_STEP * (0.5 * (grad_z[1] + grad_y[2]))
    strain_xz = TIME_STEP * (0.5 * (grad_z[0] + grad_x[2]))
    volume = strain_xx + strain_yy + strain_zz
    vol_third = volume / 3.0
    trial_xx = props[0] + 2.0 * shear_mod * (strain_xx - vol_third) + bulk_mod * volume
    trial_yy = props[1] + 2.0 * shear_mod * (strain_yy - vol_third) + bulk_mod * volume
    trial_zz = props[2] + 2.0 * shear_mod * (strain_zz - vol_third) + bulk_mod * volume
    trial_xy = props[3] + 2.0 * shear_mod * strain_xy
    trial_yz = props[4] + 2.0 * shear_mod * strain_yz
    trial_xz = props[5] + 2.0 * shear_mod * strain_xz
    pressure = (trial_xx + trial_yy + trial_zz) / 3.0
    dev_xx = trial_xx - pressure
    dev_yy = trial_yy - pressure
    dev_zz = trial_zz - pressure
    second = (
        dev_xx * dev_xx
        + dev_yy * dev_yy
        + dev_zz * dev_zz
        + 2.0 * (trial_xy * trial_xy + trial_yz * trial_yz + trial_xz * trial_xz)
    )
    equivalent = jnp.sqrt(1.5 * second)
    flow_stress = yield_eff + FRICTION * jnp.maximum(-pressure, 0.0)
    excess = equivalent - flow_stress
    active = excess > 0.0
    plastic_rate = jnp.maximum(excess, 0.0) / (3.0 * shear_mod + VISCOSITY / TIME_STEP)
    scale_back = jnp.where(
        active, 1.0 - 3.0 * shear_mod * plastic_rate / jnp.where(active, equivalent, 1.0), 1.0
    )
    updated = jnp.stack(
        [
            pressure + scale_back * dev_xx,
            pressure + scale_back * dev_yy,
            pressure + scale_back * dev_zz,
            scale_back * trial_xy,
            scale_back * trial_yz,
            scale_back * trial_xz,
        ]
    )
    heat_local = (
        HEAT_SCALE * TAYLOR_QUINNEY * (equivalent - 3.0 * shear_mod * plastic_rate) * plastic_rate
    )
    return (updated, heat_local)


def node_forces(updated):
    force_x = face_term(updated[0], 0) + face_term(updated[3], 1) + face_term(updated[5], 2)
    force_y = face_term(updated[3], 0) + face_term(updated[1], 1) + face_term(updated[4], 2)
    force_z = face_term(updated[5], 0) + face_term(updated[4], 1) + face_term(updated[2], 2)
    return -0.25 * jnp.stack([force_x, force_y, force_z])


def mechanics(padded, corner_weights_diagonal):
    node_vel = padded[0:3]
    updated, heat_local = element_state(node_vel, padded[3:, :-1, :-1, :-1])
    force = node_forces(updated)
    corner_speed_later = node_vel[:, 1:-1, 1:-1, 1:-1] - TIME_STEP * force / corner_weights_diagonal
    return (corner_speed_later, updated[:, 1:, 1:, 1:], heat_local[1:, 1:, 1:])


def stencil(values, padded, matrix_main_entries):
    beside = padded[2:, 1:-1, 1:-1] + padded[:-2, 1:-1, 1:-1]
    beside = beside + padded[1:-1, 2:, 1:-1] + padded[1:-1, :-2, 1:-1]
    beside = beside + padded[1:-1, 1:-1, 2:] + padded[1:-1, 1:-1, :-2]
    return matrix_main_entries * values - beside


def diffuse_thermal_once(values, matrix_main_entries):
    haloed = extended(values, (("gx", 0), (("gy", "gz"), 1)), 1)
    padded = jnp.pad(haloed, ((0, 0), (0, 0), (1, 1)))
    return stencil(values, padded, matrix_main_entries)


def polynomial_relaxation(
    brick_warmth_prior,
    caloric_capacity_per_timestep,
    plastic_work_heating_rise,
    diffuse_thermal_field,
    inward_cell_flags,
):
    center_value = 0.5 * (UPPER_BOUND + LOWER_BOUND)
    half_width = 0.5 * (UPPER_BOUND - LOWER_BOUND)
    ratio_sig = center_value / half_width
    matrix_main_entries = 6.0 + caloric_capacity_per_timestep
    linear_system_target = (
        caloric_capacity_per_timestep * brick_warmth_prior + plastic_work_heating_rise
    )
    implicit_kelvin_result = brick_warmth_prior
    equation_misfit = (
        linear_system_target - diffuse_thermal_field(implicit_kelvin_result, matrix_main_entries)
    ) * inward_cell_flags
    weight_now = 1.0 / ratio_sig
    search_direction = equation_misfit / center_value
    for sweep_index in range(SWEEPS):
        implicit_kelvin_result = implicit_kelvin_result + search_direction
        if sweep_index + 1 < SWEEPS:
            equation_misfit = (
                equation_misfit - diffuse_thermal_field(search_direction, matrix_main_entries)
            ) * inward_cell_flags
            weight_next = 1.0 / (2.0 * ratio_sig - weight_now)
            search_direction = (
                weight_next * weight_now * search_direction
                + 2.0 * weight_next / half_width * equation_misfit
            )
            weight_now = weight_next
    return implicit_kelvin_result


def body(
    corner_speed_prior,
    brick_stress_tensor_now,
    compact_onset_strength,
    corner_weights_diagonal,
    substance_labels,
    brick_warmth_prior,
    caloric_capacity_per_timestep,
):
    z_index = lax.axis_index("gz")
    local_mat = lax.dynamic_slice_in_dim(substance_labels, z_index * ZB, ZB, 1)
    shear_blk, bulk_blk = moduli(local_mat)
    powder_cells = spread_blocks(local_mat, BS) == 2
    yield_eff = jnp.where(powder_cells, compact_onset_strength, ELASTIC_YIELD)
    stacked = jnp.concatenate(
        [
            corner_speed_prior,
            brick_stress_tensor_now,
            yield_eff[None],
            spread_blocks(shear_blk, BS)[None],
            spread_blocks(bulk_blk, BS)[None],
        ],
        axis=0,
    )
    padded = extended(stacked, (("gx", 1), ("gy", 3), ("gz", 2)), 1)
    corner_speed_later, projected_brick_stress_tensor, heat_local = mechanics(
        padded, corner_weights_diagonal
    )
    moved = lax.all_to_all(heat_local, "gz", split_axis=2, concat_axis=1, tiled=True)
    plastic_work_heating_rise = jnp.transpose(moved, (0, 2, 1))
    diffused_kelvin_field = polynomial_relaxation(
        brick_warmth_prior,
        caloric_capacity_per_timestep,
        plastic_work_heating_rise,
        diffuse_thermal_once,
        1.0,
    )
    return (corner_speed_later, projected_brick_stress_tensor, diffused_kelvin_field)


LANES = 128
SHIFT = 4
VELS = 3
FIELDS = 11
SLOT = 4
RING = 12
PLANES = 14
MAIN = RING * 2 * BS
VMEM_BYTES = 48 * 1024 * 1024


def two_rounds_fit(mesh):
    return mesh.shape["gx"] == 2 and mesh.shape["gy"] == 2 and mesh.shape["gz"] == 8


def iota(shape, dim):
    return lax.broadcasted_iota(jnp.int32, shape, dim)


def place(q):
    return MAIN + RING * q if q < 5 else 2 * LANES + RING * (q - 5)


def bulk_of(shear_mod):
    return jnp.where(
        shear_mod == 3.0,
        5.0,
        jnp.where(shear_mod == 2.0, 4.0, jnp.where(shear_mod == 0.0, 0.0, 1.2)),
    )


def doubled(plane):
    return jnp.concatenate([plane, plane], axis=1)


def own_labels(labels_ref):
    labels = labels_ref[0].astype(jnp.float32)
    press, second = labels.shape
    rows = ZB * BS
    first = lax.axis_index("gz") * ZB
    pick = iota((rows, press), 1) == first + iota((rows, press), 0) // BS
    spread = iota((second, LANES), 0) == (iota((second, LANES), 1) // BS) % second
    picked = jnp.dot(pick.astype(jnp.float32), labels, preferred_element_type=jnp.float32)
    return jnp.dot(picked, spread.astype(jnp.float32), preferred_element_type=jnp.float32)


def field_reader(labels_ref, vel_ref, stress_ref, onset_ref):
    labels = own_labels(labels_ref)
    shear_mod = jnp.where(labels == 0.0, 3.0, jnp.where(labels == 1.0, 2.0, 0.8))

    def read(field, x):
        if field < VELS:
            return doubled(vel_ref[field, x])
        if field < 9:
            return doubled(stress_ref[field - VELS, x])
        if field == 9:
            return jnp.where(labels == 2.0, doubled(onset_ref[x]), ELASTIC_YIELD)
        return shear_mod

    return read


FACE = (
    [(field, i) for field in range(VELS) for i in range(3)]
    + [(field, i) for field in range(VELS, 10) for i in range(2)]
    + [(10, 0)]
)
FACE_ROWS = len(FACE) // 2 * ZB * BS
FACE_ALL = FACE_ROWS + 4 * BS


def pack_kernel(labels, vel, stress, onset, warmth, capacity, face, columns, corner):
    lower_x = lax.axis_index("gx") == 0
    lower_y = lax.axis_index("gy") == 0
    read = field_reader(labels, vel, stress, onset)
    lane = iota((ZB * BS, LANES), 1)
    half = lane < LANES // 2
    deep = jnp.where(lower_x, BS - 3, 0)
    shallow = jnp.where(lower_x, BS - 2, 0)
    for pair in range(len(FACE) // 2):
        one, two = (
            read(field, (deep if field < VELS else shallow) + i)
            for field, i in FACE[2 * pair : 2 * pair + 2]
        )
        face[pl.ds(pair * ZB * BS, ZB * BS), :] = jnp.where(half, one, two)
    for i in range(3):
        face[pl.ds(FACE_ROWS + i * BS, BS), :] = warmth[deep + i]
    face[pl.ds(FACE_ROWS + 3 * BS, BS), :] = capacity[jnp.where(lower_x, BS - 1, 0)]
    turns = [
        lax.rem(SLOT * field + LANES - jnp.where(lower_y, LANES // 2 - 3, 0), LANES)
        for field in range(FIELDS)
    ]
    for x in range(BS):
        packed = jnp.zeros((ZB * BS, LANES), jnp.float32)
        for field in range(FIELDS):
            inside = (lane >= SLOT * field) & (lane < SLOT * field + 3)
            packed = jnp.where(inside, pltpu.roll(read(field, x), turns[field], 1), packed)
        columns[x] = packed
    for i in range(3):
        corner[i] = columns[deep + i]


def warmth_plane(j, warmth, face):
    tile = pl.ds(FACE_ROWS + j % BS * BS, BS) if j < 3 else pl.ds(FACE_ROWS + (j - 11) * BS, BS)
    upper_x = lax.axis_index("gx") == 1
    if j < 3:
        return jnp.where(upper_x, face[tile, :], 0.0)
    if j < 11:
        return warmth[j - 3]
    return jnp.where(upper_x, 0.0, face[tile, :])


def capacity_plane(j, capacity, face):
    upper_x = lax.axis_index("gx") == 1
    if 3 <= j < 11:
        return capacity[j - 3]
    if j == 2 or j == 11:
        tile = face[pl.ds(FACE_ROWS + 3 * BS, BS), :]
        return jnp.where(upper_x == (j == 2), tile, 0.0)
    return jnp.zeros((BS, LANES), jnp.float32)


def stress_terms(shear_mod):
    bulk_mod = bulk_of(shear_mod)
    return (
        0.5 * TIME_STEP * shear_mod,
        0.25 * TIME_STEP * (bulk_mod - 2.0 / 3.0 * shear_mod),
        3.0 * shear_mod,
        1.0 / (3.0 * shear_mod + VISCOSITY / TIME_STEP),
    )


def strained(before, grads, terms):
    twice, volume_term = terms[0], terms[1]
    volume = volume_term * (grads[0] + grads[1] + grads[2])
    return [
        before[k] + twice * grads[k] + (volume if k < 3 else 0.0) for k in range(6)
    ]


def returned(trial, yield_eff, terms):
    shear_thrice, slope = terms[2], terms[3]
    pressure = (trial[0] + trial[1] + trial[2]) * (1.0 / 3.0)
    dev = [trial[k] - pressure for k in range(3)]
    second = (
        dev[0] * dev[0]
        + dev[1] * dev[1]
        + dev[2] * dev[2]
        + 2.0 * (trial[3] * trial[3] + trial[4] * trial[4] + trial[5] * trial[5])
    )
    equivalent = jnp.sqrt(1.5 * second)
    excess = equivalent - (yield_eff + FRICTION * jnp.maximum(-pressure, 0.0))
    active = excess > 0.0
    rate = jnp.maximum(excess, 0.0) * slope
    drop = shear_thrice * rate
    scale = jnp.where(active, 1.0 - drop / jnp.where(active, equivalent, 1.0), 1.0)
    heat = HEAT_SCALE * TAYLOR_QUINNEY * (equivalent - drop) * rate
    updated = [pressure + scale * dev[k] for k in range(3)] + [
        scale * trial[k] for k in range(3, 6)
    ]
    return updated, heat


def six(gx, gp, gs):
    return [
        gx[0],
        gp[1],
        gs[2],
        0.5 * (gp[0] + gx[1]),
        0.5 * (gs[1] + gp[2]),
        0.5 * (gs[0] + gx[2]),
    ]


EDGE_ROWS = 8 * RING
EDGE_ALL = EDGE_ROWS + 7 * BS


def heat_kernel(
    labels, vel, stress, onset, warmth, capacity, face, columns, corner,
    chunks, even_out, odd_out, updated_out, partial_out,
    ext, shears, lowest, stacked,
):
    upper_x = lax.axis_index("gx") == 1
    upper_y = lax.axis_index("gy") == 1
    even = lax.rem(lax.axis_index("gz"), 2) == 0
    read = field_reader(labels, vel, stress, onset)
    rows = ZB * BS
    lane = iota((rows, LANES), 1)
    row = iota((rows, LANES), 0)
    own = (lane >= SHIFT) & (lane < SHIFT + LANES // 2)
    first = jnp.where(upper_y, 1, SHIFT + LANES // 2)
    beside = (lane >= first) & (lane < first + 3)
    turns = [lax.rem(first + LANES - SLOT * field, LANES) for field in range(FIELDS)]

    def joined(field, plane, turn, side):
        halo = jnp.where(beside, pltpu.roll(side, turns[field], 1), 0.0)
        return jnp.where(own, pltpu.roll(plane, turn, 1), halo)

    for field in range(10):
        for x in range(BS):
            ext[field, x + 3] = joined(field, read(field, x), SHIFT, columns[x])
    shears[1] = joined(10, read(10, 0), SHIFT, columns[0])
    blank = jnp.zeros((rows, LANES), jnp.float32)
    for at, (field, i) in enumerate(FACE):
        plane = face[pl.ds(at // 2 * rows, rows), :]
        turn = SHIFT + at % 2 * (LANES // 2)
        if field < VELS:
            ext[field, jnp.where(upper_x, i, 11 + i)] = joined(field, plane, turn, corner[i])
            ext[field, jnp.where(upper_x, 11 + i, i)] = blank
        elif field < 10:
            side = corner[jnp.where(upper_x, i + 1, i)]
            ext[field, jnp.where(upper_x, 1 + i, 11 + i)] = joined(field, plane, turn, side)
            ext[field, jnp.where(upper_x, 11 + i, 1 + i)] = blank
        else:
            shears[jnp.where(upper_x, 0, 2)] = joined(field, plane, turn, corner[1])
            shears[jnp.where(upper_x, 2, 0)] = blank

    lowest[...] = jnp.zeros_like(lowest)
    stacked[pl.ds(MAIN, 4 * BS * 2), :] = jnp.zeros((4 * BS * 2, LANES), jnp.float32)
    stacked[pl.ds(2 * LANES + 96, 32), :] = jnp.zeros((32, LANES), jnp.float32)

    def node_terms(j):
        terms = []
        for c in range(VELS):
            here = ext[c, j]
            lowest[c, pl.ds(j - 1, 1), :] = here[0:1, :]
            above = jnp.where(row == rows - 1, 0.0, pltpu.roll(here, rows - 1, 0))
            total, change = here + above, above - here
            aside = pltpu.roll(total, LANES - 1, 1)
            terms.append((total + aside, aside - total, change + pltpu.roll(change, LANES - 1, 1)))
        return terms

    materials = [stress_terms(shears[b]) for b in range(3)]
    before = node_terms(1)
    for a in range(RING):
        after = node_terms(a + 2)
        grads = six(
            [after[c][0] - before[c][0] for c in range(VELS)],
            [after[c][2] + before[c][2] for c in range(VELS)],
            [after[c][1] + before[c][1] for c in range(VELS)],
        )
        block = 0 if a < 2 else 1 if a < 10 else 2
        yield_eff = ext[9, a + 1]
        trial = strained([ext[VELS + k, a + 1] for k in range(6)], grads, materials[block])
        updated, heat = returned(trial, yield_eff, materials[block])
        stacked[pl.ds(a * rows, rows), :] = heat
        for q, plane in enumerate(trial + [yield_eff, shears[block]]):
            partial_out[q, pl.ds(a, 1), :] = plane[rows - 1 : rows, :]
        if 1 <= a < 10:
            for k in range(6):
                updated_out[k, a - 1] = updated[k]
        before = after

    flat = []
    for c in range(VELS):
        here = lowest[c]
        aside = pltpu.roll(here, LANES - 1, 1)
        total, change = here + aside, aside - here
        nxt = pltpu.roll(total, rows - 1, 0)
        flat.append((nxt - total, nxt + total, change + pltpu.roll(change, rows - 1, 0)))
    for k, plane in enumerate(six(*[[flat[c][d] for c in range(VELS)] for d in range(3)])):
        partial_out[8 + k] = plane
    for q in range(PLANES):
        stacked[pl.ds(place(q), RING), :] = partial_out[q, pl.ds(0, RING), :]
    turned = jnp.transpose(stacked[...])
    for g in range(chunks.shape[0]):
        chunks[g] = turned[g * BS : g * BS + 2 * BS, :]

    sub = iota((BS, LANES), 0)
    ups, downs = [], []
    for j in range(14):
        u = warmth_plane(j, warmth, face)
        c = capacity_plane(j, capacity, face)
        ups.append(jnp.where(sub > 4, u, pltpu.roll(c, 5, 0)))
        downs.append(jnp.where(sub < 3, u, pltpu.roll(c, 3, 0)))

    def fill(up_ref, down_ref):
        for q in range(8):
            up_ref[pl.ds(RING * q, RING), :] = partial_out[q, pl.ds(0, RING), :]
        for k in range(6):
            down_ref[pl.ds(RING * k, RING), :] = partial_out[8 + k, pl.ds(0, RING), :]
        down_ref[pl.ds(6 * RING, 2 * RING), :] = jnp.zeros((2 * RING, LANES), jnp.float32)
        for m in range(7):
            at = pl.ds(EDGE_ROWS + m * BS, BS)
            up_ref[at, :] = jnp.where(sub < 4, pltpu.roll(ups[2 * m], 4, 0), ups[2 * m + 1])
            down_ref[at, :] = jnp.where(sub < 4, downs[2 * m], pltpu.roll(downs[2 * m + 1], 4, 0))

    @pl.when(even)
    def _():
        fill(even_out, odd_out)

    @pl.when(jnp.logical_not(even))
    def _():
        fill(odd_out, even_out)


def force_kernel(
    updated, partial, even_in, odd_in, vel, mass, vel_out, stress_out, top, bottom
):
    at_z = lax.axis_index("gz")
    even = lax.rem(at_z, 2) == 0
    has_above = at_z < lax.axis_size("gz") - 1
    has_below = at_z > 0
    rows = ZB * BS
    row = iota((rows, LANES), 0)

    def below(q):
        at = pl.ds(RING * q, rows)
        return jnp.where(has_below, jnp.where(even, odd_in[at, :], even_in[at, :]), 0.0)

    def above(k):
        at = pl.ds(RING * k, rows)
        return jnp.where(has_above, jnp.where(even, even_in[at, :], odd_in[at, :]), 0.0)

    terms = stress_terms(partial[7])
    trial = strained([partial[k] for k in range(6)], [above(k) for k in range(6)], terms)
    for k, plane in enumerate(returned(trial, partial[6], terms)[0]):
        top[k] = plane
    terms = stress_terms(below(7))
    trial = strained([below(k) for k in range(6)], [partial[8 + k] for k in range(6)], terms)
    for k, plane in enumerate(returned(trial, below(6), terms)[0]):
        bottom[k] = plane

    def element_terms(j):
        terms = []
        for k in range(6):
            here = jnp.where(row == rows - 1, top[k, pl.ds(j + 1, 1), :], updated[k, j])
            if j > 0:
                stress_out[k, j - 1] = pltpu.roll(here, LANES - SHIFT, 1)[:, : LANES // 2]
            prev = jnp.where(row == 0, bottom[k, pl.ds(j + 1, 1), :], pltpu.roll(here, 1, 0))
            total, change = here + prev, here - prev
            aside = pltpu.roll(total, 1, 1)
            terms.append((total + aside, total - aside, change + pltpu.roll(change, 1, 1)))
        return terms

    before = element_terms(0)
    for x in range(BS):
        after = element_terms(x + 1)
        weights = 0.25 * TIME_STEP / mass[x]
        for c, (kx, kp, ks) in enumerate(((0, 3, 5), (3, 1, 4), (5, 4, 2))):
            force = (
                (after[kx][0] - before[kx][0])
                + (after[kp][2] + before[kp][2])
                + (after[ks][1] + before[ks][1])
            )
            force = pltpu.roll(force, LANES - SHIFT, 1)[:, : LANES // 2]
            vel_out[c, x] = vel[c, x] + force * weights
        before = after


def conduct_kernel(chunks, warmth, capacity, face, even_in, odd_in, out):
    upper_x = lax.axis_index("gx") == 1
    at_z = lax.axis_index("gz")
    even = lax.rem(at_z, 2) == 0
    groups = lax.axis_size("gz")
    rows = ZB * BS
    at_flat = lax.axis_index("gy") * groups + at_z
    last = lax.axis_size("gy") * groups - 1
    lane = iota((rows, LANES), 1)
    row = iota((rows, LANES), 0)
    group = lane // rows
    sub = iota((BS, LANES), 0)

    heats = []
    for t, count in ((0, 8), (1, 4)):
        turned = []
        for k in range(groups):
            mixed = chunks[k, :, pl.ds(t * LANES, LANES)]
            for b in range(1, count):
                source = chunks[(b + k) % groups, :, pl.ds(t * LANES, LANES)]
                mixed = jnp.where(group == b, source, mixed)
            turned.append(pltpu.roll(mixed, k * rows, 1) if k else mixed)
        for b in range(count):
            heat = turned[(0 - b) % groups]
            for g in range(1, groups):
                heat = jnp.where(group == g, turned[(g - b) % groups], heat)
            heats.append(heat)

    planes = []
    for q in range(PLANES):
        tile, at = divmod(place(q), LANES)
        plane = jnp.zeros((rows, LANES), jnp.float32)
        for g in range(groups):
            to = g if q < 8 else g - 1
            if to < 0:
                continue
            source = chunks[g, :, pl.ds(tile * LANES, LANES)]
            inside = (lane >= to * rows) & (lane < to * rows + RING)
            plane = jnp.where(inside, pltpu.roll(source, (to * rows - at) % LANES, 1), plane)
        planes.append(plane)
    terms = stress_terms(planes[7])
    seam = returned(strained(planes[:6], planes[8:], terms), planes[6], terms)[1]
    for a in range(RING):
        heats[a] = jnp.where(
            lane % rows == rows - 1, pltpu.roll(seam, rows - 1 - a, 1), heats[a]
        )

    u_rows = (row >= jnp.where(at_flat == 0, 4, 1)) & (row < jnp.where(at_flat == last, 12, 15))
    d_rows = (row >= jnp.where(at_flat == 0, 4, 2)) & (row < jnp.where(at_flat == last, 12, 14))
    us, caps = [], []
    for j in range(14):
        at = pl.ds(EDGE_ROWS + j // 2 * BS, BS)
        low = jnp.where(even, odd_in[at, :], even_in[at, :])
        high = jnp.where(even, even_in[at, :], odd_in[at, :])
        if j % 2:
            low = pltpu.roll(low, 4, 0)
        else:
            high = pltpu.roll(high, 4, 0)
        mid = pltpu.roll(warmth_plane(j, warmth, face), 4, 0)
        u = jnp.concatenate([jnp.where(sub < 4, low, mid), jnp.where(sub < 4, mid, high)], axis=0)
        us.append(jnp.where(u_rows, u, 0.0))
        mid = pltpu.roll(capacity_plane(j, capacity, face), 4, 0)
        caps.append(
            6.0
            + jnp.concatenate(
                [
                    jnp.where(sub < 4, pltpu.roll(low, 3, 0), mid),
                    jnp.where(sub < 4, mid, pltpu.roll(high, 5, 0)),
                ],
                axis=0,
            )
        )

    def around(fields, a):
        here = fields[a]
        total = fields[a - 1] + fields[a + 1]
        total = total + pltpu.roll(here, 1, 0) + pltpu.roll(here, rows - 1, 0)
        total = total + jnp.where(lane == 0, 0.0, pltpu.roll(here, 1, 1))
        return total + jnp.where(lane == LANES - 1, 0.0, pltpu.roll(here, LANES - 1, 1))

    def inside(a):
        if a < 2:
            return d_rows & upper_x
        if a >= 10:
            return d_rows & jnp.logical_not(upper_x)
        return d_rows

    theta = 0.5 * (UPPER_BOUND + LOWER_BOUND)
    half_width = 0.5 * (UPPER_BOUND - LOWER_BOUND)
    sig = theta / half_width
    weight_now = 1.0 / sig
    misfit, step, total = {}, {}, {}
    for a in range(RING):
        misfit[a] = heats[a] - 6.0 * us[a + 1] + around(us, a + 1)
        step[a] = jnp.where(inside(a), misfit[a] * (1.0 / theta), 0.0)
        total[a] = us[a + 1] + step[a]
    for sweep in range(1, SWEEPS):
        weight_next = 1.0 / (2.0 * sig - weight_now)
        new_misfit, new_step = {}, {}
        for a in range(sweep, RING - sweep):
            new_misfit[a] = misfit[a] - caps[a + 1] * step[a] + around(step, a)
            moved = (weight_next * weight_now) * step[a] + (
                2.0 * weight_next / half_width
            ) * new_misfit[a]
            new_step[a] = jnp.where(inside(a), moved, 0.0)
            total[a] = total[a] + new_step[a]
        misfit, step, weight_now = new_misfit, new_step, weight_next
    for x in range(BS):
        result = total[x + 2]
        out[x] = jnp.where(sub < 4, pltpu.roll(result[:BS], 4, 0), pltpu.roll(result[BS:], 4, 0))


def f32(*shape):
    return jax.ShapeDtypeStruct(shape, jnp.float32)


def call(kernel, out_shape, *args, scratch=(), flops=0):
    moved = 4 * sum(a.size for a in args) + 4 * sum(o.size for o in jax.tree.leaves(out_shape))
    return pl.pallas_call(
        kernel,
        out_shape=out_shape,
        scratch_shapes=[pltpu.VMEM(shape, jnp.float32) for shape in scratch],
        compiler_params=pltpu.CompilerParams(vmem_limit_bytes=VMEM_BYTES),
        cost_estimate=pl.CostEstimate(flops=flops, bytes_accessed=moved, transcendentals=0),
    )(*args)


def paired(count, first):
    pairs = []
    for i in range(first, count - 1, 2):
        pairs += [(i, i + 1), (i + 1, i)]
    return pairs


def two_round_body(
    corner_speed_prior,
    brick_stress_tensor_now,
    compact_onset_strength,
    corner_weights_diagonal,
    substance_labels,
    brick_warmth_prior,
    caloric_capacity_per_timestep,
):
    rows = ZB * BS
    groups = lax.axis_size("gz")
    chain = groups * lax.axis_size("gy")
    raw = (
        substance_labels,
        corner_speed_prior,
        brick_stress_tensor_now,
        compact_onset_strength,
        brick_warmth_prior,
        caloric_capacity_per_timestep,
    )
    face, columns, corner = call(
        pack_kernel, (f32(FACE_ALL, LANES), f32(BS, rows, LANES), f32(3, rows, LANES)), *raw
    )
    face = lax.ppermute(face, "gx", [(0, 1), (1, 0)])
    columns = lax.ppermute(columns, "gy", [(0, 1), (1, 0)])
    corner = lax.ppermute(corner, ("gx", "gy"), [(0, 3), (3, 0), (1, 2), (2, 1)])
    chunks, even, odd, updated, partial = call(
        heat_kernel,
        (
            f32(groups, rows, 3 * LANES),
            f32(EDGE_ALL, LANES),
            f32(EDGE_ALL, LANES),
            f32(6, BS + 1, rows, LANES),
            f32(PLANES, rows, LANES),
        ),
        *raw,
        face,
        columns,
        corner,
        scratch=((10, 14, rows, LANES), (3, rows, LANES), (VELS, rows, LANES), (3 * LANES, LANES)),
    )
    chunks = lax.all_to_all(chunks, "gz", split_axis=0, concat_axis=0, tiled=True)
    even = lax.ppermute(even, ("gy", "gz"), paired(chain, 0))
    odd = lax.ppermute(odd, ("gy", "gz"), paired(chain, 1))
    corner_speed_later, projected_brick_stress_tensor = call(
        force_kernel,
        (f32(*corner_speed_prior.shape), f32(*brick_stress_tensor_now.shape)),
        updated,
        partial,
        even,
        odd,
        corner_speed_prior,
        corner_weights_diagonal,
        scratch=((6, rows, LANES), (6, rows, LANES)),
    )
    diffused_kelvin_field = call(
        conduct_kernel,
        f32(*brick_warmth_prior.shape),
        chunks,
        brick_warmth_prior,
        caloric_capacity_per_timestep,
        face,
        even,
        odd,
    )
    return (corner_speed_later, projected_brick_stress_tensor, diffused_kelvin_field)


def solution(mesh):
    placed = (
        P(None, "gx", "gz", "gy"),
        P(None, "gx", "gz", "gy"),
        P("gx", "gz", "gy"),
        P("gx", "gz", "gy"),
        P("gx", None, "gy"),
        P("gx", ("gy", "gz"), None),
        P("gx", ("gy", "gz"), None),
    )
    return jax.shard_map(
        two_round_body if two_rounds_fit(mesh) else body,
        mesh=mesh,
        in_specs=placed,
        out_specs=(
            P(None, "gx", "gz", "gy"),
            P(None, "gx", "gz", "gy"),
            P("gx", ("gy", "gz"), None),
        ),
        check_vma=False,
    )
```

```python
import jax
import jax.numpy as jnp
from jax import lax
from jax.experimental import pallas as pl
from jax.experimental.pallas import tpu as pltpu
from jax.sharding import PartitionSpec as P

BS = 8
ZB = 2
SWEEPS = 3


TIME_STEP = 0.2
VISCOSITY = 0.4
FRICTION = 0.5
TAYLOR_QUINNEY = 0.9
HEAT_SCALE = 5.0
ELASTIC_YIELD = 10000.0
LOWER_BOUND = 0.5
UPPER_BOUND = 16.0


def extended(cells, sides, width):
    for axis, dim in sides:
        count = lax.axis_size(axis)
        ends = count - 1
        head = lax.slice_in_dim(cells, 0, width, axis=dim)
        tail = lax.slice_in_dim(cells, cells.shape[dim] - width, cells.shape[dim], axis=dim)
        cells = jnp.concatenate(
            [
                lax.ppermute(tail, axis, [(i, (i + 1) % count) for i in range(ends)]),
                cells,
                lax.ppermute(head, axis, [((i + 1) % count, i) for i in range(ends)]),
            ],
            axis=dim,
        )
    return cells


def shifted_diff(values, axis_num):
    extent = values.shape[axis_num]
    return lax.slice_in_dim(values, 1, extent, axis=axis_num) - lax.slice_in_dim(
        values, 0, extent - 1, axis=axis_num
    )


def shifted_sum(values, axis_num):
    extent = values.shape[axis_num]
    return lax.slice_in_dim(values, 1, extent, axis=axis_num) + lax.slice_in_dim(
        values, 0, extent - 1, axis=axis_num
    )


def spread_blocks(values, width):
    extent_a, extent_b, extent_c = values.shape
    wide = jnp.broadcast_to(
        values[:, None, :, None, :, None], (extent_a, width, extent_b, width, extent_c, width)
    )
    return wide.reshape(extent_a * width, extent_b * width, extent_c * width)


def moduli(substance_labels):
    shear_mod = jnp.where(
        substance_labels == 0, 3.0, jnp.where(substance_labels == 1, 2.0, 0.8)
    ).astype(jnp.float32)
    bulk_mod = jnp.where(
        substance_labels == 0, 5.0, jnp.where(substance_labels == 1, 4.0, 1.2)
    ).astype(jnp.float32)
    return (shear_mod, bulk_mod)


def face_term(element_values, axis_num):
    others = [other for other in (0, 1, 2) if other != axis_num]
    return shifted_diff(shifted_sum(shifted_sum(element_values, others[0]), others[1]), axis_num)


def element_state(node_vel, props):
    grad_x = 0.25 * shifted_diff(shifted_sum(shifted_sum(node_vel, 2), 3), 1)
    grad_y = 0.25 * shifted_diff(shifted_sum(shifted_sum(node_vel, 1), 3), 2)
    grad_z = 0.25 * shifted_diff(shifted_sum(shifted_sum(node_vel, 1), 2), 3)
    yield_eff = props[6]
    shear_mod = props[7]
    bulk_mod = props[8]
    strain_xx = TIME_STEP * grad_x[0]
    strain_yy = TIME_STEP * grad_y[1]
    strain_zz = TIME_STEP * grad_z[2]
    strain_xy = TIME_STEP * (0.5 * (grad_y[0] + grad_x[1]))
    strain_yz = TIME_STEP * (0.5 * (grad_z[1] + grad_y[2]))
    strain_xz = TIME_STEP * (0.5 * (grad_z[0] + grad_x[2]))
    volume = strain_xx + strain_yy + strain_zz
    vol_third = volume / 3.0
    trial_xx = props[0] + 2.0 * shear_mod * (strain_xx - vol_third) + bulk_mod * volume
    trial_yy = props[1] + 2.0 * shear_mod * (strain_yy - vol_third) + bulk_mod * volume
    trial_zz = props[2] + 2.0 * shear_mod * (strain_zz - vol_third) + bulk_mod * volume
    trial_xy = props[3] + 2.0 * shear_mod * strain_xy
    trial_yz = props[4] + 2.0 * shear_mod * strain_yz
    trial_xz = props[5] + 2.0 * shear_mod * strain_xz
    pressure = (trial_xx + trial_yy + trial_zz) / 3.0
    dev_xx = trial_xx - pressure
    dev_yy = trial_yy - pressure
    dev_zz = trial_zz - pressure
    second = (
        dev_xx * dev_xx
        + dev_yy * dev_yy
        + dev_zz * dev_zz
        + 2.0 * (trial_xy * trial_xy + trial_yz * trial_yz + trial_xz * trial_xz)
    )
    equivalent = jnp.sqrt(1.5 * second)
    flow_stress = yield_eff + FRICTION * jnp.maximum(-pressure, 0.0)
    excess = equivalent - flow_stress
    active = excess > 0.0
    plastic_rate = jnp.maximum(excess, 0.0) / (3.0 * shear_mod + VISCOSITY / TIME_STEP)
    scale_back = jnp.where(
        active, 1.0 - 3.0 * shear_mod * plastic_rate / jnp.where(active, equivalent, 1.0), 1.0
    )
    updated = jnp.stack(
        [
            pressure + scale_back * dev_xx,
            pressure + scale_back * dev_yy,
            pressure + scale_back * dev_zz,
            scale_back * trial_xy,
            scale_back * trial_yz,
            scale_back * trial_xz,
        ]
    )
    heat_local = (
        HEAT_SCALE * TAYLOR_QUINNEY * (equivalent - 3.0 * shear_mod * plastic_rate) * plastic_rate
    )
    return (updated, heat_local)


def node_forces(updated):
    force_x = face_term(updated[0], 0) + face_term(updated[3], 1) + face_term(updated[5], 2)
    force_y = face_term(updated[3], 0) + face_term(updated[1], 1) + face_term(updated[4], 2)
    force_z = face_term(updated[5], 0) + face_term(updated[4], 1) + face_term(updated[2], 2)
    return -0.25 * jnp.stack([force_x, force_y, force_z])


def mechanics(padded, corner_weights_diagonal):
    node_vel = padded[0:3]
    updated, heat_local = element_state(node_vel, padded[3:, :-1, :-1, :-1])
    force = node_forces(updated)
    corner_speed_later = node_vel[:, 1:-1, 1:-1, 1:-1] - TIME_STEP * force / corner_weights_diagonal
    return (corner_speed_later, updated[:, 1:, 1:, 1:], heat_local[1:, 1:, 1:])


def stencil(values, padded, matrix_main_entries):
    beside = padded[2:, 1:-1, 1:-1] + padded[:-2, 1:-1, 1:-1]
    beside = beside + padded[1:-1, 2:, 1:-1] + padded[1:-1, :-2, 1:-1]
    beside = beside + padded[1:-1, 1:-1, 2:] + padded[1:-1, 1:-1, :-2]
    return matrix_main_entries * values - beside


def diffuse_thermal_once(values, matrix_main_entries):
    haloed = extended(values, (("gx", 0), (("gy", "gz"), 1)), 1)
    padded = jnp.pad(haloed, ((0, 0), (0, 0), (1, 1)))
    return stencil(values, padded, matrix_main_entries)


def polynomial_relaxation(
    brick_warmth_prior,
    caloric_capacity_per_timestep,
    plastic_work_heating_rise,
    diffuse_thermal_field,
    inward_cell_flags,
):
    center_value = 0.5 * (UPPER_BOUND + LOWER_BOUND)
    half_width = 0.5 * (UPPER_BOUND - LOWER_BOUND)
    ratio_sig = center_value / half_width
    matrix_main_entries = 6.0 + caloric_capacity_per_timestep
    linear_system_target = (
        caloric_capacity_per_timestep * brick_warmth_prior + plastic_work_heating_rise
    )
    implicit_kelvin_result = brick_warmth_prior
    equation_misfit = (
        linear_system_target - diffuse_thermal_field(implicit_kelvin_result, matrix_main_entries)
    ) * inward_cell_flags
    weight_now = 1.0 / ratio_sig
    search_direction = equation_misfit / center_value
    for sweep_index in range(SWEEPS):
        implicit_kelvin_result = implicit_kelvin_result + search_direction
        if sweep_index + 1 < SWEEPS:
            equation_misfit = (
                equation_misfit - diffuse_thermal_field(search_direction, matrix_main_entries)
            ) * inward_cell_flags
            weight_next = 1.0 / (2.0 * ratio_sig - weight_now)
            search_direction = (
                weight_next * weight_now * search_direction
                + 2.0 * weight_next / half_width * equation_misfit
            )
            weight_now = weight_next
    return implicit_kelvin_result


def body(
    corner_speed_prior,
    brick_stress_tensor_now,
    compact_onset_strength,
    corner_weights_diagonal,
    substance_labels,
    brick_warmth_prior,
    caloric_capacity_per_timestep,
):
    z_index = lax.axis_index("gz")
    local_mat = lax.dynamic_slice_in_dim(substance_labels, z_index * ZB, ZB, 1)
    shear_blk, bulk_blk = moduli(local_mat)
    powder_cells = spread_blocks(local_mat, BS) == 2
    yield_eff = jnp.where(powder_cells, compact_onset_strength, ELASTIC_YIELD)
    stacked = jnp.concatenate(
        [
            corner_speed_prior,
            brick_stress_tensor_now,
            yield_eff[None],
            spread_blocks(shear_blk, BS)[None],
            spread_blocks(bulk_blk, BS)[None],
        ],
        axis=0,
    )
    padded = extended(stacked, (("gx", 1), ("gy", 3), ("gz", 2)), 1)
    corner_speed_later, projected_brick_stress_tensor, heat_local = mechanics(
        padded, corner_weights_diagonal
    )
    moved = lax.all_to_all(heat_local, "gz", split_axis=2, concat_axis=1, tiled=True)
    plastic_work_heating_rise = jnp.transpose(moved, (0, 2, 1))
    diffused_kelvin_field = polynomial_relaxation(
        brick_warmth_prior,
        caloric_capacity_per_timestep,
        plastic_work_heating_rise,
        diffuse_thermal_once,
        1.0,
    )
    return (corner_speed_later, projected_brick_stress_tensor, diffused_kelvin_field)


LANES = 128
SHIFT = 4
VELS = 3
FIELDS = 11
SLOT = 4
RING = 12
PLANES = 14
MAIN = RING * 2 * BS
VMEM_BYTES = 48 * 1024 * 1024


def two_rounds_fit(mesh):
    return mesh.shape["gx"] == 2 and mesh.shape["gy"] == 2 and mesh.shape["gz"] == 8


def iota(shape, dim):
    return lax.broadcasted_iota(jnp.int32, shape, dim)


def place(q):
    return MAIN + RING * q if q < 5 else 2 * LANES + RING * (q - 5)


def bulk_of(shear_mod):
    return jnp.where(
        shear_mod == 3.0,
        5.0,
        jnp.where(shear_mod == 2.0, 4.0, jnp.where(shear_mod == 0.0, 0.0, 1.2)),
    )


def own_labels(labels):
    second, press = labels.shape
    rows = ZB * BS
    first = lax.axis_index("gz") * ZB
    pick = iota((rows, press), 1) == first + iota((rows, press), 0) // BS
    spread = iota((second, LANES), 0) == (iota((second, LANES), 1) // BS) % second
    picked = lax.dot_general(
        pick.astype(jnp.float32),
        labels.astype(jnp.float32),
        (((1,), (1,)), ((), ())),
        preferred_element_type=jnp.float32,
    )
    return jnp.dot(picked, spread.astype(jnp.float32), preferred_element_type=jnp.float32)


FACE = (
    [(field, i) for field in range(VELS) for i in range(3)]
    + [(field, i) for field in range(VELS, 10) for i in range(2)]
    + [(10, 0)]
)
FACE_TILES = len(FACE) // 2 * ZB
PLANE = ZB * BS


def slot_at(lane, field, first):
    where = lax.rem(lane + (2 * LANES - SLOT * field) - first, LANES)
    return where < 3


def pack_kernel(
    labels, vel, stress, onset, warmth, capacity,
    wide, shear_out, face, columns, corner,
    own, own_labels_in, sems,
):
    lower_x = lax.axis_index("gx") == 0
    lower_y = lax.axis_index("gy") == 0
    deep = jnp.where(lower_x, BS - 3, 0)
    shallow = jnp.where(lower_x, BS - 2, 0)
    edge = jnp.where(lower_x, BS - 1, 0)
    copies = [
        pltpu.make_async_copy(*pair, sems.at[n])
        for n, pair in enumerate(
            (
                (labels, own_labels_in),
                (vel, own.at[pl.ds(0, VELS)]),
                (onset, own.at[9]),
                (stress, own.at[pl.ds(VELS, 6)]),
                (warmth.at[pl.ds(deep, 3)], face.at[pl.ds(FACE_TILES, 3)]),
                (capacity.at[edge], face.at[FACE_TILES + 3]),
            )
        )
    ]
    for copy in copies:
        copy.start()
    lane = iota((PLANE, LANES), 1)
    half = LANES // 2
    copies[0].wait()
    material = own_labels(own_labels_in[0])
    shear_mod = jnp.where(material == 0.0, 3.0, jnp.where(material == 1.0, 2.0, 0.8))
    shear_out[...] = shear_mod
    copies[1].wait()
    copies[2].wait()
    for field in range(VELS):
        wide[pl.ds(field * BS * PLANE, BS * PLANE), 0:half] = own[field].reshape(BS * PLANE, half)
    powder = material[:, 0:half] == 2.0
    for x in range(BS):
        at = pl.ds((9 * BS + x) * PLANE, PLANE)
        wide[at, 0:half] = jnp.where(powder, own[9, x], ELASTIC_YIELD)
    copies[3].wait()
    for field in range(VELS, 9):
        wide[pl.ds(field * BS * PLANE, BS * PLANE), 0:half] = own[field].reshape(BS * PLANE, half)

    def read(field, x):
        if field == 10:
            return shear_mod
        return wide[pl.ds(pl.multiple_of((field * BS + x) * PLANE, PLANE), PLANE), :]

    for pair in range(len(FACE) // 2):
        one, two = (
            read(field, (deep if field < VELS else shallow) + i)
            for field, i in FACE[2 * pair : 2 * pair + 2]
        )
        joined = jnp.where(lane < half, one, pltpu.roll(two, half, 1))
        face[2 * pair] = joined[:BS]
        face[2 * pair + 1] = joined[BS:]
    first = jnp.where(lower_y, half - 3, 0)
    insides = [slot_at(lane, field, first) for field in range(FIELDS)]
    for x in range(BS):
        packed = jnp.zeros((PLANE, LANES), jnp.float32)
        for field in range(FIELDS):
            turned = read(field, x)
            if field:
                turned = pltpu.roll(turned, SLOT * field, 1)
            packed = jnp.where(insides[field], turned, packed)
        columns[x] = packed
    for i in range(3):
        corner[i] = columns[deep + i]
    copies[4].wait()
    copies[5].wait()


def warmth_plane(j, warmth, face):
    upper_x = lax.axis_index("gx") == 1
    if j < 3:
        return jnp.where(upper_x, face[FACE_TILES + j], 0.0)
    if j < 11:
        return warmth[j - 3]
    return jnp.where(upper_x, 0.0, face[FACE_TILES + j - 11])


def capacity_plane(j, capacity, face):
    upper_x = lax.axis_index("gx") == 1
    if 3 <= j < 11:
        return capacity[j - 3]
    if j == 2 or j == 11:
        return jnp.where(upper_x == (j == 2), face[FACE_TILES + 3], 0.0)
    return jnp.zeros((BS, LANES), jnp.float32)


def stress_terms(shear_mod):
    bulk_mod = bulk_of(shear_mod)
    return (
        0.5 * TIME_STEP * shear_mod,
        0.25 * TIME_STEP * (bulk_mod - 2.0 / 3.0 * shear_mod),
        3.0 * shear_mod,
        1.0 / (3.0 * shear_mod + VISCOSITY / TIME_STEP),
    )


def strained(before, grads, terms):
    twice, volume_term = terms[0], terms[1]
    volume = volume_term * (grads[0] + grads[1] + grads[2])
    return [
        before[k] + twice * grads[k] + (volume if k < 3 else 0.0) for k in range(6)
    ]


def returned(trial, yield_eff, terms):
    shear_thrice, slope = terms[2], terms[3]
    pressure = (trial[0] + trial[1] + trial[2]) * (1.0 / 3.0)
    dev = [trial[k] - pressure for k in range(3)]
    second = (
        dev[0] * dev[0]
        + dev[1] * dev[1]
        + dev[2] * dev[2]
        + 2.0 * (trial[3] * trial[3] + trial[4] * trial[4] + trial[5] * trial[5])
    )
    equivalent = jnp.sqrt(1.5 * second)
    excess = equivalent - (yield_eff + FRICTION * jnp.maximum(-pressure, 0.0))
    active = excess > 0.0
    rate = jnp.maximum(excess, 0.0) * slope
    drop = shear_thrice * rate
    scale = jnp.where(active, 1.0 - drop / jnp.where(active, equivalent, 1.0), 1.0)
    heat = HEAT_SCALE * TAYLOR_QUINNEY * (equivalent - drop) * rate
    updated = [pressure + scale * dev[k] for k in range(3)] + [
        scale * trial[k] for k in range(3, 6)
    ]
    return updated, heat


def six(gx, gp, gs):
    return [
        gx[0],
        gp[1],
        gs[2],
        0.5 * (gp[0] + gx[1]),
        0.5 * (gs[1] + gp[2]),
        0.5 * (gs[0] + gx[2]),
    ]


EDGE_ROWS = 8 * RING
EDGE_ALL = EDGE_ROWS + 7 * BS


def heat_kernel(
    wide, shear, warmth, capacity, face, columns, corner,
    chunks, even_out, odd_out, updated_out, partial_out,
    lowest, stacked,
):
    upper_x = lax.axis_index("gx") == 1
    upper_y = lax.axis_index("gy") == 1
    even = lax.rem(lax.axis_index("gz"), 2) == 0
    rows = PLANE
    half = LANES // 2
    lane = iota((rows, LANES), 1)
    row = iota((rows, LANES), 0)
    first = jnp.where(upper_y, LANES - 3, half)
    beside = (lane >= first) & (lane < first + 3)
    faces = {key: at for at, key in enumerate(FACE)}

    def joined(field, plane, side):
        side = pltpu.roll(side, (half - SLOT * field) % LANES, 1)
        return jnp.where(lane < half, plane, jnp.where(beside, side, 0.0))

    def far(field, i, side):
        at = faces[field, i]
        pair = at // 2
        plane = jnp.concatenate([face[2 * pair], face[2 * pair + 1]], axis=0)
        return joined(field, pltpu.roll(plane, half, 1) if at % 2 else plane, side)

    def layer(field, j):
        if 3 <= j < 11:
            at = (field * BS + j - 3) * rows
            return joined(field, wide[pl.ds(at, rows), :], columns[j - 3])
        side = corner[j] if j < 3 else corner[j - 11]
        i = j - 11 if j >= 11 else j if field < VELS else j - 1
        plane = far(field, i, side)
        return jnp.where(upper_x, plane, 0.0) if j < 3 else jnp.where(upper_x, 0.0, plane)

    outer = far(10, 0, corner[1])
    shears = [
        jnp.where(upper_x, outer, 0.0),
        joined(10, shear[...], columns[0]),
        jnp.where(upper_x, 0.0, outer),
    ]
    lowest[...] = jnp.zeros_like(lowest)
    stacked[pl.ds(MAIN, 4 * BS * 2), :] = jnp.zeros((4 * BS * 2, LANES), jnp.float32)
    stacked[pl.ds(2 * LANES + 96, 32), :] = jnp.zeros((32, LANES), jnp.float32)

    def node_terms(j):
        terms = []
        for c in range(VELS):
            here = layer(c, j)
            lowest[c, pl.ds(j - 1, 1), :] = here[0:1, :]
            above = jnp.where(row == rows - 1, 0.0, pltpu.roll(here, rows - 1, 0))
            total, change = here + above, above - here
            aside = pltpu.roll(total, LANES - 1, 1)
            terms.append((total + aside, aside - total, change + pltpu.roll(change, LANES - 1, 1)))
        return terms

    materials = [stress_terms(s) for s in shears]
    before = node_terms(1)
    for a in range(RING):
        after = node_terms(a + 2)
        grads = six(
            [after[c][0] - before[c][0] for c in range(VELS)],
            [after[c][2] + before[c][2] for c in range(VELS)],
            [after[c][1] + before[c][1] for c in range(VELS)],
        )
        block = 0 if a < 2 else 1 if a < 10 else 2
        yield_eff = layer(9, a + 1)
        trial = strained([layer(VELS + k, a + 1) for k in range(6)], grads, materials[block])
        updated, heat = returned(trial, yield_eff, materials[block])
        stacked[pl.ds(a * rows, rows), :] = heat
        for q, plane in enumerate(trial + [yield_eff, shears[block]]):
            partial_out[q, pl.ds(a, 1), :] = plane[rows - 1 : rows, :]
        if 1 <= a < 10:
            for k in range(6):
                updated_out[k, a - 1] = updated[k]
        before = after

    flat = []
    for c in range(VELS):
        here = lowest[c]
        aside = pltpu.roll(here, LANES - 1, 1)
        total, change = here + aside, aside - here
        nxt = pltpu.roll(total, rows - 1, 0)
        flat.append((nxt - total, nxt + total, change + pltpu.roll(change, rows - 1, 0)))
    for k, plane in enumerate(six(*[[flat[c][d] for c in range(VELS)] for d in range(3)])):
        partial_out[8 + k] = plane
    for q in range(PLANES):
        stacked[pl.ds(place(q), RING), :] = partial_out[q, pl.ds(0, RING), :]
    turned = jnp.transpose(pltpu.roll(stacked[...], SHIFT, 1))
    for g in range(chunks.shape[0]):
        chunks[g] = turned[g * BS : g * BS + 2 * BS, :]

    sub = iota((BS, LANES), 0)
    ups, downs = [], []
    for j in range(14):
        u = warmth_plane(j, warmth, face)
        c = capacity_plane(j, capacity, face)
        ups.append(jnp.where(sub > 4, u, pltpu.roll(c, 5, 0)))
        downs.append(jnp.where(sub < 3, u, pltpu.roll(c, 3, 0)))

    def fill(up_ref, down_ref):
        for q in range(8):
            up_ref[pl.ds(RING * q, RING), :] = partial_out[q, pl.ds(0, RING), :]
        for k in range(6):
            down_ref[pl.ds(RING * k, RING), :] = partial_out[8 + k, pl.ds(0, RING), :]
        down_ref[pl.ds(6 * RING, 2 * RING), :] = jnp.zeros((2 * RING, LANES), jnp.float32)
        for m in range(7):
            at = pl.ds(EDGE_ROWS + m * BS, BS)
            up_ref[at, :] = jnp.where(sub < 4, pltpu.roll(ups[2 * m], 4, 0), ups[2 * m + 1])
            down_ref[at, :] = jnp.where(sub < 4, downs[2 * m], pltpu.roll(downs[2 * m + 1], 4, 0))

    @pl.when(even)
    def _():
        fill(even_out, odd_out)

    @pl.when(jnp.logical_not(even))
    def _():
        fill(odd_out, even_out)


def force_kernel(
    updated, partial, even_in, odd_in, vel, mass, vel_out, stress_out, top, bottom
):
    at_z = lax.axis_index("gz")
    even = lax.rem(at_z, 2) == 0
    has_above = at_z < lax.axis_size("gz") - 1
    has_below = at_z > 0
    rows = ZB * BS
    row = iota((rows, LANES), 0)

    def below(q):
        at = pl.ds(RING * q, rows)
        return jnp.where(has_below, jnp.where(even, odd_in[at, :], even_in[at, :]), 0.0)

    def above(k):
        at = pl.ds(RING * k, rows)
        return jnp.where(has_above, jnp.where(even, even_in[at, :], odd_in[at, :]), 0.0)

    terms = stress_terms(partial[7])
    trial = strained([partial[k] for k in range(6)], [above(k) for k in range(6)], terms)
    for k, plane in enumerate(returned(trial, partial[6], terms)[0]):
        top[k] = plane
    terms = stress_terms(below(7))
    trial = strained([below(k) for k in range(6)], [partial[8 + k] for k in range(6)], terms)
    for k, plane in enumerate(returned(trial, below(6), terms)[0]):
        bottom[k] = plane

    def element_terms(j):
        terms = []
        for k in range(6):
            here = jnp.where(row == rows - 1, top[k, pl.ds(j + 1, 1), :], updated[k, j])
            if j > 0:
                stress_out[k, j - 1] = here[:, : LANES // 2]
            prev = jnp.where(row == 0, bottom[k, pl.ds(j + 1, 1), :], pltpu.roll(here, 1, 0))
            total, change = here + prev, here - prev
            aside = pltpu.roll(total, 1, 1)
            terms.append((total + aside, total - aside, change + pltpu.roll(change, 1, 1)))
        return terms

    before = element_terms(0)
    for x in range(BS):
        after = element_terms(x + 1)
        weights = 0.25 * TIME_STEP / mass[x]
        for c, (kx, kp, ks) in enumerate(((0, 3, 5), (3, 1, 4), (5, 4, 2))):
            force = (
                (after[kx][0] - before[kx][0])
                + (after[kp][2] + before[kp][2])
                + (after[ks][1] + before[ks][1])
            )
            vel_out[c, x] = vel[c, x] + force[:, : LANES // 2] * weights
        before = after


def conduct_kernel(chunks, warmth, capacity, face, even_in, odd_in, out):
    upper_x = lax.axis_index("gx") == 1
    at_z = lax.axis_index("gz")
    even = lax.rem(at_z, 2) == 0
    groups = lax.axis_size("gz")
    rows = ZB * BS
    at_flat = lax.axis_index("gy") * groups + at_z
    last = lax.axis_size("gy") * groups - 1
    lane = iota((rows, LANES), 1)
    row = iota((rows, LANES), 0)
    group = lane // rows
    sub = iota((BS, LANES), 0)

    heats = []
    for t, count in ((0, 8), (1, 4)):
        turned = []
        for k in range(groups):
            mixed = chunks[k, :, pl.ds(t * LANES, LANES)]
            for b in range(1, count):
                source = chunks[(b + k) % groups, :, pl.ds(t * LANES, LANES)]
                mixed = jnp.where(group == b, source, mixed)
            turned.append(pltpu.roll(mixed, k * rows, 1) if k else mixed)
        for b in range(count):
            heat = turned[(0 - b) % groups]
            for g in range(1, groups):
                heat = jnp.where(group == g, turned[(g - b) % groups], heat)
            heats.append(heat)

    planes = []
    for q in range(PLANES):
        tile, at = divmod(place(q), LANES)
        plane = jnp.zeros((rows, LANES), jnp.float32)
        for g in range(groups):
            to = g if q < 8 else g - 1
            if to < 0:
                continue
            source = chunks[g, :, pl.ds(tile * LANES, LANES)]
            inside = (lane >= to * rows) & (lane < to * rows + RING)
            plane = jnp.where(inside, pltpu.roll(source, (to * rows - at) % LANES, 1), plane)
        planes.append(plane)
    terms = stress_terms(planes[7])
    seam = returned(strained(planes[:6], planes[8:], terms), planes[6], terms)[1]
    for a in range(RING):
        heats[a] = jnp.where(
            lane % rows == rows - 1, pltpu.roll(seam, rows - 1 - a, 1), heats[a]
        )

    u_rows = (row >= jnp.where(at_flat == 0, 4, 1)) & (row < jnp.where(at_flat == last, 12, 15))
    d_rows = (row >= jnp.where(at_flat == 0, 4, 2)) & (row < jnp.where(at_flat == last, 12, 14))
    us, caps = [], []
    for j in range(14):
        at = pl.ds(EDGE_ROWS + j // 2 * BS, BS)
        low = jnp.where(even, odd_in[at, :], even_in[at, :])
        high = jnp.where(even, even_in[at, :], odd_in[at, :])
        if j % 2:
            low = pltpu.roll(low, 4, 0)
        else:
            high = pltpu.roll(high, 4, 0)
        mid = pltpu.roll(warmth_plane(j, warmth, face), 4, 0)
        u = jnp.concatenate([jnp.where(sub < 4, low, mid), jnp.where(sub < 4, mid, high)], axis=0)
        us.append(jnp.where(u_rows, u, 0.0))
        mid = pltpu.roll(capacity_plane(j, capacity, face), 4, 0)
        caps.append(
            6.0
            + jnp.concatenate(
                [
                    jnp.where(sub < 4, pltpu.roll(low, 3, 0), mid),
                    jnp.where(sub < 4, mid, pltpu.roll(high, 5, 0)),
                ],
                axis=0,
            )
        )

    def around(fields, a):
        here = fields[a]
        total = fields[a - 1] + fields[a + 1]
        total = total + pltpu.roll(here, 1, 0) + pltpu.roll(here, rows - 1, 0)
        total = total + jnp.where(lane == 0, 0.0, pltpu.roll(here, 1, 1))
        return total + jnp.where(lane == LANES - 1, 0.0, pltpu.roll(here, LANES - 1, 1))

    def inside(a):
        if a < 2:
            return d_rows & upper_x
        if a >= 10:
            return d_rows & jnp.logical_not(upper_x)
        return d_rows

    theta = 0.5 * (UPPER_BOUND + LOWER_BOUND)
    half_width = 0.5 * (UPPER_BOUND - LOWER_BOUND)
    sig = theta / half_width
    weight_now = 1.0 / sig
    misfit, step, total = {}, {}, {}
    for a in range(RING):
        misfit[a] = heats[a] - 6.0 * us[a + 1] + around(us, a + 1)
        step[a] = jnp.where(inside(a), misfit[a] * (1.0 / theta), 0.0)
        total[a] = us[a + 1] + step[a]
    for sweep in range(1, SWEEPS):
        weight_next = 1.0 / (2.0 * sig - weight_now)
        new_misfit, new_step = {}, {}
        for a in range(sweep, RING - sweep):
            new_misfit[a] = misfit[a] - caps[a + 1] * step[a] + around(step, a)
            moved = (weight_next * weight_now) * step[a] + (
                2.0 * weight_next / half_width
            ) * new_misfit[a]
            new_step[a] = jnp.where(inside(a), moved, 0.0)
            total[a] = total[a] + new_step[a]
        misfit, step, weight_now = new_misfit, new_step, weight_next
    for x in range(BS):
        result = total[x + 2]
        out[x] = jnp.where(sub < 4, pltpu.roll(result[:BS], 4, 0), pltpu.roll(result[BS:], 4, 0))


def f32(*shape):
    return jax.ShapeDtypeStruct(shape, jnp.float32)


def call(kernel, out_shape, *args, scratch=(), in_specs=None, flops=0):
    moved = 4 * sum(a.size for a in args) + 4 * sum(o.size for o in jax.tree.leaves(out_shape))
    options = {} if in_specs is None else dict(in_specs=in_specs)
    return pl.pallas_call(
        kernel,
        out_shape=out_shape,
        scratch_shapes=scratch,
        compiler_params=pltpu.CompilerParams(vmem_limit_bytes=VMEM_BYTES),
        cost_estimate=pl.CostEstimate(flops=flops, bytes_accessed=moved, transcendentals=0),
        **options,
    )(*args)


def room(*shape):
    return pltpu.VMEM(shape, jnp.float32)


def paired(count, first):
    pairs = []
    for i in range(first, count - 1, 2):
        pairs += [(i, i + 1), (i + 1, i)]
    return pairs


def two_round_body(
    corner_speed_prior,
    brick_stress_tensor_now,
    compact_onset_strength,
    corner_weights_diagonal,
    substance_labels,
    brick_warmth_prior,
    caloric_capacity_per_timestep,
):
    rows = PLANE
    groups = lax.axis_size("gz")
    chain = groups * lax.axis_size("gy")
    labels = jnp.transpose(substance_labels, (0, 2, 1))
    raw = (
        labels,
        corner_speed_prior,
        brick_stress_tensor_now,
        compact_onset_strength,
        brick_warmth_prior,
        caloric_capacity_per_timestep,
    )
    raw = [pltpu.with_memory_space_constraint(array, pltpu.HBM) for array in raw]
    second = compact_onset_strength.shape[-1]
    wide, shear, face, columns, corner = call(
        pack_kernel,
        (
            f32(10 * BS * rows, LANES),
            f32(rows, LANES),
            f32(FACE_TILES + 4, BS, LANES),
            f32(BS, rows, LANES),
            f32(3, rows, LANES),
        ),
        *raw,
        in_specs=[pl.BlockSpec(memory_space=pltpu.HBM)] * len(raw),
        scratch=(
            room(10, BS, rows, second),
            pltpu.VMEM(labels.shape, jnp.int32),
            pltpu.SemaphoreType.DMA((len(raw),)),
        ),
    )
    face = lax.ppermute(face, "gx", [(0, 1), (1, 0)])
    columns = lax.ppermute(columns, "gy", [(0, 1), (1, 0)])
    corner = lax.ppermute(corner, ("gx", "gy"), [(0, 3), (3, 0), (1, 2), (2, 1)])
    chunks, even, odd, updated, partial = call(
        heat_kernel,
        (
            f32(groups, rows, 3 * LANES),
            f32(EDGE_ALL, LANES),
            f32(EDGE_ALL, LANES),
            f32(6, BS + 1, rows, LANES),
            f32(PLANES, rows, LANES),
        ),
        wide,
        shear,
        brick_warmth_prior,
        caloric_capacity_per_timestep,
        face,
        columns,
        corner,
        scratch=(room(VELS, rows, LANES), room(3 * LANES, LANES)),
    )
    chunks = lax.all_to_all(chunks, "gz", split_axis=0, concat_axis=0, tiled=True)
    even = lax.ppermute(even, ("gy", "gz"), paired(chain, 0))
    odd = lax.ppermute(odd, ("gy", "gz"), paired(chain, 1))
    corner_speed_later, projected_brick_stress_tensor = call(
        force_kernel,
        (f32(*corner_speed_prior.shape), f32(*brick_stress_tensor_now.shape)),
        updated,
        partial,
        even,
        odd,
        corner_speed_prior,
        corner_weights_diagonal,
        scratch=(room(6, rows, LANES), room(6, rows, LANES)),
    )
    diffused_kelvin_field = call(
        conduct_kernel,
        f32(*brick_warmth_prior.shape),
        chunks,
        brick_warmth_prior,
        caloric_capacity_per_timestep,
        face,
        even,
        odd,
    )
    return (corner_speed_later, projected_brick_stress_tensor, diffused_kelvin_field)


def solution(mesh):
    placed = (
        P(None, "gx", "gz", "gy"),
        P(None, "gx", "gz", "gy"),
        P("gx", "gz", "gy"),
        P("gx", "gz", "gy"),
        P("gx", None, "gy"),
        P("gx", ("gy", "gz"), None),
        P("gx", ("gy", "gz"), None),
    )
    return jax.shard_map(
        two_round_body if two_rounds_fit(mesh) else body,
        mesh=mesh,
        in_specs=placed,
        out_specs=(
            P(None, "gx", "gz", "gy"),
            P(None, "gx", "gz", "gy"),
            P("gx", ("gy", "gz"), None),
        ),
        check_vma=False,
    )
```

```python
import jax
import jax.numpy as jnp
from jax import lax
from jax.experimental import pallas as pl
from jax.experimental.pallas import tpu as pltpu
from jax.sharding import PartitionSpec as P

BS = 8
ZB = 2
SWEEPS = 3


TIME_STEP = 0.2
VISCOSITY = 0.4
FRICTION = 0.5
TAYLOR_QUINNEY = 0.9
HEAT_SCALE = 5.0
ELASTIC_YIELD = 10000.0
LOWER_BOUND = 0.5
UPPER_BOUND = 16.0


def extended(cells, sides, width):
    for axis, dim in sides:
        count = lax.axis_size(axis)
        ends = count - 1
        head = lax.slice_in_dim(cells, 0, width, axis=dim)
        tail = lax.slice_in_dim(cells, cells.shape[dim] - width, cells.shape[dim], axis=dim)
        cells = jnp.concatenate(
            [
                lax.ppermute(tail, axis, [(i, (i + 1) % count) for i in range(ends)]),
                cells,
                lax.ppermute(head, axis, [((i + 1) % count, i) for i in range(ends)]),
            ],
            axis=dim,
        )
    return cells


def shifted_diff(values, axis_num):
    extent = values.shape[axis_num]
    return lax.slice_in_dim(values, 1, extent, axis=axis_num) - lax.slice_in_dim(
        values, 0, extent - 1, axis=axis_num
    )


def shifted_sum(values, axis_num):
    extent = values.shape[axis_num]
    return lax.slice_in_dim(values, 1, extent, axis=axis_num) + lax.slice_in_dim(
        values, 0, extent - 1, axis=axis_num
    )


def spread_blocks(values, width):
    extent_a, extent_b, extent_c = values.shape
    wide = jnp.broadcast_to(
        values[:, None, :, None, :, None], (extent_a, width, extent_b, width, extent_c, width)
    )
    return wide.reshape(extent_a * width, extent_b * width, extent_c * width)


def moduli(substance_labels):
    shear_mod = jnp.where(
        substance_labels == 0, 3.0, jnp.where(substance_labels == 1, 2.0, 0.8)
    ).astype(jnp.float32)
    bulk_mod = jnp.where(
        substance_labels == 0, 5.0, jnp.where(substance_labels == 1, 4.0, 1.2)
    ).astype(jnp.float32)
    return (shear_mod, bulk_mod)


def face_term(element_values, axis_num):
    others = [other for other in (0, 1, 2) if other != axis_num]
    return shifted_diff(shifted_sum(shifted_sum(element_values, others[0]), others[1]), axis_num)


def element_state(node_vel, props):
    grad_x = 0.25 * shifted_diff(shifted_sum(shifted_sum(node_vel, 2), 3), 1)
    grad_y = 0.25 * shifted_diff(shifted_sum(shifted_sum(node_vel, 1), 3), 2)
    grad_z = 0.25 * shifted_diff(shifted_sum(shifted_sum(node_vel, 1), 2), 3)
    yield_eff = props[6]
    shear_mod = props[7]
    bulk_mod = props[8]
    strain_xx = TIME_STEP * grad_x[0]
    strain_yy = TIME_STEP * grad_y[1]
    strain_zz = TIME_STEP * grad_z[2]
    strain_xy = TIME_STEP * (0.5 * (grad_y[0] + grad_x[1]))
    strain_yz = TIME_STEP * (0.5 * (grad_z[1] + grad_y[2]))
    strain_xz = TIME_STEP * (0.5 * (grad_z[0] + grad_x[2]))
    volume = strain_xx + strain_yy + strain_zz
    vol_third = volume / 3.0
    trial_xx = props[0] + 2.0 * shear_mod * (strain_xx - vol_third) + bulk_mod * volume
    trial_yy = props[1] + 2.0 * shear_mod * (strain_yy - vol_third) + bulk_mod * volume
    trial_zz = props[2] + 2.0 * shear_mod * (strain_zz - vol_third) + bulk_mod * volume
    trial_xy = props[3] + 2.0 * shear_mod * strain_xy
    trial_yz = props[4] + 2.0 * shear_mod * strain_yz
    trial_xz = props[5] + 2.0 * shear_mod * strain_xz
    pressure = (trial_xx + trial_yy + trial_zz) / 3.0
    dev_xx = trial_xx - pressure
    dev_yy = trial_yy - pressure
    dev_zz = trial_zz - pressure
    second = (
        dev_xx * dev_xx
        + dev_yy * dev_yy
        + dev_zz * dev_zz
        + 2.0 * (trial_xy * trial_xy + trial_yz * trial_yz + trial_xz * trial_xz)
    )
    equivalent = jnp.sqrt(1.5 * second)
    flow_stress = yield_eff + FRICTION * jnp.maximum(-pressure, 0.0)
    excess = equivalent - flow_stress
    active = excess > 0.0
    plastic_rate = jnp.maximum(excess, 0.0) / (3.0 * shear_mod + VISCOSITY / TIME_STEP)
    scale_back = jnp.where(
        active, 1.0 - 3.0 * shear_mod * plastic_rate / jnp.where(active, equivalent, 1.0), 1.0
    )
    updated = jnp.stack(
        [
            pressure + scale_back * dev_xx,
            pressure + scale_back * dev_yy,
            pressure + scale_back * dev_zz,
            scale_back * trial_xy,
            scale_back * trial_yz,
            scale_back * trial_xz,
        ]
    )
    heat_local = (
        HEAT_SCALE * TAYLOR_QUINNEY * (equivalent - 3.0 * shear_mod * plastic_rate) * plastic_rate
    )
    return (updated, heat_local)


def node_forces(updated):
    force_x = face_term(updated[0], 0) + face_term(updated[3], 1) + face_term(updated[5], 2)
    force_y = face_term(updated[3], 0) + face_term(updated[1], 1) + face_term(updated[4], 2)
    force_z = face_term(updated[5], 0) + face_term(updated[4], 1) + face_term(updated[2], 2)
    return -0.25 * jnp.stack([force_x, force_y, force_z])


def mechanics(padded, corner_weights_diagonal):
    node_vel = padded[0:3]
    updated, heat_local = element_state(node_vel, padded[3:, :-1, :-1, :-1])
    force = node_forces(updated)
    corner_speed_later = node_vel[:, 1:-1, 1:-1, 1:-1] - TIME_STEP * force / corner_weights_diagonal
    return (corner_speed_later, updated[:, 1:, 1:, 1:], heat_local[1:, 1:, 1:])


def stencil(values, padded, matrix_main_entries):
    beside = padded[2:, 1:-1, 1:-1] + padded[:-2, 1:-1, 1:-1]
    beside = beside + padded[1:-1, 2:, 1:-1] + padded[1:-1, :-2, 1:-1]
    beside = beside + padded[1:-1, 1:-1, 2:] + padded[1:-1, 1:-1, :-2]
    return matrix_main_entries * values - beside


def diffuse_thermal_once(values, matrix_main_entries):
    haloed = extended(values, (("gx", 0), (("gy", "gz"), 1)), 1)
    padded = jnp.pad(haloed, ((0, 0), (0, 0), (1, 1)))
    return stencil(values, padded, matrix_main_entries)


def polynomial_relaxation(
    brick_warmth_prior,
    caloric_capacity_per_timestep,
    plastic_work_heating_rise,
    diffuse_thermal_field,
    inward_cell_flags,
):
    center_value = 0.5 * (UPPER_BOUND + LOWER_BOUND)
    half_width = 0.5 * (UPPER_BOUND - LOWER_BOUND)
    ratio_sig = center_value / half_width
    matrix_main_entries = 6.0 + caloric_capacity_per_timestep
    linear_system_target = (
        caloric_capacity_per_timestep * brick_warmth_prior + plastic_work_heating_rise
    )
    implicit_kelvin_result = brick_warmth_prior
    equation_misfit = (
        linear_system_target - diffuse_thermal_field(implicit_kelvin_result, matrix_main_entries)
    ) * inward_cell_flags
    weight_now = 1.0 / ratio_sig
    search_direction = equation_misfit / center_value
    for sweep_index in range(SWEEPS):
        implicit_kelvin_result = implicit_kelvin_result + search_direction
        if sweep_index + 1 < SWEEPS:
            equation_misfit = (
                equation_misfit - diffuse_thermal_field(search_direction, matrix_main_entries)
            ) * inward_cell_flags
            weight_next = 1.0 / (2.0 * ratio_sig - weight_now)
            search_direction = (
                weight_next * weight_now * search_direction
                + 2.0 * weight_next / half_width * equation_misfit
            )
            weight_now = weight_next
    return implicit_kelvin_result


def body(
    corner_speed_prior,
    brick_stress_tensor_now,
    compact_onset_strength,
    corner_weights_diagonal,
    substance_labels,
    brick_warmth_prior,
    caloric_capacity_per_timestep,
):
    z_index = lax.axis_index("gz")
    local_mat = lax.dynamic_slice_in_dim(substance_labels, z_index * ZB, ZB, 1)
    shear_blk, bulk_blk = moduli(local_mat)
    powder_cells = spread_blocks(local_mat, BS) == 2
    yield_eff = jnp.where(powder_cells, compact_onset_strength, ELASTIC_YIELD)
    stacked = jnp.concatenate(
        [
            corner_speed_prior,
            brick_stress_tensor_now,
            yield_eff[None],
            spread_blocks(shear_blk, BS)[None],
            spread_blocks(bulk_blk, BS)[None],
        ],
        axis=0,
    )
    padded = extended(stacked, (("gx", 1), ("gy", 3), ("gz", 2)), 1)
    corner_speed_later, projected_brick_stress_tensor, heat_local = mechanics(
        padded, corner_weights_diagonal
    )
    moved = lax.all_to_all(heat_local, "gz", split_axis=2, concat_axis=1, tiled=True)
    plastic_work_heating_rise = jnp.transpose(moved, (0, 2, 1))
    diffused_kelvin_field = polynomial_relaxation(
        brick_warmth_prior,
        caloric_capacity_per_timestep,
        plastic_work_heating_rise,
        diffuse_thermal_once,
        1.0,
    )
    return (corner_speed_later, projected_brick_stress_tensor, diffused_kelvin_field)


LANES = 128
SHIFT = 4
VELS = 3
FIELDS = 11
SLOT = 4
RING = 12
PLANES = 14
MAIN = RING * 2 * BS
VMEM_BYTES = 48 * 1024 * 1024


def two_rounds_fit(mesh):
    return mesh.shape["gx"] == 2 and mesh.shape["gy"] == 2 and mesh.shape["gz"] == 8


def iota(shape, dim):
    return lax.broadcasted_iota(jnp.int32, shape, dim)


def place(q):
    return MAIN + RING * q if q < 5 else 2 * LANES + RING * (q - 5)


def bulk_of(shear_mod):
    return jnp.where(
        shear_mod == 3.0,
        5.0,
        jnp.where(shear_mod == 2.0, 4.0, jnp.where(shear_mod == 0.0, 0.0, 1.2)),
    )


def own_labels(labels):
    second, press = labels.shape
    rows = ZB * BS
    first = lax.axis_index("gz") * ZB
    pick = iota((rows, press), 1) == first + iota((rows, press), 0) // BS
    spread = iota((second, LANES), 0) == (iota((second, LANES), 1) // BS) % second
    picked = lax.dot_general(
        pick.astype(jnp.float32),
        labels.astype(jnp.float32),
        (((1,), (1,)), ((), ())),
        preferred_element_type=jnp.float32,
    )
    return jnp.dot(picked, spread.astype(jnp.float32), preferred_element_type=jnp.float32)


FACE = (
    [(field, i) for field in range(VELS) for i in range(3)]
    + [(field, i) for field in range(VELS, 10) for i in range(2)]
    + [(10, 0)]
)
FACE_TILES = len(FACE) // 2 * ZB
PLANE = ZB * BS


def slot_at(lane, field, first):
    where = lax.rem(lane + (2 * LANES - SLOT * field) - first, LANES)
    return where < 3


def pack_kernel(
    labels, vel, stress, onset, warmth, capacity,
    wide, shear_out, face, columns, corner,
    own, own_labels_in, sems,
):
    lower_x = lax.axis_index("gx") == 0
    lower_y = lax.axis_index("gy") == 0
    deep = jnp.where(lower_x, BS - 3, 0)
    shallow = jnp.where(lower_x, BS - 2, 0)
    edge = jnp.where(lower_x, BS - 1, 0)
    copies = [
        pltpu.make_async_copy(*pair, sems.at[n])
        for n, pair in enumerate(
            (
                (labels, own_labels_in),
                (vel, own.at[pl.ds(0, VELS)]),
                (onset, own.at[9]),
                (stress, own.at[pl.ds(VELS, 6)]),
                (warmth.at[pl.ds(deep, 3)], face.at[pl.ds(FACE_TILES, 3)]),
                (capacity.at[edge], face.at[FACE_TILES + 3]),
            )
        )
    ]
    for copy in copies:
        copy.start()
    lane = iota((PLANE, LANES), 1)
    half = LANES // 2
    copies[0].wait()
    material = own_labels(own_labels_in[0])
    shear_mod = jnp.where(material == 0.0, 3.0, jnp.where(material == 1.0, 2.0, 0.8))
    shear_out[...] = shear_mod
    copies[1].wait()
    copies[2].wait()
    for field in range(VELS):
        wide[pl.ds(field * BS * PLANE, BS * PLANE), 0:half] = own[field].reshape(BS * PLANE, half)
    powder = material[:, 0:half] == 2.0
    for x in range(BS):
        at = pl.ds((9 * BS + x) * PLANE, PLANE)
        wide[at, 0:half] = jnp.where(powder, own[9, x], ELASTIC_YIELD)
    copies[3].wait()
    for field in range(VELS, 9):
        wide[pl.ds(field * BS * PLANE, BS * PLANE), 0:half] = own[field].reshape(BS * PLANE, half)

    def read(field, x):
        if field == 10:
            return shear_mod
        return wide[pl.ds(pl.multiple_of((field * BS + x) * PLANE, PLANE), PLANE), :]

    for pair in range(len(FACE) // 2):
        one, two = (
            read(field, (deep if field < VELS else shallow) + i)
            for field, i in FACE[2 * pair : 2 * pair + 2]
        )
        joined = jnp.where(lane < half, one, pltpu.roll(two, half, 1))
        face[2 * pair] = joined[:BS]
        face[2 * pair + 1] = joined[BS:]
    first = jnp.where(lower_y, half - 3, 0)
    insides = [slot_at(lane, field, first) for field in range(FIELDS)]
    for x in range(BS):
        packed = jnp.zeros((PLANE, LANES), jnp.float32)
        for field in range(FIELDS):
            turned = read(field, x)
            if field:
                turned = pltpu.roll(turned, SLOT * field, 1)
            packed = jnp.where(insides[field], turned, packed)
        columns[x] = packed
    for i in range(3):
        corner[i] = columns[deep + i]
    copies[4].wait()
    copies[5].wait()


def warmth_plane(j, warmth, face):
    upper_x = lax.axis_index("gx") == 1
    if j < 3:
        return jnp.where(upper_x, face[FACE_TILES + j], 0.0)
    if j < 11:
        return warmth[j - 3]
    return jnp.where(upper_x, 0.0, face[FACE_TILES + j - 11])


def capacity_plane(j, capacity, face):
    upper_x = lax.axis_index("gx") == 1
    if 3 <= j < 11:
        return capacity[j - 3]
    if j == 2 or j == 11:
        return jnp.where(upper_x == (j == 2), face[FACE_TILES + 3], 0.0)
    return jnp.zeros((BS, LANES), jnp.float32)


def stress_terms(shear_mod):
    bulk_mod = bulk_of(shear_mod)
    return (
        0.5 * TIME_STEP * shear_mod,
        0.25 * TIME_STEP * (bulk_mod - 2.0 / 3.0 * shear_mod),
        3.0 * shear_mod,
        1.0 / (3.0 * shear_mod + VISCOSITY / TIME_STEP),
    )


def strained(before, grads, terms):
    twice, volume_term = terms[0], terms[1]
    volume = volume_term * (grads[0] + grads[1] + grads[2])
    return [
        before[k] + twice * grads[k] + (volume if k < 3 else 0.0) for k in range(6)
    ]


def returned(trial, yield_eff, terms):
    shear_thrice, slope = terms[2], terms[3]
    pressure = (trial[0] + trial[1] + trial[2]) * (1.0 / 3.0)
    dev = [trial[k] - pressure for k in range(3)]
    second = (
        dev[0] * dev[0]
        + dev[1] * dev[1]
        + dev[2] * dev[2]
        + 2.0 * (trial[3] * trial[3] + trial[4] * trial[4] + trial[5] * trial[5])
    )
    equivalent = jnp.sqrt(1.5 * second)
    excess = equivalent - (yield_eff + FRICTION * jnp.maximum(-pressure, 0.0))
    active = excess > 0.0
    rate = jnp.maximum(excess, 0.0) * slope
    drop = shear_thrice * rate
    scale = jnp.where(active, 1.0 - drop / jnp.where(active, equivalent, 1.0), 1.0)
    heat = HEAT_SCALE * TAYLOR_QUINNEY * (equivalent - drop) * rate
    updated = [pressure + scale * dev[k] for k in range(3)] + [
        scale * trial[k] for k in range(3, 6)
    ]
    return updated, heat


def six(gx, gp, gs):
    return [
        gx[0],
        gp[1],
        gs[2],
        0.5 * (gp[0] + gx[1]),
        0.5 * (gs[1] + gp[2]),
        0.5 * (gs[0] + gx[2]),
    ]


EDGE_ROWS = 8 * RING
EDGE_ALL = EDGE_ROWS + 7 * BS


def heat_kernel(
    wide, shear, warmth, capacity, face, columns, corner,
    chunks, even_out, odd_out, updated_out, partial_out,
    lowest, stacked, ext,
):
    upper_x = lax.axis_index("gx") == 1
    upper_y = lax.axis_index("gy") == 1
    even = lax.rem(lax.axis_index("gz"), 2) == 0
    rows = PLANE
    half = LANES // 2
    lane = iota((rows, LANES), 1)
    row = iota((rows, LANES), 0)
    first = jnp.where(upper_y, LANES - 3, half)
    beside = (lane >= first) & (lane < first + 3)
    faces = {key: at for at, key in enumerate(FACE)}

    def joined(field, plane, side):
        side = pltpu.roll(side, (half - SLOT * field) % LANES, 1)
        return jnp.where(lane < half, plane, jnp.where(beside, side, 0.0))

    def far(field, i, side):
        at = faces[field, i]
        pair = at // 2
        plane = jnp.concatenate([face[2 * pair], face[2 * pair + 1]], axis=0)
        return joined(field, pltpu.roll(plane, half, 1) if at % 2 else plane, side)

    def layer(field, j):
        if 3 <= j < 11:
            at = (field * BS + j - 3) * rows
            return joined(field, wide[pl.ds(at, rows), :], columns[j - 3])
        side = corner[j] if j < 3 else corner[j - 11]
        i = j - 11 if j >= 11 else j if field < VELS else j - 1
        plane = far(field, i, side)
        return jnp.where(upper_x, plane, 0.0) if j < 3 else jnp.where(upper_x, 0.0, plane)

    outer = far(10, 0, corner[1])
    shears = [
        jnp.where(upper_x, outer, 0.0),
        joined(10, shear[...], columns[0]),
        jnp.where(upper_x, 0.0, outer),
    ]
    for field in range(10):
        for j in range(1, 14 if field < VELS else 13):
            ext[field, j] = layer(field, j)
    lowest[...] = jnp.zeros_like(lowest)
    stacked[pl.ds(MAIN, 4 * BS * 2), :] = jnp.zeros((4 * BS * 2, LANES), jnp.float32)
    stacked[pl.ds(2 * LANES + 96, 32), :] = jnp.zeros((32, LANES), jnp.float32)

    def node_terms(j):
        terms = []
        for c in range(VELS):
            here = ext[c, j]
            lowest[c, pl.ds(j - 1, 1), :] = here[0:1, :]
            above = jnp.where(row == rows - 1, 0.0, pltpu.roll(here, rows - 1, 0))
            total, change = here + above, above - here
            aside = pltpu.roll(total, LANES - 1, 1)
            terms.append((total + aside, aside - total, change + pltpu.roll(change, LANES - 1, 1)))
        return terms

    materials = [stress_terms(s) for s in shears]
    before = node_terms(1)
    for a in range(RING):
        after = node_terms(a + 2)
        grads = six(
            [after[c][0] - before[c][0] for c in range(VELS)],
            [after[c][2] + before[c][2] for c in range(VELS)],
            [after[c][1] + before[c][1] for c in range(VELS)],
        )
        block = 0 if a < 2 else 1 if a < 10 else 2
        yield_eff = ext[9, a + 1]
        trial = strained([ext[VELS + k, a + 1] for k in range(6)], grads, materials[block])
        updated, heat = returned(trial, yield_eff, materials[block])
        stacked[pl.ds(a * rows, rows), :] = heat
        for q, plane in enumerate(trial + [yield_eff, shears[block]]):
            partial_out[q, pl.ds(a, 1), :] = plane[rows - 1 : rows, :]
        if 1 <= a < 10:
            for k in range(6):
                updated_out[k, a - 1] = updated[k]
        before = after

    flat = []
    for c in range(VELS):
        here = lowest[c]
        aside = pltpu.roll(here, LANES - 1, 1)
        total, change = here + aside, aside - here
        nxt = pltpu.roll(total, rows - 1, 0)
        flat.append((nxt - total, nxt + total, change + pltpu.roll(change, rows - 1, 0)))
    for k, plane in enumerate(six(*[[flat[c][d] for c in range(VELS)] for d in range(3)])):
        partial_out[8 + k] = plane
    for q in range(PLANES):
        stacked[pl.ds(place(q), RING), :] = partial_out[q, pl.ds(0, RING), :]
    turned = jnp.transpose(pltpu.roll(stacked[...], SHIFT, 1))
    for g in range(chunks.shape[0]):
        chunks[g] = turned[g * BS : g * BS + 2 * BS, :]

    sub = iota((BS, LANES), 0)
    ups, downs = [], []
    for j in range(14):
        u = warmth_plane(j, warmth, face)
        c = capacity_plane(j, capacity, face)
        ups.append(jnp.where(sub > 4, u, pltpu.roll(c, 5, 0)))
        downs.append(jnp.where(sub < 3, u, pltpu.roll(c, 3, 0)))

    def fill(up_ref, down_ref):
        for q in range(8):
            up_ref[pl.ds(RING * q, RING), :] = partial_out[q, pl.ds(0, RING), :]
        for k in range(6):
            down_ref[pl.ds(RING * k, RING), :] = partial_out[8 + k, pl.ds(0, RING), :]
        down_ref[pl.ds(6 * RING, 2 * RING), :] = jnp.zeros((2 * RING, LANES), jnp.float32)
        for m in range(7):
            at = pl.ds(EDGE_ROWS + m * BS, BS)
            up_ref[at, :] = jnp.where(sub < 4, pltpu.roll(ups[2 * m], 4, 0), ups[2 * m + 1])
            down_ref[at, :] = jnp.where(sub < 4, downs[2 * m], pltpu.roll(downs[2 * m + 1], 4, 0))

    @pl.when(even)
    def _():
        fill(even_out, odd_out)

    @pl.when(jnp.logical_not(even))
    def _():
        fill(odd_out, even_out)


def force_kernel(
    updated, partial, even_in, odd_in, vel, mass, vel_out, stress_out, top, bottom
):
    at_z = lax.axis_index("gz")
    even = lax.rem(at_z, 2) == 0
    has_above = at_z < lax.axis_size("gz") - 1
    has_below = at_z > 0
    rows = ZB * BS
    row = iota((rows, LANES), 0)

    def below(q):
        at = pl.ds(RING * q, rows)
        return jnp.where(has_below, jnp.where(even, odd_in[at, :], even_in[at, :]), 0.0)

    def above(k):
        at = pl.ds(RING * k, rows)
        return jnp.where(has_above, jnp.where(even, even_in[at, :], odd_in[at, :]), 0.0)

    terms = stress_terms(partial[7])
    trial = strained([partial[k] for k in range(6)], [above(k) for k in range(6)], terms)
    for k, plane in enumerate(returned(trial, partial[6], terms)[0]):
        top[k] = plane
    terms = stress_terms(below(7))
    trial = strained([below(k) for k in range(6)], [partial[8 + k] for k in range(6)], terms)
    for k, plane in enumerate(returned(trial, below(6), terms)[0]):
        bottom[k] = plane

    def element_terms(j):
        terms = []
        for k in range(6):
            here = jnp.where(row == rows - 1, top[k, pl.ds(j + 1, 1), :], updated[k, j])
            if j > 0:
                stress_out[k, j - 1] = here[:, : LANES // 2]
            prev = jnp.where(row == 0, bottom[k, pl.ds(j + 1, 1), :], pltpu.roll(here, 1, 0))
            total, change = here + prev, here - prev
            aside = pltpu.roll(total, 1, 1)
            terms.append((total + aside, total - aside, change + pltpu.roll(change, 1, 1)))
        return terms

    before = element_terms(0)
    for x in range(BS):
        after = element_terms(x + 1)
        weights = 0.25 * TIME_STEP / mass[x]
        for c, (kx, kp, ks) in enumerate(((0, 3, 5), (3, 1, 4), (5, 4, 2))):
            force = (
                (after[kx][0] - before[kx][0])
                + (after[kp][2] + before[kp][2])
                + (after[ks][1] + before[ks][1])
            )
            vel_out[c, x] = vel[c, x] + force[:, : LANES // 2] * weights
        before = after


def conduct_kernel(chunks, warmth, capacity, face, even_in, odd_in, out):
    upper_x = lax.axis_index("gx") == 1
    at_z = lax.axis_index("gz")
    even = lax.rem(at_z, 2) == 0
    groups = lax.axis_size("gz")
    rows = ZB * BS
    at_flat = lax.axis_index("gy") * groups + at_z
    last = lax.axis_size("gy") * groups - 1
    lane = iota((rows, LANES), 1)
    row = iota((rows, LANES), 0)
    group = lane // rows
    sub = iota((BS, LANES), 0)

    heats = []
    for t, count in ((0, 8), (1, 4)):
        turned = []
        for k in range(groups):
            mixed = chunks[k, :, pl.ds(t * LANES, LANES)]
            for b in range(1, count):
                source = chunks[(b + k) % groups, :, pl.ds(t * LANES, LANES)]
                mixed = jnp.where(group == b, source, mixed)
            turned.append(pltpu.roll(mixed, k * rows, 1) if k else mixed)
        for b in range(count):
            heat = turned[(0 - b) % groups]
            for g in range(1, groups):
                heat = jnp.where(group == g, turned[(g - b) % groups], heat)
            heats.append(heat)

    planes = []
    for q in range(PLANES):
        tile, at = divmod(place(q), LANES)
        plane = jnp.zeros((rows, LANES), jnp.float32)
        for g in range(groups):
            to = g if q < 8 else g - 1
            if to < 0:
                continue
            source = chunks[g, :, pl.ds(tile * LANES, LANES)]
            inside = (lane >= to * rows) & (lane < to * rows + RING)
            plane = jnp.where(inside, pltpu.roll(source, (to * rows - at) % LANES, 1), plane)
        planes.append(plane)
    terms = stress_terms(planes[7])
    seam = returned(strained(planes[:6], planes[8:], terms), planes[6], terms)[1]
    for a in range(RING):
        heats[a] = jnp.where(
            lane % rows == rows - 1, pltpu.roll(seam, rows - 1 - a, 1), heats[a]
        )

    u_rows = (row >= jnp.where(at_flat == 0, 4, 1)) & (row < jnp.where(at_flat == last, 12, 15))
    d_rows = (row >= jnp.where(at_flat == 0, 4, 2)) & (row < jnp.where(at_flat == last, 12, 14))
    us, caps = [], []
    for j in range(14):
        at = pl.ds(EDGE_ROWS + j // 2 * BS, BS)
        low = jnp.where(even, odd_in[at, :], even_in[at, :])
        high = jnp.where(even, even_in[at, :], odd_in[at, :])
        if j % 2:
            low = pltpu.roll(low, 4, 0)
        else:
            high = pltpu.roll(high, 4, 0)
        mid = pltpu.roll(warmth_plane(j, warmth, face), 4, 0)
        u = jnp.concatenate([jnp.where(sub < 4, low, mid), jnp.where(sub < 4, mid, high)], axis=0)
        us.append(jnp.where(u_rows, u, 0.0))
        mid = pltpu.roll(capacity_plane(j, capacity, face), 4, 0)
        caps.append(
            6.0
            + jnp.concatenate(
                [
                    jnp.where(sub < 4, pltpu.roll(low, 3, 0), mid),
                    jnp.where(sub < 4, mid, pltpu.roll(high, 5, 0)),
                ],
                axis=0,
            )
        )

    def around(fields, a):
        here = fields[a]
        total = fields[a - 1] + fields[a + 1]
        total = total + pltpu.roll(here, 1, 0) + pltpu.roll(here, rows - 1, 0)
        total = total + jnp.where(lane == 0, 0.0, pltpu.roll(here, 1, 1))
        return total + jnp.where(lane == LANES - 1, 0.0, pltpu.roll(here, LANES - 1, 1))

    def inside(a):
        if a < 2:
            return d_rows & upper_x
        if a >= 10:
            return d_rows & jnp.logical_not(upper_x)
        return d_rows

    theta = 0.5 * (UPPER_BOUND + LOWER_BOUND)
    half_width = 0.5 * (UPPER_BOUND - LOWER_BOUND)
    sig = theta / half_width
    weight_now = 1.0 / sig
    misfit, step, total = {}, {}, {}
    for a in range(RING):
        misfit[a] = heats[a] - 6.0 * us[a + 1] + around(us, a + 1)
        step[a] = jnp.where(inside(a), misfit[a] * (1.0 / theta), 0.0)
        total[a] = us[a + 1] + step[a]
    for sweep in range(1, SWEEPS):
        weight_next = 1.0 / (2.0 * sig - weight_now)
        new_misfit, new_step = {}, {}
        for a in range(sweep, RING - sweep):
            new_misfit[a] = misfit[a] - caps[a + 1] * step[a] + around(step, a)
            moved = (weight_next * weight_now) * step[a] + (
                2.0 * weight_next / half_width
            ) * new_misfit[a]
            new_step[a] = jnp.where(inside(a), moved, 0.0)
            total[a] = total[a] + new_step[a]
        misfit, step, weight_now = new_misfit, new_step, weight_next
    for x in range(BS):
        result = total[x + 2]
        out[x] = jnp.where(sub < 4, pltpu.roll(result[:BS], 4, 0), pltpu.roll(result[BS:], 4, 0))


def f32(*shape):
    return jax.ShapeDtypeStruct(shape, jnp.float32)


def call(kernel, out_shape, *args, scratch=(), in_specs=None, flops=0):
    moved = 4 * sum(a.size for a in args) + 4 * sum(o.size for o in jax.tree.leaves(out_shape))
    options = {} if in_specs is None else dict(in_specs=in_specs)
    return pl.pallas_call(
        kernel,
        out_shape=out_shape,
        scratch_shapes=scratch,
        compiler_params=pltpu.CompilerParams(vmem_limit_bytes=VMEM_BYTES),
        cost_estimate=pl.CostEstimate(flops=flops, bytes_accessed=moved, transcendentals=0),
        **options,
    )(*args)


def room(*shape):
    return pltpu.VMEM(shape, jnp.float32)


def paired(count, first):
    pairs = []
    for i in range(first, count - 1, 2):
        pairs += [(i, i + 1), (i + 1, i)]
    return pairs


def two_round_body(
    corner_speed_prior,
    brick_stress_tensor_now,
    compact_onset_strength,
    corner_weights_diagonal,
    substance_labels,
    brick_warmth_prior,
    caloric_capacity_per_timestep,
):
    rows = PLANE
    groups = lax.axis_size("gz")
    chain = groups * lax.axis_size("gy")
    labels = jnp.transpose(substance_labels, (0, 2, 1))
    raw = (
        labels,
        corner_speed_prior,
        brick_stress_tensor_now,
        compact_onset_strength,
        brick_warmth_prior,
        caloric_capacity_per_timestep,
    )
    raw = [pltpu.with_memory_space_constraint(array, pltpu.HBM) for array in raw]
    second = compact_onset_strength.shape[-1]
    wide, shear, face, columns, corner = call(
        pack_kernel,
        (
            f32(10 * BS * rows, LANES),
            f32(rows, LANES),
            f32(FACE_TILES + 4, BS, LANES),
            f32(BS, rows, LANES),
            f32(3, rows, LANES),
        ),
        *raw,
        in_specs=[pl.BlockSpec(memory_space=pltpu.HBM)] * len(raw),
        scratch=(
            room(10, BS, rows, second),
            pltpu.VMEM(labels.shape, jnp.int32),
            pltpu.SemaphoreType.DMA((len(raw),)),
        ),
    )
    face = lax.ppermute(face, "gx", [(0, 1), (1, 0)])
    columns = lax.ppermute(columns, "gy", [(0, 1), (1, 0)])
    corner = lax.ppermute(corner, ("gx", "gy"), [(0, 3), (3, 0), (1, 2), (2, 1)])
    chunks, even, odd, updated, partial = call(
        heat_kernel,
        (
            f32(groups, rows, 3 * LANES),
            f32(EDGE_ALL, LANES),
            f32(EDGE_ALL, LANES),
            f32(6, BS + 1, rows, LANES),
            f32(PLANES, rows, LANES),
        ),
        wide,
        shear,
        brick_warmth_prior,
        caloric_capacity_per_timestep,
        face,
        columns,
        corner,
        scratch=(room(VELS, rows, LANES), room(3 * LANES, LANES), room(10, 14, rows, LANES)),
    )
    chunks = lax.all_to_all(chunks, "gz", split_axis=0, concat_axis=0, tiled=True)
    even = lax.ppermute(even, ("gy", "gz"), paired(chain, 0))
    odd = lax.ppermute(odd, ("gy", "gz"), paired(chain, 1))
    corner_speed_later, projected_brick_stress_tensor = call(
        force_kernel,
        (f32(*corner_speed_prior.shape), f32(*brick_stress_tensor_now.shape)),
        updated,
        partial,
        even,
        odd,
        corner_speed_prior,
        corner_weights_diagonal,
        scratch=(room(6, rows, LANES), room(6, rows, LANES)),
    )
    diffused_kelvin_field = call(
        conduct_kernel,
        f32(*brick_warmth_prior.shape),
        chunks,
        brick_warmth_prior,
        caloric_capacity_per_timestep,
        face,
        even,
        odd,
    )
    return (corner_speed_later, projected_brick_stress_tensor, diffused_kelvin_field)


def solution(mesh):
    placed = (
        P(None, "gx", "gz", "gy"),
        P(None, "gx", "gz", "gy"),
        P("gx", "gz", "gy"),
        P("gx", "gz", "gy"),
        P("gx", None, "gy"),
        P("gx", ("gy", "gz"), None),
        P("gx", ("gy", "gz"), None),
    )
    return jax.shard_map(
        two_round_body if two_rounds_fit(mesh) else body,
        mesh=mesh,
        in_specs=placed,
        out_specs=(
            P(None, "gx", "gz", "gy"),
            P(None, "gx", "gz", "gy"),
            P("gx", ("gy", "gz"), None),
        ),
        check_vma=False,
    )
```

```python
import jax
import jax.numpy as jnp
from jax import lax
from jax.experimental import pallas as pl
from jax.experimental.pallas import tpu as pltpu
from jax.sharding import PartitionSpec as P

BS = 8
ZB = 2
SWEEPS = 3


TIME_STEP = 0.2
VISCOSITY = 0.4
FRICTION = 0.5
TAYLOR_QUINNEY = 0.9
HEAT_SCALE = 5.0
ELASTIC_YIELD = 10000.0
LOWER_BOUND = 0.5
UPPER_BOUND = 16.0


def extended(cells, sides, width):
    for axis, dim in sides:
        count = lax.axis_size(axis)
        ends = count - 1
        head = lax.slice_in_dim(cells, 0, width, axis=dim)
        tail = lax.slice_in_dim(cells, cells.shape[dim] - width, cells.shape[dim], axis=dim)
        cells = jnp.concatenate(
            [
                lax.ppermute(tail, axis, [(i, (i + 1) % count) for i in range(ends)]),
                cells,
                lax.ppermute(head, axis, [((i + 1) % count, i) for i in range(ends)]),
            ],
            axis=dim,
        )
    return cells


def shifted_diff(values, axis_num):
    extent = values.shape[axis_num]
    return lax.slice_in_dim(values, 1, extent, axis=axis_num) - lax.slice_in_dim(
        values, 0, extent - 1, axis=axis_num
    )


def shifted_sum(values, axis_num):
    extent = values.shape[axis_num]
    return lax.slice_in_dim(values, 1, extent, axis=axis_num) + lax.slice_in_dim(
        values, 0, extent - 1, axis=axis_num
    )


def spread_blocks(values, width):
    extent_a, extent_b, extent_c = values.shape
    wide = jnp.broadcast_to(
        values[:, None, :, None, :, None], (extent_a, width, extent_b, width, extent_c, width)
    )
    return wide.reshape(extent_a * width, extent_b * width, extent_c * width)


def moduli(substance_labels):
    shear_mod = jnp.where(
        substance_labels == 0, 3.0, jnp.where(substance_labels == 1, 2.0, 0.8)
    ).astype(jnp.float32)
    bulk_mod = jnp.where(
        substance_labels == 0, 5.0, jnp.where(substance_labels == 1, 4.0, 1.2)
    ).astype(jnp.float32)
    return (shear_mod, bulk_mod)


def face_term(element_values, axis_num):
    others = [other for other in (0, 1, 2) if other != axis_num]
    return shifted_diff(shifted_sum(shifted_sum(element_values, others[0]), others[1]), axis_num)


def element_state(node_vel, props):
    grad_x = 0.25 * shifted_diff(shifted_sum(shifted_sum(node_vel, 2), 3), 1)
    grad_y = 0.25 * shifted_diff(shifted_sum(shifted_sum(node_vel, 1), 3), 2)
    grad_z = 0.25 * shifted_diff(shifted_sum(shifted_sum(node_vel, 1), 2), 3)
    yield_eff = props[6]
    shear_mod = props[7]
    bulk_mod = props[8]
    strain_xx = TIME_STEP * grad_x[0]
    strain_yy = TIME_STEP * grad_y[1]
    strain_zz = TIME_STEP * grad_z[2]
    strain_xy = TIME_STEP * (0.5 * (grad_y[0] + grad_x[1]))
    strain_yz = TIME_STEP * (0.5 * (grad_z[1] + grad_y[2]))
    strain_xz = TIME_STEP * (0.5 * (grad_z[0] + grad_x[2]))
    volume = strain_xx + strain_yy + strain_zz
    vol_third = volume / 3.0
    trial_xx = props[0] + 2.0 * shear_mod * (strain_xx - vol_third) + bulk_mod * volume
    trial_yy = props[1] + 2.0 * shear_mod * (strain_yy - vol_third) + bulk_mod * volume
    trial_zz = props[2] + 2.0 * shear_mod * (strain_zz - vol_third) + bulk_mod * volume
    trial_xy = props[3] + 2.0 * shear_mod * strain_xy
    trial_yz = props[4] + 2.0 * shear_mod * strain_yz
    trial_xz = props[5] + 2.0 * shear_mod * strain_xz
    pressure = (trial_xx + trial_yy + trial_zz) / 3.0
    dev_xx = trial_xx - pressure
    dev_yy = trial_yy - pressure
    dev_zz = trial_zz - pressure
    second = (
        dev_xx * dev_xx
        + dev_yy * dev_yy
        + dev_zz * dev_zz
        + 2.0 * (trial_xy * trial_xy + trial_yz * trial_yz + trial_xz * trial_xz)
    )
    equivalent = jnp.sqrt(1.5 * second)
    flow_stress = yield_eff + FRICTION * jnp.maximum(-pressure, 0.0)
    excess = equivalent - flow_stress
    active = excess > 0.0
    plastic_rate = jnp.maximum(excess, 0.0) / (3.0 * shear_mod + VISCOSITY / TIME_STEP)
    scale_back = jnp.where(
        active, 1.0 - 3.0 * shear_mod * plastic_rate / jnp.where(active, equivalent, 1.0), 1.0
    )
    updated = jnp.stack(
        [
            pressure + scale_back * dev_xx,
            pressure + scale_back * dev_yy,
            pressure + scale_back * dev_zz,
            scale_back * trial_xy,
            scale_back * trial_yz,
            scale_back * trial_xz,
        ]
    )
    heat_local = (
        HEAT_SCALE * TAYLOR_QUINNEY * (equivalent - 3.0 * shear_mod * plastic_rate) * plastic_rate
    )
    return (updated, heat_local)


def node_forces(updated):
    force_x = face_term(updated[0], 0) + face_term(updated[3], 1) + face_term(updated[5], 2)
    force_y = face_term(updated[3], 0) + face_term(updated[1], 1) + face_term(updated[4], 2)
    force_z = face_term(updated[5], 0) + face_term(updated[4], 1) + face_term(updated[2], 2)
    return -0.25 * jnp.stack([force_x, force_y, force_z])


def mechanics(padded, corner_weights_diagonal):
    node_vel = padded[0:3]
    updated, heat_local = element_state(node_vel, padded[3:, :-1, :-1, :-1])
    force = node_forces(updated)
    corner_speed_later = node_vel[:, 1:-1, 1:-1, 1:-1] - TIME_STEP * force / corner_weights_diagonal
    return (corner_speed_later, updated[:, 1:, 1:, 1:], heat_local[1:, 1:, 1:])


def stencil(values, padded, matrix_main_entries):
    beside = padded[2:, 1:-1, 1:-1] + padded[:-2, 1:-1, 1:-1]
    beside = beside + padded[1:-1, 2:, 1:-1] + padded[1:-1, :-2, 1:-1]
    beside = beside + padded[1:-1, 1:-1, 2:] + padded[1:-1, 1:-1, :-2]
    return matrix_main_entries * values - beside


def diffuse_thermal_once(values, matrix_main_entries):
    haloed = extended(values, (("gx", 0), (("gy", "gz"), 1)), 1)
    padded = jnp.pad(haloed, ((0, 0), (0, 0), (1, 1)))
    return stencil(values, padded, matrix_main_entries)


def polynomial_relaxation(
    brick_warmth_prior,
    caloric_capacity_per_timestep,
    plastic_work_heating_rise,
    diffuse_thermal_field,
    inward_cell_flags,
):
    center_value = 0.5 * (UPPER_BOUND + LOWER_BOUND)
    half_width = 0.5 * (UPPER_BOUND - LOWER_BOUND)
    ratio_sig = center_value / half_width
    matrix_main_entries = 6.0 + caloric_capacity_per_timestep
    linear_system_target = (
        caloric_capacity_per_timestep * brick_warmth_prior + plastic_work_heating_rise
    )
    implicit_kelvin_result = brick_warmth_prior
    equation_misfit = (
        linear_system_target - diffuse_thermal_field(implicit_kelvin_result, matrix_main_entries)
    ) * inward_cell_flags
    weight_now = 1.0 / ratio_sig
    search_direction = equation_misfit / center_value
    for sweep_index in range(SWEEPS):
        implicit_kelvin_result = implicit_kelvin_result + search_direction
        if sweep_index + 1 < SWEEPS:
            equation_misfit = (
                equation_misfit - diffuse_thermal_field(search_direction, matrix_main_entries)
            ) * inward_cell_flags
            weight_next = 1.0 / (2.0 * ratio_sig - weight_now)
            search_direction = (
                weight_next * weight_now * search_direction
                + 2.0 * weight_next / half_width * equation_misfit
            )
            weight_now = weight_next
    return implicit_kelvin_result


def body(
    corner_speed_prior,
    brick_stress_tensor_now,
    compact_onset_strength,
    corner_weights_diagonal,
    substance_labels,
    brick_warmth_prior,
    caloric_capacity_per_timestep,
):
    z_index = lax.axis_index("gz")
    local_mat = lax.dynamic_slice_in_dim(substance_labels, z_index * ZB, ZB, 1)
    shear_blk, bulk_blk = moduli(local_mat)
    powder_cells = spread_blocks(local_mat, BS) == 2
    yield_eff = jnp.where(powder_cells, compact_onset_strength, ELASTIC_YIELD)
    stacked = jnp.concatenate(
        [
            corner_speed_prior,
            brick_stress_tensor_now,
            yield_eff[None],
            spread_blocks(shear_blk, BS)[None],
            spread_blocks(bulk_blk, BS)[None],
        ],
        axis=0,
    )
    padded = extended(stacked, (("gx", 1), ("gy", 3), ("gz", 2)), 1)
    corner_speed_later, projected_brick_stress_tensor, heat_local = mechanics(
        padded, corner_weights_diagonal
    )
    moved = lax.all_to_all(heat_local, "gz", split_axis=2, concat_axis=1, tiled=True)
    plastic_work_heating_rise = jnp.transpose(moved, (0, 2, 1))
    diffused_kelvin_field = polynomial_relaxation(
        brick_warmth_prior,
        caloric_capacity_per_timestep,
        plastic_work_heating_rise,
        diffuse_thermal_once,
        1.0,
    )
    return (corner_speed_later, projected_brick_stress_tensor, diffused_kelvin_field)


LANES = 128
VELS = 3
FIELDS = 11
SLOT = 4
RING = 12
PLANES = 14
MAIN = RING * 2 * BS
VMEM_BYTES = 48 * 1024 * 1024


def two_rounds_fit(mesh):
    return mesh.shape["gx"] == 2 and mesh.shape["gy"] == 2 and mesh.shape["gz"] == 8


def iota(shape, dim):
    return lax.broadcasted_iota(jnp.int32, shape, dim)


def place(q):
    return MAIN + RING * q if q < 5 else 2 * LANES + RING * (q - 5)


def bulk_of(shear_mod):
    return jnp.where(
        shear_mod == 3.0,
        5.0,
        jnp.where(shear_mod == 2.0, 4.0, jnp.where(shear_mod == 0.0, 0.0, 1.2)),
    )


def own_labels(labels):
    second, press = labels.shape
    rows = ZB * BS
    first = lax.axis_index("gz") * ZB
    pick = iota((rows, press), 1) == first + iota((rows, press), 0) // BS
    spread = iota((second, LANES), 0) == (iota((second, LANES), 1) // BS) % second
    picked = lax.dot_general(
        pick.astype(jnp.float32),
        labels.astype(jnp.float32),
        (((1,), (1,)), ((), ())),
        preferred_element_type=jnp.float32,
    )
    return jnp.dot(picked, spread.astype(jnp.float32), preferred_element_type=jnp.float32)


FACE = (
    [(field, i) for field in range(VELS) for i in range(3)]
    + [(field, i) for field in range(VELS, 10) for i in range(2)]
    + [(10, 0)]
)
FACE_TILES = len(FACE) // 2 * ZB
PLANE = ZB * BS


def slot_at(lane, field, first):
    where = lax.rem(lane + (2 * LANES - SLOT * field) - first, LANES)
    return where < 3


def pack_kernel(
    labels, vel, stress, onset, warmth, capacity,
    wide, shear_out, face, columns, corner, warmth_out, capacity_out,
    own, own_labels_in, sems,
):
    lower_x = lax.axis_index("gx") == 0
    lower_y = lax.axis_index("gy") == 0
    deep = jnp.where(lower_x, BS - 3, 0)
    shallow = jnp.where(lower_x, BS - 2, 0)
    edge = jnp.where(lower_x, BS - 1, 0)
    copies = [
        pltpu.make_async_copy(*pair, sems.at[n])
        for n, pair in enumerate(
            (
                (labels, own_labels_in),
                (vel, own.at[pl.ds(0, VELS)]),
                (onset, own.at[9]),
                (stress, own.at[pl.ds(VELS, 6)]),
                (warmth.at[pl.ds(deep, 3)], face.at[pl.ds(FACE_TILES, 3)]),
                (capacity.at[edge], face.at[FACE_TILES + 3]),
                (warmth, warmth_out),
                (capacity, capacity_out),
            )
        )
    ]
    for copy in copies:
        copy.start()
    lane = iota((PLANE, LANES), 1)
    half = LANES // 2
    copies[0].wait()
    material = own_labels(own_labels_in[0])
    shear_mod = jnp.where(material == 0.0, 3.0, jnp.where(material == 1.0, 2.0, 0.8))
    shear_out[...] = shear_mod
    copies[1].wait()
    copies[2].wait()
    for field in range(VELS):
        wide[pl.ds(field * BS * PLANE, BS * PLANE), 0:half] = own[field].reshape(BS * PLANE, half)
    powder = material[:, 0:half] == 2.0
    for x in range(BS):
        at = pl.ds((9 * BS + x) * PLANE, PLANE)
        wide[at, 0:half] = jnp.where(powder, own[9, x], ELASTIC_YIELD)
    copies[3].wait()
    for field in range(VELS, 9):
        wide[pl.ds(field * BS * PLANE, BS * PLANE), 0:half] = own[field].reshape(BS * PLANE, half)

    def read(field, x):
        if field == 10:
            return shear_mod
        return wide[pl.ds(pl.multiple_of((field * BS + x) * PLANE, PLANE), PLANE), :]

    for pair in range(len(FACE) // 2):
        one, two = (
            read(field, (deep if field < VELS else shallow) + i)
            for field, i in FACE[2 * pair : 2 * pair + 2]
        )
        joined = jnp.where(lane < half, one, pltpu.roll(two, half, 1))
        face[2 * pair] = joined[:BS]
        face[2 * pair + 1] = joined[BS:]
    first = jnp.where(lower_y, half - 3, 0)
    insides = [slot_at(lane, field, first) for field in range(FIELDS)]
    for x in range(BS):
        packed = jnp.zeros((PLANE, LANES), jnp.float32)
        for field in range(FIELDS):
            turned = read(field, x)
            if field:
                turned = pltpu.roll(turned, SLOT * field, 1)
            packed = jnp.where(insides[field], turned, packed)
        columns[x] = packed
    for i in range(3):
        corner[i] = columns[deep + i]
    for copy in copies[4:]:
        copy.wait()


def warmth_plane(j, warmth, face):
    upper_x = lax.axis_index("gx") == 1
    if j < 3:
        return jnp.where(upper_x, face[FACE_TILES + j], 0.0)
    if j < 11:
        return warmth[j - 3]
    return jnp.where(upper_x, 0.0, face[FACE_TILES + j - 11])


def capacity_plane(j, capacity, face):
    upper_x = lax.axis_index("gx") == 1
    if 3 <= j < 11:
        return capacity[j - 3]
    if j == 2 or j == 11:
        return jnp.where(upper_x == (j == 2), face[FACE_TILES + 3], 0.0)
    return jnp.zeros((BS, LANES), jnp.float32)


def stress_terms(shear_mod):
    bulk_mod = bulk_of(shear_mod)
    return (
        0.5 * TIME_STEP * shear_mod,
        0.25 * TIME_STEP * (bulk_mod - 2.0 / 3.0 * shear_mod),
        3.0 * shear_mod,
        1.0 / (3.0 * shear_mod + VISCOSITY / TIME_STEP),
    )


def strained(before, grads, terms):
    twice, volume_term = terms[0], terms[1]
    volume = volume_term * (grads[0] + grads[1] + grads[2])
    return [
        before[k] + twice * grads[k] + (volume if k < 3 else 0.0) for k in range(6)
    ]


def returned(trial, yield_eff, terms):
    shear_thrice, slope = terms[2], terms[3]
    pressure = (trial[0] + trial[1] + trial[2]) * (1.0 / 3.0)
    dev = [trial[k] - pressure for k in range(3)]
    second = (
        dev[0] * dev[0]
        + dev[1] * dev[1]
        + dev[2] * dev[2]
        + 2.0 * (trial[3] * trial[3] + trial[4] * trial[4] + trial[5] * trial[5])
    )
    equivalent = jnp.sqrt(1.5 * second)
    excess = equivalent - (yield_eff + FRICTION * jnp.maximum(-pressure, 0.0))
    active = excess > 0.0
    rate = jnp.maximum(excess, 0.0) * slope
    drop = shear_thrice * rate
    scale = jnp.where(active, 1.0 - drop / jnp.where(active, equivalent, 1.0), 1.0)
    heat = HEAT_SCALE * TAYLOR_QUINNEY * (equivalent - drop) * rate
    updated = [pressure + scale * dev[k] for k in range(3)] + [
        scale * trial[k] for k in range(3, 6)
    ]
    return updated, heat


def six(gx, gp, gs):
    return [
        gx[0],
        gp[1],
        gs[2],
        0.5 * (gp[0] + gx[1]),
        0.5 * (gs[1] + gp[2]),
        0.5 * (gs[0] + gx[2]),
    ]


LAYERS = 14


def heat_kernel(
    wide, shear, warmth, capacity, face, columns, corner,
    chunks_out, even_out, odd_out, updated_out, partial_out,
    ext, stacked, chunks, sem,
):
    upper_x = lax.axis_index("gx") == 1
    upper_y = lax.axis_index("gy") == 1
    even = lax.rem(lax.axis_index("gz"), 2) == 0
    rows = PLANE
    half = LANES // 2
    lane = iota((rows, LANES), 1)
    first = jnp.where(upper_y, LANES - 3, half)
    beside = (lane >= first) & (lane < first + 3)
    faces = {key: at for at, key in enumerate(FACE)}

    def joined(field, plane, side):
        side = pltpu.roll(side, (half - SLOT * field) % LANES, 1)
        return jnp.where(lane < half, plane, jnp.where(beside, side, 0.0))

    def far(field, i, side):
        at = faces[field, i]
        pair = at // 2
        plane = jnp.concatenate([face[2 * pair], face[2 * pair + 1]], axis=0)
        return joined(field, pltpu.roll(plane, half, 1) if at % 2 else plane, side)

    def layer(field, j):
        if 3 <= j < 11:
            at = (field * BS + j - 3) * rows
            return joined(field, wide[pl.ds(at, rows), :], columns[j - 3])
        side = corner[j] if j < 3 else corner[j - 11]
        i = j - 11 if j >= 11 else j if field < VELS else j - 1
        plane = far(field, i, side)
        return jnp.where(upper_x, plane, 0.0) if j < 3 else jnp.where(upper_x, 0.0, plane)

    for field in range(10):
        for j in range(1, LAYERS if field < VELS else LAYERS - 1):
            ext[pl.ds((field * LAYERS + j) * rows, rows), :] = layer(field, j)
    outer = far(10, 0, corner[1])
    shears = [
        jnp.where(upper_x, outer, 0.0),
        joined(10, shear[...], columns[0]),
        jnp.where(upper_x, 0.0, outer),
    ]

    row = iota((rows, LANES), 0)

    def across(field, press):
        at = (field * LAYERS + 1) * rows + press
        return ext[pl.ds(at, rows, stride=rows), :]

    def parts(press, sign):
        terms = []
        for c in range(VELS):
            here = across(c, press)
            aside = pltpu.roll(here, LANES - 1, 1)
            total, change = here + aside, aside - here
            nxt = pltpu.roll(total, rows - 1, 0)
            both = nxt + total
            terms.append((nxt - total, sign * both, change + pltpu.roll(change, rows - 1, 0)))
        return six(*[[terms[c][d] for c in range(VELS)] for d in range(3)])

    last = rows - 1
    shear_row = [shears[block][last:, :] for block in range(3)]
    shear_mod = jnp.where(row < 2, shear_row[0], jnp.where(row < 10, shear_row[1], shear_row[2]))
    trial = strained(
        [across(VELS + k, last) for k in range(6)], parts(last, -1.0), stress_terms(shear_mod)
    )
    for q, plane in enumerate(trial + [across(9, last), shear_mod]):
        partial_out[q] = plane
    for k, plane in enumerate(parts(0, 1.0)):
        partial_out[8 + k] = plane

    sub = iota((BS, LANES), 0)
    stacked[pl.ds(MAIN, 64), :] = jnp.zeros((64, LANES), jnp.float32)
    stacked[pl.ds(2 * LANES + 96, 32), :] = jnp.zeros((32, LANES), jnp.float32)
    for q in range(PLANES):
        stacked[pl.ds(place(q), RING), :] = partial_out[q, pl.ds(0, RING), :]

    def read(field, j):
        return ext[pl.ds((field * LAYERS + j) * rows, rows), :]

    def node_terms(j):
        terms = []
        for c in range(VELS):
            here = read(c, j)
            above = jnp.where(row == rows - 1, 0.0, pltpu.roll(here, rows - 1, 0))
            total, change = here + above, above - here
            aside = pltpu.roll(total, LANES - 1, 1)
            terms.append((total + aside, aside - total, change + pltpu.roll(change, LANES - 1, 1)))
        return terms

    materials = [stress_terms(plane) for plane in shears]
    before = node_terms(1)
    for a in range(RING):
        after = node_terms(a + 2)
        grads = six(
            [after[c][0] - before[c][0] for c in range(VELS)],
            [after[c][2] + before[c][2] for c in range(VELS)],
            [after[c][1] + before[c][1] for c in range(VELS)],
        )
        material = materials[0 if a < 2 else 1 if a < 10 else 2]
        trial = strained([read(VELS + k, a + 1) for k in range(6)], grads, material)
        updated, heat = returned(trial, read(9, a + 1), material)
        stacked[pl.ds(a * rows, rows), :] = heat
        if 1 <= a < 10:
            for k in range(6):
                updated_out[k, a - 1] = updated[k]
        before = after
    turned = jnp.transpose(stacked[...])
    for g in range(chunks.shape[0]):
        here, after, before = (
            turned[at % LANES : at % LANES + BS, :] for at in (g * BS, g * BS + BS, g * BS - BS)
        )
        for t in range(3):
            chunks[g, pl.ds(t * BS, BS), :] = here[:, t * LANES : (t + 1) * LANES]
        sides = [
            jnp.where(
                sub < 4,
                after[:, t * LANES : (t + 1) * LANES],
                before[:, t * LANES : (t + 1) * LANES],
            )
            for t in range(3)
        ]
        inner = jnp.where(sub < 4, pltpu.roll(sides[1], 2, 0), pltpu.roll(sides[1], 6, 0))
        chunks[g, pl.ds(3 * BS, BS), :] = jnp.where((sub < 2) | (sub > 5), sides[0], inner)
        chunks[g, pl.ds(4 * BS, BS), :] = sides[2]
    copy = pltpu.make_async_copy(chunks, chunks_out, sem)
    copy.start()

    ups, downs = [], []
    for j in range(14):
        u = warmth_plane(j, warmth, face)
        c = capacity_plane(j, capacity, face)
        ups.append(jnp.where(sub > 4, u, pltpu.roll(c, 5, 0)))
        downs.append(jnp.where(sub < 3, u, pltpu.roll(c, 3, 0)))

    def fill(up_ref, down_ref):
        for q in range(8):
            up_ref[pl.ds(RING * q, RING), :] = partial_out[q, pl.ds(0, RING), :]
        for k in range(6):
            down_ref[pl.ds(RING * k, RING), :] = partial_out[8 + k, pl.ds(0, RING), :]
        down_ref[pl.ds(6 * RING, 2 * RING), :] = jnp.zeros((2 * RING, LANES), jnp.float32)
        for m in range(7):
            at = pl.ds(EDGE_ROWS + m * BS, BS)
            up_ref[at, :] = jnp.where(sub < 4, pltpu.roll(ups[2 * m], 4, 0), ups[2 * m + 1])
            down_ref[at, :] = jnp.where(sub < 4, downs[2 * m], pltpu.roll(downs[2 * m + 1], 4, 0))

    @pl.when(even)
    def _():
        fill(even_out, odd_out)

    @pl.when(jnp.logical_not(even))
    def _():
        fill(odd_out, even_out)

    copy.wait()


EDGE_ROWS = 8 * RING
EDGE_ALL = EDGE_ROWS + 7 * BS


def corrected(planes, sign):
    rows = PLANE
    total, change, press = [], [], []
    for plane in planes:
        aside = pltpu.roll(plane, 1, 1)
        total.append(plane + aside)
        change.append(plane - aside)
        press.append(sign * (plane + aside))
    forces = []
    for kx, kp, ks in FORCE_TERMS:
        both = press[kp] + change[ks]
        forces.append(
            total[kx] - pltpu.roll(total[kx], 1, 0) + both + pltpu.roll(both, 1, 0)
        )
    return forces


FORCE_TERMS = ((0, 3, 5), (3, 1, 4), (5, 4, 2))


def gather_kernel(chunks, updated, vel, mass, heats_out, base_out):
    groups = lax.axis_size("gz")
    rows = PLANE
    lane = iota((rows, LANES), 1)
    row = iota((rows, LANES), 0)
    group = lane // rows
    sub = iota((BS, LANES), 0)

    sources = [[], [], []]
    for g in range(groups):
        sides = chunks[g, pl.ds(3 * BS, BS), :]
        inner = jnp.where(sub < 4, pltpu.roll(sides, 6, 0), pltpu.roll(sides, 2, 0))
        for t, side in enumerate((sides, inner, chunks[g, pl.ds(4 * BS, BS), :])):
            sources[t].append(jnp.concatenate([chunks[g, pl.ds(t * BS, BS), :], side], axis=0))

    heats = []
    for t, count in ((0, 8), (1, 4)):
        turned = []
        for k in range(groups):
            mixed = sources[t][k]
            for b in range(1, count):
                mixed = jnp.where(group == b, sources[t][(b + k) % groups], mixed)
            turned.append(pltpu.roll(mixed, k * rows, 1) if k else mixed)
        for b in range(count):
            heat = turned[(0 - b) % groups]
            for g in range(1, groups):
                heat = jnp.where(group == g, turned[(g - b) % groups], heat)
            heats.append(heat)

    planes = []
    for q in range(PLANES):
        tile, at = divmod(place(q), LANES)
        plane = jnp.zeros((rows, LANES), jnp.float32)
        for g in range(groups):
            to = g if q < 8 else g - 1
            if to < 0:
                continue
            inside = (lane >= to * rows) & (lane < to * rows + RING)
            turn = (to * rows - at) % LANES
            plane = jnp.where(inside, pltpu.roll(sources[tile][g], turn, 1), plane)
        planes.append(plane)
    terms = stress_terms(planes[7])
    seam = returned(strained(planes[:6], planes[8:], terms), planes[6], terms)[1]
    for a in range(RING):
        heats_out[a] = jnp.where(
            lane % rows == rows - 1, pltpu.roll(seam, rows - 1 - a, 1), heats[a]
        )

    def element_terms(j):
        terms = []
        for k in range(6):
            here = jnp.where(row == rows - 1, 0.0, updated[k, j])
            prev = pltpu.roll(here, 1, 0)
            total, change = here + prev, here - prev
            aside = pltpu.roll(total, 1, 1)
            terms.append((total + aside, total - aside, change + pltpu.roll(change, 1, 1)))
        return terms

    before = element_terms(0)
    for x in range(BS):
        after = element_terms(x + 1)
        weights = 0.25 * TIME_STEP / mass[x]
        for c, (kx, kp, ks) in enumerate(FORCE_TERMS):
            force = (
                (after[kx][0] - before[kx][0])
                + (after[kp][2] + before[kp][2])
                + (after[ks][1] + before[ks][1])
            )
            base_out[c, x] = vel[c, x] + force[:, : LANES // 2] * weights
        before = after


def finish_kernel(
    heats, base, updated, partial, mass, warmth, capacity, face, even_in, odd_in,
    vel_hbm, stress_hbm, out_hbm,
    vel_out, stress_out, out, top, low_force, high_force, sems,
):
    upper_x = lax.axis_index("gx") == 1
    at_z = lax.axis_index("gz")
    even = lax.rem(at_z, 2) == 0
    groups = lax.axis_size("gz")
    rows = PLANE
    half = LANES // 2
    at_flat = lax.axis_index("gy") * groups + at_z
    last = lax.axis_size("gy") * groups - 1
    has_above = at_z < groups - 1
    has_below = at_z > 0
    lane = iota((rows, LANES), 1)
    row = iota((rows, LANES), 0)
    sub = iota((BS, LANES), 0)

    def below_plane(q):
        at = pl.ds(RING * q, rows)
        return jnp.where(has_below, jnp.where(even, odd_in[at, :], even_in[at, :]), 0.0)

    def above_plane(k):
        at = pl.ds(RING * k, rows)
        return jnp.where(has_above, jnp.where(even, even_in[at, :], odd_in[at, :]), 0.0)

    terms = stress_terms(partial[7])
    trial = strained([partial[k] for k in range(6)], [above_plane(k) for k in range(6)], terms)
    uppermost = returned(trial, partial[6], terms)[0]
    for k, plane in enumerate(uppermost):
        top[k] = plane
    for c, plane in enumerate(corrected(uppermost, 1.0)):
        high_force[c] = plane
    terms = stress_terms(below_plane(7))
    trial = strained([below_plane(k) for k in range(6)], [partial[8 + k] for k in range(6)], terms)
    for c, plane in enumerate(corrected(returned(trial, below_plane(6), terms)[0], -1.0)):
        low_force[c] = plane
    for x in range(BS):
        at = pl.ds(x + 2, 1)
        weights = 0.25 * TIME_STEP / mass[x]
        for k in range(6):
            plane = jnp.where(row == rows - 1, top[k, at, :], updated[k, x + 1])
            stress_out[k, x] = plane[:, :half]
        for c in range(VELS):
            force = jnp.where(
                row == 0, low_force[c, at, :], jnp.where(row == rows - 1, high_force[c, at, :], 0.0)
            )
            vel_out[c, x] = base[c, x] + force[:, :half] * weights
    copies = [
        pltpu.make_async_copy(*pair, sems.at[n])
        for n, pair in enumerate(((vel_out, vel_hbm), (stress_out, stress_hbm), (out, out_hbm)))
    ]
    copies[0].start()
    copies[1].start()

    above, below = at_flat < last, at_flat > 0
    u_rows = (row < BS) | ((row < BS + 3) & above) | ((row >= rows - 3) & below)
    d_rows = (row < BS) | ((row < BS + 2) & above) | ((row >= rows - 2) & below)
    us, caps = [], []
    for j in range(14):
        at = pl.ds(EDGE_ROWS + j // 2 * BS, BS)
        low = jnp.where(even, odd_in[at, :], even_in[at, :])
        high = jnp.where(even, even_in[at, :], odd_in[at, :])
        if j % 2:
            high = pltpu.roll(high, 4, 0)
        else:
            low = pltpu.roll(low, 4, 0)
        side = jnp.where(sub < 4, high, low)
        u = jnp.concatenate([warmth_plane(j, warmth, face), side], axis=0)
        us.append(jnp.where(u_rows, u, 0.0))
        side = jnp.where(sub < 4, pltpu.roll(high, 5, 0), pltpu.roll(low, 3, 0))
        caps.append(6.0 + jnp.concatenate([capacity_plane(j, capacity, face), side], axis=0))

    def around(fields, a):
        here = fields[a]
        total = fields[a - 1] + fields[a + 1]
        total = total + pltpu.roll(here, 1, 0) + pltpu.roll(here, rows - 1, 0)
        total = total + jnp.where(lane == 0, 0.0, pltpu.roll(here, 1, 1))
        return total + jnp.where(lane == LANES - 1, 0.0, pltpu.roll(here, LANES - 1, 1))

    def inside(a):
        if a < 2:
            return d_rows & upper_x
        if a >= 10:
            return d_rows & jnp.logical_not(upper_x)
        return d_rows

    theta = 0.5 * (UPPER_BOUND + LOWER_BOUND)
    half_width = 0.5 * (UPPER_BOUND - LOWER_BOUND)
    sig = theta / half_width
    weight_now = 1.0 / sig
    misfit, step, total = {}, {}, {}
    for a in range(RING):
        misfit[a] = heats[a] - 6.0 * us[a + 1] + around(us, a + 1)
        step[a] = jnp.where(inside(a), misfit[a] * (1.0 / theta), 0.0)
        total[a] = us[a + 1] + step[a]
    for sweep in range(1, SWEEPS):
        weight_next = 1.0 / (2.0 * sig - weight_now)
        new_misfit, new_step = {}, {}
        for a in range(sweep, RING - sweep):
            new_misfit[a] = misfit[a] - caps[a + 1] * step[a] + around(step, a)
            moved = (weight_next * weight_now) * step[a] + (
                2.0 * weight_next / half_width
            ) * new_misfit[a]
            new_step[a] = jnp.where(inside(a), moved, 0.0)
            total[a] = total[a] + new_step[a]
        misfit, step, weight_now = new_misfit, new_step, weight_next
    for x in range(BS):
        out[x] = total[x + 2][:BS]
    copies[2].start()
    for copy in copies:
        copy.wait()


def f32(*shape):
    return jax.ShapeDtypeStruct(shape, jnp.float32)


def call(kernel, out_shape, *args, scratch=(), far_in=False, far_out=0):
    moved = 4 * sum(a.size for a in args) + 4 * sum(o.size for o in jax.tree.leaves(out_shape))
    hbm, vmem = (pl.BlockSpec(memory_space=space) for space in (pltpu.HBM, pltpu.VMEM))
    return pl.pallas_call(
        kernel,
        out_shape=out_shape,
        in_specs=[hbm if far_in else vmem] * len(args),
        out_specs=tuple(hbm if n < far_out else vmem for n in range(len(out_shape))),
        scratch_shapes=scratch,
        compiler_params=pltpu.CompilerParams(vmem_limit_bytes=VMEM_BYTES),
        cost_estimate=pl.CostEstimate(flops=0, bytes_accessed=moved, transcendentals=0),
    )(*args)


def room(*shape):
    return pltpu.VMEM(shape, jnp.float32)


def paired(count, first):
    pairs = []
    for i in range(first, count - 1, 2):
        pairs += [(i, i + 1), (i + 1, i)]
    return pairs


def two_round_body(
    corner_speed_prior,
    brick_stress_tensor_now,
    compact_onset_strength,
    corner_weights_diagonal,
    substance_labels,
    brick_warmth_prior,
    caloric_capacity_per_timestep,
):
    rows = PLANE
    groups = lax.axis_size("gz")
    chain = groups * lax.axis_size("gy")
    labels = jnp.transpose(substance_labels, (0, 2, 1))
    raw = (
        labels,
        corner_speed_prior,
        brick_stress_tensor_now,
        compact_onset_strength,
        brick_warmth_prior,
        caloric_capacity_per_timestep,
    )
    raw = [pltpu.with_memory_space_constraint(array, pltpu.HBM) for array in raw]
    second = compact_onset_strength.shape[-1]
    wide, shear, face, columns, corner, warmth, capacity = call(
        pack_kernel,
        (
            f32(10 * BS * rows, LANES),
            f32(rows, LANES),
            f32(FACE_TILES + 4, BS, LANES),
            f32(BS, rows, LANES),
            f32(3, rows, LANES),
            f32(*brick_warmth_prior.shape),
            f32(*brick_warmth_prior.shape),
        ),
        *raw,
        far_in=True,
        scratch=(
            room(10, BS, rows, second),
            pltpu.VMEM(labels.shape, jnp.int32),
            pltpu.SemaphoreType.DMA((len(raw) + 2,)),
        ),
    )
    face = lax.ppermute(face, "gx", [(0, 1), (1, 0)])
    columns = lax.ppermute(columns, "gy", [(0, 1), (1, 0)])
    corner = lax.ppermute(corner, ("gx", "gy"), [(0, 3), (3, 0), (1, 2), (2, 1)])
    chunks, even, odd, updated, partial = call(
        heat_kernel,
        (
            f32(groups, 5 * BS, LANES),
            f32(EDGE_ALL, LANES),
            f32(EDGE_ALL, LANES),
            f32(6, BS + 1, rows, LANES),
            f32(PLANES, rows, LANES),
        ),
        wide,
        shear,
        warmth,
        capacity,
        face,
        columns,
        corner,
        scratch=(
            room((10 * LAYERS + 3) * rows, LANES),
            room(3 * LANES, LANES),
            room(groups, 5 * BS, LANES),
            pltpu.SemaphoreType.DMA,
        ),
        far_out=1,
    )
    chunks = lax.all_to_all(chunks, "gz", split_axis=0, concat_axis=0, tiled=True)
    even = lax.ppermute(even, ("gy", "gz"), paired(chain, 0))
    odd = lax.ppermute(odd, ("gy", "gz"), paired(chain, 1))
    heats, base = call(
        gather_kernel,
        (f32(RING, rows, LANES), f32(*corner_speed_prior.shape)),
        chunks,
        updated,
        corner_speed_prior,
        corner_weights_diagonal,
    )
    heats, base, even, odd = lax.optimization_barrier((heats, base, even, odd))
    results = (corner_speed_prior.shape, brick_stress_tensor_now.shape, brick_warmth_prior.shape)
    return call(
        finish_kernel,
        tuple(f32(*shape) for shape in results),
        heats,
        base,
        updated,
        partial,
        corner_weights_diagonal,
        warmth,
        capacity,
        face,
        even,
        odd,
        scratch=(
            *[room(*shape) for shape in results],
            room(6, rows, LANES),
            room(VELS, rows, LANES),
            room(VELS, rows, LANES),
            pltpu.SemaphoreType.DMA((3,)),
        ),
        far_out=3,
    )


def solution(mesh):
    placed = (
        P(None, "gx", "gz", "gy"),
        P(None, "gx", "gz", "gy"),
        P("gx", "gz", "gy"),
        P("gx", "gz", "gy"),
        P("gx", None, "gy"),
        P("gx", ("gy", "gz"), None),
        P("gx", ("gy", "gz"), None),
    )
    return jax.shard_map(
        two_round_body if two_rounds_fit(mesh) else body,
        mesh=mesh,
        in_specs=placed,
        out_specs=(
            P(None, "gx", "gz", "gy"),
            P(None, "gx", "gz", "gy"),
            P("gx", ("gy", "gz"), None),
        ),
        check_vma=False,
    )
```

```python
import jax
import jax.numpy as jnp
from jax import lax
from jax.experimental import pallas as pl
from jax.experimental.pallas import tpu as pltpu
from jax.sharding import PartitionSpec as P

BS = 8
ZB = 2
SWEEPS = 3


TIME_STEP = 0.2
VISCOSITY = 0.4
FRICTION = 0.5
TAYLOR_QUINNEY = 0.9
HEAT_SCALE = 5.0
ELASTIC_YIELD = 10000.0
LOWER_BOUND = 0.5
UPPER_BOUND = 16.0


def extended(cells, sides, width):
    for axis, dim in sides:
        count = lax.axis_size(axis)
        ends = count - 1
        head = lax.slice_in_dim(cells, 0, width, axis=dim)
        tail = lax.slice_in_dim(cells, cells.shape[dim] - width, cells.shape[dim], axis=dim)
        cells = jnp.concatenate(
            [
                lax.ppermute(tail, axis, [(i, (i + 1) % count) for i in range(ends)]),
                cells,
                lax.ppermute(head, axis, [((i + 1) % count, i) for i in range(ends)]),
            ],
            axis=dim,
        )
    return cells


def shifted_diff(values, axis_num):
    extent = values.shape[axis_num]
    return lax.slice_in_dim(values, 1, extent, axis=axis_num) - lax.slice_in_dim(
        values, 0, extent - 1, axis=axis_num
    )


def shifted_sum(values, axis_num):
    extent = values.shape[axis_num]
    return lax.slice_in_dim(values, 1, extent, axis=axis_num) + lax.slice_in_dim(
        values, 0, extent - 1, axis=axis_num
    )


def spread_blocks(values, width):
    extent_a, extent_b, extent_c = values.shape
    wide = jnp.broadcast_to(
        values[:, None, :, None, :, None], (extent_a, width, extent_b, width, extent_c, width)
    )
    return wide.reshape(extent_a * width, extent_b * width, extent_c * width)


def moduli(substance_labels):
    shear_mod = jnp.where(
        substance_labels == 0, 3.0, jnp.where(substance_labels == 1, 2.0, 0.8)
    ).astype(jnp.float32)
    bulk_mod = jnp.where(
        substance_labels == 0, 5.0, jnp.where(substance_labels == 1, 4.0, 1.2)
    ).astype(jnp.float32)
    return (shear_mod, bulk_mod)


def face_term(element_values, axis_num):
    others = [other for other in (0, 1, 2) if other != axis_num]
    return shifted_diff(shifted_sum(shifted_sum(element_values, others[0]), others[1]), axis_num)


def element_state(node_vel, props):
    grad_x = 0.25 * shifted_diff(shifted_sum(shifted_sum(node_vel, 2), 3), 1)
    grad_y = 0.25 * shifted_diff(shifted_sum(shifted_sum(node_vel, 1), 3), 2)
    grad_z = 0.25 * shifted_diff(shifted_sum(shifted_sum(node_vel, 1), 2), 3)
    yield_eff = props[6]
    shear_mod = props[7]
    bulk_mod = props[8]
    strain_xx = TIME_STEP * grad_x[0]
    strain_yy = TIME_STEP * grad_y[1]
    strain_zz = TIME_STEP * grad_z[2]
    strain_xy = TIME_STEP * (0.5 * (grad_y[0] + grad_x[1]))
    strain_yz = TIME_STEP * (0.5 * (grad_z[1] + grad_y[2]))
    strain_xz = TIME_STEP * (0.5 * (grad_z[0] + grad_x[2]))
    volume = strain_xx + strain_yy + strain_zz
    vol_third = volume / 3.0
    trial_xx = props[0] + 2.0 * shear_mod * (strain_xx - vol_third) + bulk_mod * volume
    trial_yy = props[1] + 2.0 * shear_mod * (strain_yy - vol_third) + bulk_mod * volume
    trial_zz = props[2] + 2.0 * shear_mod * (strain_zz - vol_third) + bulk_mod * volume
    trial_xy = props[3] + 2.0 * shear_mod * strain_xy
    trial_yz = props[4] + 2.0 * shear_mod * strain_yz
    trial_xz = props[5] + 2.0 * shear_mod * strain_xz
    pressure = (trial_xx + trial_yy + trial_zz) / 3.0
    dev_xx = trial_xx - pressure
    dev_yy = trial_yy - pressure
    dev_zz = trial_zz - pressure
    second = (
        dev_xx * dev_xx
        + dev_yy * dev_yy
        + dev_zz * dev_zz
        + 2.0 * (trial_xy * trial_xy + trial_yz * trial_yz + trial_xz * trial_xz)
    )
    equivalent = jnp.sqrt(1.5 * second)
    flow_stress = yield_eff + FRICTION * jnp.maximum(-pressure, 0.0)
    excess = equivalent - flow_stress
    active = excess > 0.0
    plastic_rate = jnp.maximum(excess, 0.0) / (3.0 * shear_mod + VISCOSITY / TIME_STEP)
    scale_back = jnp.where(
        active, 1.0 - 3.0 * shear_mod * plastic_rate / jnp.where(active, equivalent, 1.0), 1.0
    )
    updated = jnp.stack(
        [
            pressure + scale_back * dev_xx,
            pressure + scale_back * dev_yy,
            pressure + scale_back * dev_zz,
            scale_back * trial_xy,
            scale_back * trial_yz,
            scale_back * trial_xz,
        ]
    )
    heat_local = (
        HEAT_SCALE * TAYLOR_QUINNEY * (equivalent - 3.0 * shear_mod * plastic_rate) * plastic_rate
    )
    return (updated, heat_local)


def node_forces(updated):
    force_x = face_term(updated[0], 0) + face_term(updated[3], 1) + face_term(updated[5], 2)
    force_y = face_term(updated[3], 0) + face_term(updated[1], 1) + face_term(updated[4], 2)
    force_z = face_term(updated[5], 0) + face_term(updated[4], 1) + face_term(updated[2], 2)
    return -0.25 * jnp.stack([force_x, force_y, force_z])


def mechanics(padded, corner_weights_diagonal):
    node_vel = padded[0:3]
    updated, heat_local = element_state(node_vel, padded[3:, :-1, :-1, :-1])
    force = node_forces(updated)
    corner_speed_later = node_vel[:, 1:-1, 1:-1, 1:-1] - TIME_STEP * force / corner_weights_diagonal
    return (corner_speed_later, updated[:, 1:, 1:, 1:], heat_local[1:, 1:, 1:])


def stencil(values, padded, matrix_main_entries):
    beside = padded[2:, 1:-1, 1:-1] + padded[:-2, 1:-1, 1:-1]
    beside = beside + padded[1:-1, 2:, 1:-1] + padded[1:-1, :-2, 1:-1]
    beside = beside + padded[1:-1, 1:-1, 2:] + padded[1:-1, 1:-1, :-2]
    return matrix_main_entries * values - beside


def diffuse_thermal_once(values, matrix_main_entries):
    haloed = extended(values, (("gx", 0), (("gy", "gz"), 1)), 1)
    padded = jnp.pad(haloed, ((0, 0), (0, 0), (1, 1)))
    return stencil(values, padded, matrix_main_entries)


def polynomial_relaxation(
    brick_warmth_prior,
    caloric_capacity_per_timestep,
    plastic_work_heating_rise,
    diffuse_thermal_field,
    inward_cell_flags,
):
    center_value = 0.5 * (UPPER_BOUND + LOWER_BOUND)
    half_width = 0.5 * (UPPER_BOUND - LOWER_BOUND)
    ratio_sig = center_value / half_width
    matrix_main_entries = 6.0 + caloric_capacity_per_timestep
    linear_system_target = (
        caloric_capacity_per_timestep * brick_warmth_prior + plastic_work_heating_rise
    )
    implicit_kelvin_result = brick_warmth_prior
    equation_misfit = (
        linear_system_target - diffuse_thermal_field(implicit_kelvin_result, matrix_main_entries)
    ) * inward_cell_flags
    weight_now = 1.0 / ratio_sig
    search_direction = equation_misfit / center_value
    for sweep_index in range(SWEEPS):
        implicit_kelvin_result = implicit_kelvin_result + search_direction
        if sweep_index + 1 < SWEEPS:
            equation_misfit = (
                equation_misfit - diffuse_thermal_field(search_direction, matrix_main_entries)
            ) * inward_cell_flags
            weight_next = 1.0 / (2.0 * ratio_sig - weight_now)
            search_direction = (
                weight_next * weight_now * search_direction
                + 2.0 * weight_next / half_width * equation_misfit
            )
            weight_now = weight_next
    return implicit_kelvin_result


def body(
    corner_speed_prior,
    brick_stress_tensor_now,
    compact_onset_strength,
    corner_weights_diagonal,
    substance_labels,
    brick_warmth_prior,
    caloric_capacity_per_timestep,
):
    z_index = lax.axis_index("gz")
    local_mat = lax.dynamic_slice_in_dim(substance_labels, z_index * ZB, ZB, 1)
    shear_blk, bulk_blk = moduli(local_mat)
    powder_cells = spread_blocks(local_mat, BS) == 2
    yield_eff = jnp.where(powder_cells, compact_onset_strength, ELASTIC_YIELD)
    stacked = jnp.concatenate(
        [
            corner_speed_prior,
            brick_stress_tensor_now,
            yield_eff[None],
            spread_blocks(shear_blk, BS)[None],
            spread_blocks(bulk_blk, BS)[None],
        ],
        axis=0,
    )
    padded = extended(stacked, (("gx", 1), ("gy", 3), ("gz", 2)), 1)
    corner_speed_later, projected_brick_stress_tensor, heat_local = mechanics(
        padded, corner_weights_diagonal
    )
    moved = lax.all_to_all(heat_local, "gz", split_axis=2, concat_axis=1, tiled=True)
    plastic_work_heating_rise = jnp.transpose(moved, (0, 2, 1))
    diffused_kelvin_field = polynomial_relaxation(
        brick_warmth_prior,
        caloric_capacity_per_timestep,
        plastic_work_heating_rise,
        diffuse_thermal_once,
        1.0,
    )
    return (corner_speed_later, projected_brick_stress_tensor, diffused_kelvin_field)


LANES = 128
VELS = 3
FIELDS = 11
SLOT = 4
RING = 12
PLANES = 14
MAIN = RING * 2 * BS
VMEM_BYTES = 48 * 1024 * 1024


def two_rounds_fit(mesh):
    return mesh.shape["gx"] == 2 and mesh.shape["gy"] == 2 and mesh.shape["gz"] == 8


def iota(shape, dim):
    return lax.broadcasted_iota(jnp.int32, shape, dim)


def place(q):
    return MAIN + RING * q if q < 5 else 2 * LANES + RING * (q - 5)


NODES = 2 * LANES + 2 * RING


def bulk_of(shear_mod):
    return jnp.where(
        shear_mod == 3.0,
        5.0,
        jnp.where(shear_mod == 2.0, 4.0, jnp.where(shear_mod == 0.0, 0.0, 1.2)),
    )


def own_labels(labels):
    second, press = labels.shape
    rows = ZB * BS
    first = lax.axis_index("gz") * ZB
    pick = iota((rows, press), 1) == first + iota((rows, press), 0) // BS
    spread = iota((second, LANES), 0) == (iota((second, LANES), 1) // BS) % second
    picked = lax.dot_general(
        pick.astype(jnp.float32),
        labels.astype(jnp.float32),
        (((1,), (1,)), ((), ())),
        preferred_element_type=jnp.float32,
    )
    return jnp.dot(picked, spread.astype(jnp.float32), preferred_element_type=jnp.float32)


FACE = (
    [(field, i) for field in range(VELS) for i in range(3)]
    + [(field, i) for field in range(VELS, 10) for i in range(2)]
    + [(10, 0)]
)
FACE_TILES = len(FACE) // 2 * ZB
PLANE = ZB * BS


def slot_at(lane, field, first):
    where = lax.rem(lane + (2 * LANES - SLOT * field) - first, LANES)
    return where < 3


def pack_kernel(
    labels, vel, stress, onset, warmth, capacity,
    wide, shear_out, face, columns, corner, warmth_out, capacity_out,
    own, own_labels_in, sems,
):
    lower_x = lax.axis_index("gx") == 0
    lower_y = lax.axis_index("gy") == 0
    deep = jnp.where(lower_x, BS - 3, 0)
    shallow = jnp.where(lower_x, BS - 2, 0)
    edge = jnp.where(lower_x, BS - 1, 0)
    copies = [
        pltpu.make_async_copy(*pair, sems.at[n])
        for n, pair in enumerate(
            (
                (labels, own_labels_in),
                (vel, own.at[pl.ds(0, VELS)]),
                (onset, own.at[9]),
                (stress, own.at[pl.ds(VELS, 6)]),
                (warmth.at[pl.ds(deep, 3)], face.at[pl.ds(FACE_TILES, 3)]),
                (capacity.at[edge], face.at[FACE_TILES + 3]),
                (warmth, warmth_out),
                (capacity, capacity_out),
            )
        )
    ]
    for copy in copies:
        copy.start()
    lane = iota((PLANE, LANES), 1)
    half = LANES // 2
    copies[0].wait()
    material = own_labels(own_labels_in[0])
    shear_mod = jnp.where(material == 0.0, 3.0, jnp.where(material == 1.0, 2.0, 0.8))
    shear_out[...] = shear_mod
    copies[1].wait()
    copies[2].wait()
    for field in range(VELS):
        wide[pl.ds(field * BS * PLANE, BS * PLANE), 0:half] = own[field].reshape(BS * PLANE, half)
    powder = material[:, 0:half] == 2.0
    for x in range(BS):
        at = pl.ds((9 * BS + x) * PLANE, PLANE)
        wide[at, 0:half] = jnp.where(powder, own[9, x], ELASTIC_YIELD)
    def read(field, x):
        if field == 10:
            return shear_mod
        return wide[pl.ds(pl.multiple_of((field * BS + x) * PLANE, PLANE), PLANE), :]

    first = jnp.where(lower_y, half - 3, 0)
    insides = [slot_at(lane, field, first) for field in range(FIELDS)]

    def pack_columns(fields, x, packed):
        for field in fields:
            turned = read(field, x)
            if field:
                turned = pltpu.roll(turned, SLOT * field, 1)
            packed = jnp.where(insides[field], turned, packed)
        columns[x] = packed

    for x in range(BS):
        pack_columns((0, 1, 2, 9, 10), x, jnp.zeros((PLANE, LANES), jnp.float32))
    copies[3].wait()
    for field in range(VELS, 9):
        wide[pl.ds(field * BS * PLANE, BS * PLANE), 0:half] = own[field].reshape(BS * PLANE, half)
    for pair in range(len(FACE) // 2):
        one, two = (
            read(field, (deep if field < VELS else shallow) + i)
            for field, i in FACE[2 * pair : 2 * pair + 2]
        )
        joined = jnp.where(lane < half, one, pltpu.roll(two, half, 1))
        face[2 * pair] = joined[:BS]
        face[2 * pair + 1] = joined[BS:]
    for x in range(BS):
        pack_columns(range(VELS, 9), x, columns[x])
    for i in range(3):
        corner[i] = columns[deep + i]
    for copy in copies[4:]:
        copy.wait()


def warmth_plane(j, warmth, face):
    upper_x = lax.axis_index("gx") == 1
    if j < 3:
        return jnp.where(upper_x, face[FACE_TILES + j], 0.0)
    if j < 11:
        return warmth[j - 3]
    return jnp.where(upper_x, 0.0, face[FACE_TILES + j - 11])


def capacity_plane(j, capacity, face):
    upper_x = lax.axis_index("gx") == 1
    if 3 <= j < 11:
        return capacity[j - 3]
    if j == 2 or j == 11:
        return jnp.where(upper_x == (j == 2), face[FACE_TILES + 3], 0.0)
    return jnp.zeros((BS, LANES), jnp.float32)


def stress_terms(shear_mod):
    bulk_mod = bulk_of(shear_mod)
    return (
        0.5 * TIME_STEP * shear_mod,
        0.25 * TIME_STEP * (bulk_mod - 2.0 / 3.0 * shear_mod),
        3.0 * shear_mod,
        1.0 / (3.0 * shear_mod + VISCOSITY / TIME_STEP),
    )


def strained(before, grads, terms):
    twice, volume_term = terms[0], terms[1]
    volume = volume_term * (grads[0] + grads[1] + grads[2])
    return [
        before[k] + twice * grads[k] + (volume if k < 3 else 0.0) for k in range(6)
    ]


def returned(trial, yield_eff, terms):
    shear_thrice, slope = terms[2], terms[3]
    pressure = (trial[0] + trial[1] + trial[2]) * (1.0 / 3.0)
    dev = [trial[k] - pressure for k in range(3)]
    second = (
        dev[0] * dev[0]
        + dev[1] * dev[1]
        + dev[2] * dev[2]
        + 2.0 * (trial[3] * trial[3] + trial[4] * trial[4] + trial[5] * trial[5])
    )
    equivalent = jnp.sqrt(1.5 * second)
    excess = equivalent - (yield_eff + FRICTION * jnp.maximum(-pressure, 0.0))
    active = excess > 0.0
    rate = jnp.maximum(excess, 0.0) * slope
    drop = shear_thrice * rate
    scale = jnp.where(active, 1.0 - drop / jnp.where(active, equivalent, 1.0), 1.0)
    heat = HEAT_SCALE * TAYLOR_QUINNEY * (equivalent - drop) * rate
    updated = [pressure + scale * dev[k] for k in range(3)] + [
        scale * trial[k] for k in range(3, 6)
    ]
    return updated, heat


def six(gx, gp, gs):
    return [
        gx[0],
        gp[1],
        gs[2],
        0.5 * (gp[0] + gx[1]),
        0.5 * (gs[1] + gp[2]),
        0.5 * (gs[0] + gx[2]),
    ]


LAYERS = 14


RIM_ROWS = 7 * BS


def rim_kernel(warmth, capacity, face, rim_out, twin_out):
    even = lax.rem(lax.axis_index("gz"), 2) == 0
    sub = iota((BS, LANES), 0)
    ups, downs = [], []
    for j in range(14):
        u = warmth_plane(j, warmth, face)
        c = capacity_plane(j, capacity, face)
        ups.append(jnp.where(sub > 4, u, pltpu.roll(c, 5, 0)))
        downs.append(jnp.where(sub < 3, u, pltpu.roll(c, 3, 0)))
    for m in range(7):
        at = pl.ds(m * BS, BS)
        up = jnp.where(sub < 4, pltpu.roll(ups[2 * m], 4, 0), ups[2 * m + 1])
        down = jnp.where(sub < 4, downs[2 * m], pltpu.roll(downs[2 * m + 1], 4, 0))
        rim_out[at, :] = jnp.where(even, down, up)
        twin_out[at, :] = jnp.where(even, up, down)


def heat_kernel(
    wide, shear, rim, rim_twin, face, columns, corner,
    chunks_out, even_out, odd_out, updated_out, partial_out,
    ext, stacked, chunks, sem,
):
    upper_x = lax.axis_index("gx") == 1
    upper_y = lax.axis_index("gy") == 1
    even = lax.rem(lax.axis_index("gz"), 2) == 0
    rows = PLANE
    half = LANES // 2
    lane = iota((rows, LANES), 1)
    first = jnp.where(upper_y, LANES - 3, half)
    beside = (lane >= first) & (lane < first + 3)
    faces = {key: at for at, key in enumerate(FACE)}

    def joined(field, plane, side):
        side = pltpu.roll(side, (half - SLOT * field) % LANES, 1)
        return jnp.where(lane < half, plane, jnp.where(beside, side, 0.0))

    def far(field, i, side):
        at = faces[field, i]
        pair = at // 2
        plane = jnp.concatenate([face[2 * pair], face[2 * pair + 1]], axis=0)
        return joined(field, pltpu.roll(plane, half, 1) if at % 2 else plane, side)

    def layer(field, j):
        if 3 <= j < 11:
            at = (field * BS + j - 3) * rows
            return joined(field, wide[pl.ds(at, rows), :], columns[j - 3])
        side = corner[j] if j < 3 else corner[j - 11]
        i = j - 11 if j >= 11 else j if field < VELS else j - 1
        plane = far(field, i, side)
        return jnp.where(upper_x, plane, 0.0) if j < 3 else jnp.where(upper_x, 0.0, plane)

    for field in range(10):
        for j in range(1, LAYERS if field < VELS else LAYERS - 1):
            ext[pl.ds((field * LAYERS + j) * rows, rows), :] = layer(field, j)
    outer = far(10, 0, corner[1])
    shears = [
        jnp.where(upper_x, outer, 0.0),
        joined(10, shear[...], columns[0]),
        jnp.where(upper_x, 0.0, outer),
    ]

    row = iota((rows, LANES), 0)

    def across(field, press):
        at = (field * LAYERS + 1) * rows + press
        return ext[pl.ds(at, rows, stride=rows), :]

    def parts(press, sign):
        terms = []
        for c in range(VELS):
            here = across(c, press)
            aside = pltpu.roll(here, LANES - 1, 1)
            total, change = here + aside, aside - here
            nxt = pltpu.roll(total, rows - 1, 0)
            both = nxt + total
            terms.append((nxt - total, sign * both, change + pltpu.roll(change, rows - 1, 0)))
        return six(*[[terms[c][d] for c in range(VELS)] for d in range(3)])

    last = rows - 1
    shear_row = [shears[block][last:, :] for block in range(3)]
    shear_mod = jnp.where(row < 2, shear_row[0], jnp.where(row < 10, shear_row[1], shear_row[2]))
    trial = strained(
        [across(VELS + k, last) for k in range(6)], parts(last, -1.0), stress_terms(shear_mod)
    )
    for q, plane in enumerate(trial + [across(9, last), shear_mod]):
        partial_out[q] = plane
    for k, plane in enumerate(parts(0, 1.0)):
        partial_out[8 + k] = plane

    sub = iota((BS, LANES), 0)
    for q in range(7):
        stacked[pl.ds(place(q), RING), :] = partial_out[q, pl.ds(0, RING), :]
    for c in range(VELS):
        stacked[pl.ds(NODES + (RING + 1) * c, RING + 1), :] = across(c, 0)[: RING + 1]

    def read(field, j):
        return ext[pl.ds((field * LAYERS + j) * rows, rows), :]

    def node_terms(j):
        terms = []
        for c in range(VELS):
            here = read(c, j)
            above = jnp.where(row == rows - 1, 0.0, pltpu.roll(here, rows - 1, 0))
            total, change = here + above, above - here
            aside = pltpu.roll(total, LANES - 1, 1)
            terms.append((total + aside, aside - total, change + pltpu.roll(change, LANES - 1, 1)))
        return terms

    materials = [stress_terms(plane) for plane in shears]
    before = node_terms(1)
    for a in range(RING):
        after = node_terms(a + 2)
        grads = six(
            [after[c][0] - before[c][0] for c in range(VELS)],
            [after[c][2] + before[c][2] for c in range(VELS)],
            [after[c][1] + before[c][1] for c in range(VELS)],
        )
        block = 0 if a < 2 else 1 if a < 10 else 2
        material = materials[block]
        trial = strained([read(VELS + k, a + 1) for k in range(6)], grads, material)
        updated, heat = returned(trial, read(9, a + 1), material)
        stacked[pl.ds(a * rows, rows), :] = jnp.where(row == rows - 1, shears[block], heat)
        if 1 <= a < 10:
            for k in range(6):
                updated_out[k, a - 1] = updated[k]
        before = after
    turned = jnp.transpose(stacked[...])
    for g in range(chunks.shape[0]):
        here, after, before = (
            turned[at % LANES : at % LANES + BS, :] for at in (g * BS, g * BS + BS, g * BS - BS)
        )
        for t in range(2):
            chunks[g, pl.ds(t * BS, BS), :] = here[:, t * LANES : (t + 1) * LANES]
        sides = [
            jnp.where(
                sub < 4,
                after[:, t * LANES : (t + 1) * LANES],
                before[:, t * LANES : (t + 1) * LANES],
            )
            for t in range(3)
        ]
        inner = jnp.where(sub < 4, pltpu.roll(sides[1], 2, 0), pltpu.roll(sides[1], 6, 0))
        chunks[g, pl.ds(2 * BS, BS), :] = jnp.where((sub < 2) | (sub > 5), sides[0], inner)
        chunks[g, pl.ds(3 * BS, BS), :] = jnp.where(
            lane[:BS] < half, here[:, 2 * LANES :], pltpu.roll(sides[2], half, 1)
        )
    copy = pltpu.make_async_copy(chunks, chunks_out, sem)
    copy.start()

    def fill(up_ref, down_ref):
        for q in range(8):
            up_ref[pl.ds(RING * q, RING), :] = partial_out[q, pl.ds(0, RING), :]
        for k in range(6):
            down_ref[pl.ds(RING * k, RING), :] = partial_out[8 + k, pl.ds(0, RING), :]
        down_ref[pl.ds(6 * RING, 2 * RING), :] = jnp.zeros((2 * RING, LANES), jnp.float32)

    @pl.when(even)
    def _():
        fill(even_out, odd_out)
        even_out[pl.ds(EDGE_ROWS, RIM_ROWS), :] = rim_twin[...]
        odd_out[pl.ds(EDGE_ROWS, RIM_ROWS), :] = rim[...]

    @pl.when(jnp.logical_not(even))
    def _():
        fill(odd_out, even_out)
        even_out[pl.ds(EDGE_ROWS, RIM_ROWS), :] = rim_twin[...]
        odd_out[pl.ds(EDGE_ROWS, RIM_ROWS), :] = rim[...]

    copy.wait()


EDGE_ROWS = 8 * RING
EDGE_ALL = EDGE_ROWS + RIM_ROWS


def corrected(planes, sign):
    rows = PLANE
    total, change, press = [], [], []
    for plane in planes:
        aside = pltpu.roll(plane, 1, 1)
        total.append(plane + aside)
        change.append(plane - aside)
        press.append(sign * (plane + aside))
    forces = []
    for kx, kp, ks in FORCE_TERMS:
        both = press[kp] + change[ks]
        forces.append(
            total[kx] - pltpu.roll(total[kx], 1, 0) + both + pltpu.roll(both, 1, 0)
        )
    return forces


FORCE_TERMS = ((0, 3, 5), (3, 1, 4), (5, 4, 2))


def gather_kernel(chunks, heats_out):
    groups = lax.axis_size("gz")
    rows = PLANE
    lane = iota((rows, LANES), 1)
    group = lane // rows
    sub = iota((BS, LANES), 0)

    sources = [[], [], []]
    for g in range(groups):
        tiles = [chunks[g, pl.ds(t * BS, BS), :] for t in range(4)]
        inner = jnp.where(sub < 4, pltpu.roll(tiles[2], 6, 0), pltpu.roll(tiles[2], 2, 0))
        outer = pltpu.roll(tiles[3], LANES // 2, 1)
        for t, pair in enumerate(((tiles[0], tiles[2]), (tiles[1], inner), (tiles[3], outer))):
            sources[t].append(jnp.concatenate(pair, axis=0))

    heats = []
    for t, count in ((0, 8), (1, 4)):
        turned = []
        for k in range(groups):
            mixed = sources[t][k]
            for b in range(1, count):
                mixed = jnp.where(group == b, sources[t][(b + k) % groups], mixed)
            turned.append(pltpu.roll(mixed, k * rows, 1) if k else mixed)
        for b in range(count):
            heat = turned[(0 - b) % groups]
            for g in range(1, groups):
                heat = jnp.where(group == g, turned[(g - b) % groups], heat)
            heats.append(heat)

    def spread(position, width, first):
        tile, at = divmod(position, LANES)
        plane = jnp.zeros((rows, LANES), jnp.float32)
        for g in range(first, groups):
            to = (g - first) * rows
            inside = (lane >= to) & (lane < to + width)
            plane = jnp.where(inside, pltpu.roll(sources[tile][g], (to - at) % LANES, 1), plane)
        return plane

    place_in = lane % rows
    trial = [spread(place(k), RING, 0) for k in range(6)]
    yield_eff = spread(place(6), RING, 0)
    shear_mod = jnp.zeros((rows, LANES), jnp.float32)
    for a in range(RING):
        turned = pltpu.roll(heats[a], (a - rows + 1) % LANES, 1)
        shear_mod = jnp.where(place_in == a, turned, shear_mod)
    gx, gp, gs = [], [], []
    for c in range(VELS):
        here = spread(NODES + (RING + 1) * c, RING + 1, 1)
        aside = pltpu.roll(here, rows - 1, 0)
        total, change = here + aside, aside - here
        nxt = pltpu.roll(total, LANES - 1, 1)
        gx.append(nxt - total)
        gp.append(nxt + total)
        gs.append(change + pltpu.roll(change, LANES - 1, 1))
    terms = stress_terms(shear_mod)
    seam = returned(strained(trial, six(gx, gp, gs), terms), yield_eff, terms)[1]
    for a in range(RING):
        heats_out[a] = jnp.where(
            place_in == rows - 1, pltpu.roll(seam, rows - 1 - a, 1), heats[a]
        )


def force_kernel(updated, vel, mass, base_out):
    rows = PLANE
    row = iota((rows, LANES), 0)

    def element_terms(j):
        terms = []
        for k in range(6):
            here = jnp.where(row == rows - 1, 0.0, updated[k, j])
            prev = pltpu.roll(here, 1, 0)
            total, change = here + prev, here - prev
            aside = pltpu.roll(total, 1, 1)
            terms.append((total + aside, total - aside, change + pltpu.roll(change, 1, 1)))
        return terms

    before = element_terms(0)
    for x in range(BS):
        after = element_terms(x + 1)
        weights = 0.25 * TIME_STEP / mass[x]
        for c, (kx, kp, ks) in enumerate(FORCE_TERMS):
            force = (
                (after[kx][0] - before[kx][0])
                + (after[kp][2] + before[kp][2])
                + (after[ks][1] + before[ks][1])
            )
            base_out[c, x] = vel[c, x] + force[:, : LANES // 2] * weights
        before = after


def finish_kernel(
    heats, base, updated, partial, mass, warmth, capacity, face, odd_in, even_in,
    vel_hbm, stress_hbm, out_hbm,
    vel_out, stress_out, out, top, low_force, high_force, sems,
):
    upper_x = lax.axis_index("gx") == 1
    at_z = lax.axis_index("gz")
    even = lax.rem(at_z, 2) == 0
    groups = lax.axis_size("gz")
    rows = PLANE
    half = LANES // 2
    at_flat = lax.axis_index("gy") * groups + at_z
    last = lax.axis_size("gy") * groups - 1
    has_above = at_z < groups - 1
    has_below = at_z > 0
    lane = iota((rows, LANES), 1)
    row = iota((rows, LANES), 0)
    sub = iota((BS, LANES), 0)

    def below_plane(q):
        at = pl.ds(RING * q, rows)
        return jnp.where(has_below, jnp.where(even, odd_in[at, :], even_in[at, :]), 0.0)

    def above_plane(k):
        at = pl.ds(RING * k, rows)
        return jnp.where(has_above, jnp.where(even, even_in[at, :], odd_in[at, :]), 0.0)

    terms = stress_terms(partial[7])
    trial = strained([partial[k] for k in range(6)], [above_plane(k) for k in range(6)], terms)
    uppermost = returned(trial, partial[6], terms)[0]
    for k, plane in enumerate(uppermost):
        top[k] = plane
    for c, plane in enumerate(corrected(uppermost, 1.0)):
        high_force[c] = plane
    terms = stress_terms(below_plane(7))
    trial = strained([below_plane(k) for k in range(6)], [partial[8 + k] for k in range(6)], terms)
    for c, plane in enumerate(corrected(returned(trial, below_plane(6), terms)[0], -1.0)):
        low_force[c] = plane
    for x in range(BS):
        at = pl.ds(x + 2, 1)
        weights = 0.25 * TIME_STEP / mass[x]
        for k in range(6):
            plane = jnp.where(row == rows - 1, top[k, at, :], updated[k, x + 1])
            stress_out[k, x] = plane[:, :half]
        for c in range(VELS):
            force = jnp.where(
                row == 0, low_force[c, at, :], jnp.where(row == rows - 1, high_force[c, at, :], 0.0)
            )
            vel_out[c, x] = base[c, x] + force[:, :half] * weights
    copies = [
        pltpu.make_async_copy(*pair, sems.at[n])
        for n, pair in enumerate(((vel_out, vel_hbm), (stress_out, stress_hbm), (out, out_hbm)))
    ]
    copies[0].start()
    copies[1].start()

    above, below = at_flat < last, at_flat > 0
    u_rows = (row < BS) | ((row < BS + 3) & above) | ((row >= rows - 3) & below)
    d_rows = (row < BS) | ((row < BS + 2) & above) | ((row >= rows - 2) & below)
    us, caps = [], []
    for j in range(14):
        at = pl.ds(EDGE_ROWS + j // 2 * BS, BS)
        low = jnp.where(even, odd_in[at, :], even_in[at, :])
        high = jnp.where(even, even_in[at, :], odd_in[at, :])
        if j % 2:
            high = pltpu.roll(high, 4, 0)
        else:
            low = pltpu.roll(low, 4, 0)
        side = jnp.where(sub < 4, high, low)
        u = jnp.concatenate([warmth_plane(j, warmth, face), side], axis=0)
        us.append(jnp.where(u_rows, u, 0.0))
        side = jnp.where(sub < 4, pltpu.roll(high, 5, 0), pltpu.roll(low, 3, 0))
        caps.append(6.0 + jnp.concatenate([capacity_plane(j, capacity, face), side], axis=0))

    def around(fields, a):
        here = fields[a]
        total = fields[a - 1] + fields[a + 1]
        total = total + pltpu.roll(here, 1, 0) + pltpu.roll(here, rows - 1, 0)
        total = total + jnp.where(lane == 0, 0.0, pltpu.roll(here, 1, 1))
        return total + jnp.where(lane == LANES - 1, 0.0, pltpu.roll(here, LANES - 1, 1))

    def inside(a):
        if a < 2:
            return d_rows & upper_x
        if a >= 10:
            return d_rows & jnp.logical_not(upper_x)
        return d_rows

    theta = 0.5 * (UPPER_BOUND + LOWER_BOUND)
    half_width = 0.5 * (UPPER_BOUND - LOWER_BOUND)
    sig = theta / half_width
    weight_now = 1.0 / sig
    misfit, step, total = {}, {}, {}
    for a in range(RING):
        misfit[a] = heats[a] - 6.0 * us[a + 1] + around(us, a + 1)
        step[a] = jnp.where(inside(a), misfit[a] * (1.0 / theta), 0.0)
        total[a] = us[a + 1] + step[a]
    for sweep in range(1, SWEEPS):
        weight_next = 1.0 / (2.0 * sig - weight_now)
        new_misfit, new_step = {}, {}
        for a in range(sweep, RING - sweep):
            new_misfit[a] = misfit[a] - caps[a + 1] * step[a] + around(step, a)
            moved = (weight_next * weight_now) * step[a] + (
                2.0 * weight_next / half_width
            ) * new_misfit[a]
            new_step[a] = jnp.where(inside(a), moved, 0.0)
            total[a] = total[a] + new_step[a]
        misfit, step, weight_now = new_misfit, new_step, weight_next
    for x in range(BS):
        out[x] = total[x + 2][:BS]
    copies[2].start()
    for copy in copies:
        copy.wait()


def f32(*shape):
    return jax.ShapeDtypeStruct(shape, jnp.float32)


def call(kernel, out_shape, *args, scratch=(), far_in=False, far_out=0):
    moved = 4 * sum(a.size for a in args) + 4 * sum(o.size for o in jax.tree.leaves(out_shape))
    hbm, vmem = (pl.BlockSpec(memory_space=space) for space in (pltpu.HBM, pltpu.VMEM))
    return pl.pallas_call(
        kernel,
        out_shape=out_shape,
        in_specs=[hbm if far_in else vmem] * len(args),
        out_specs=tuple(hbm if n < far_out else vmem for n in range(len(out_shape))),
        scratch_shapes=scratch,
        compiler_params=pltpu.CompilerParams(vmem_limit_bytes=VMEM_BYTES),
        cost_estimate=pl.CostEstimate(flops=0, bytes_accessed=moved, transcendentals=0),
    )(*args)


def room(*shape):
    return pltpu.VMEM(shape, jnp.float32)


def paired(count, first):
    pairs = []
    for i in range(first, count - 1, 2):
        pairs += [(i, i + 1), (i + 1, i)]
    return pairs


def two_round_body(
    corner_speed_prior,
    brick_stress_tensor_now,
    compact_onset_strength,
    corner_weights_diagonal,
    substance_labels,
    brick_warmth_prior,
    caloric_capacity_per_timestep,
):
    rows = PLANE
    groups = lax.axis_size("gz")
    chain = groups * lax.axis_size("gy")
    labels = jnp.transpose(substance_labels, (0, 2, 1))
    raw = (
        labels,
        corner_speed_prior,
        brick_stress_tensor_now,
        compact_onset_strength,
        brick_warmth_prior,
        caloric_capacity_per_timestep,
    )
    raw = [pltpu.with_memory_space_constraint(array, pltpu.HBM) for array in raw]
    second = compact_onset_strength.shape[-1]
    wide, shear, face, columns, corner, warmth, capacity = call(
        pack_kernel,
        (
            f32(10 * BS * rows, LANES),
            f32(rows, LANES),
            f32(FACE_TILES + 4, BS, LANES),
            f32(BS, rows, LANES),
            f32(3, rows, LANES),
            f32(*brick_warmth_prior.shape),
            f32(*brick_warmth_prior.shape),
        ),
        *raw,
        far_in=True,
        scratch=(
            room(10, BS, rows, second),
            pltpu.VMEM(labels.shape, jnp.int32),
            pltpu.SemaphoreType.DMA((len(raw) + 2,)),
        ),
    )
    face = lax.ppermute(face, "gx", [(0, 1), (1, 0)])
    columns = lax.ppermute(columns, "gy", [(0, 1), (1, 0)])
    corner = lax.ppermute(corner, ("gx", "gy"), [(0, 3), (3, 0), (1, 2), (2, 1)])
    rim, twin = call(
        rim_kernel, (f32(RIM_ROWS, LANES), f32(RIM_ROWS, LANES)), warmth, capacity, face
    )
    chunks, even, odd, updated, partial = call(
        heat_kernel,
        (
            f32(groups, 4 * BS, LANES),
            f32(EDGE_ALL, LANES),
            f32(EDGE_ALL, LANES),
            f32(6, BS + 1, rows, LANES),
            f32(PLANES, rows, LANES),
        ),
        wide,
        shear,
        rim,
        twin,
        face,
        columns,
        corner,
        scratch=(
            room((10 * LAYERS + 3) * rows, LANES),
            room(3 * LANES, LANES),
            room(groups, 4 * BS, LANES),
            pltpu.SemaphoreType.DMA,
        ),
        far_out=1,
    )
    chunks = lax.all_to_all(chunks, "gz", split_axis=0, concat_axis=0, tiled=True)
    odd = lax.ppermute(odd, ("gy", "gz"), paired(chain, 1))
    even = lax.ppermute(even, "gz", paired(groups, 0))
    (base,) = call(
        force_kernel,
        (f32(*corner_speed_prior.shape),),
        updated,
        corner_speed_prior,
        corner_weights_diagonal,
    )
    (heats,) = call(gather_kernel, (f32(RING, rows, LANES),), chunks)
    odd, even, heats, base = lax.optimization_barrier((odd, even, heats, base))
    results = (corner_speed_prior.shape, brick_stress_tensor_now.shape, brick_warmth_prior.shape)
    return call(
        finish_kernel,
        tuple(f32(*shape) for shape in results),
        heats,
        base,
        updated,
        partial,
        corner_weights_diagonal,
        warmth,
        capacity,
        face,
        odd,
        even,
        scratch=(
            *[room(*shape) for shape in results],
            room(6, rows, LANES),
            room(VELS, rows, LANES),
            room(VELS, rows, LANES),
            pltpu.SemaphoreType.DMA((3,)),
        ),
        far_out=3,
    )


def solution(mesh):
    placed = (
        P(None, "gx", "gz", "gy"),
        P(None, "gx", "gz", "gy"),
        P("gx", "gz", "gy"),
        P("gx", "gz", "gy"),
        P("gx", None, "gy"),
        P("gx", ("gy", "gz"), None),
        P("gx", ("gy", "gz"), None),
    )
    return jax.shard_map(
        two_round_body if two_rounds_fit(mesh) else body,
        mesh=mesh,
        in_specs=placed,
        out_specs=(
            P(None, "gx", "gz", "gy"),
            P(None, "gx", "gz", "gy"),
            P("gx", ("gy", "gz"), None),
        ),
        check_vma=False,
    )
```

```python
import jax
import jax.numpy as jnp
from jax import lax
from jax.experimental import pallas as pl
from jax.experimental.pallas import tpu as pltpu
from jax.sharding import PartitionSpec as P

BS = 8
ZB = 2
SWEEPS = 3


TIME_STEP = 0.2
VISCOSITY = 0.4
FRICTION = 0.5
TAYLOR_QUINNEY = 0.9
HEAT_SCALE = 5.0
ELASTIC_YIELD = 10000.0
LOWER_BOUND = 0.5
UPPER_BOUND = 16.0


def extended(cells, sides, width):
    for axis, dim in sides:
        count = lax.axis_size(axis)
        ends = count - 1
        head = lax.slice_in_dim(cells, 0, width, axis=dim)
        tail = lax.slice_in_dim(cells, cells.shape[dim] - width, cells.shape[dim], axis=dim)
        cells = jnp.concatenate(
            [
                lax.ppermute(tail, axis, [(i, (i + 1) % count) for i in range(ends)]),
                cells,
                lax.ppermute(head, axis, [((i + 1) % count, i) for i in range(ends)]),
            ],
            axis=dim,
        )
    return cells


def shifted_diff(values, axis_num):
    extent = values.shape[axis_num]
    return lax.slice_in_dim(values, 1, extent, axis=axis_num) - lax.slice_in_dim(
        values, 0, extent - 1, axis=axis_num
    )


def shifted_sum(values, axis_num):
    extent = values.shape[axis_num]
    return lax.slice_in_dim(values, 1, extent, axis=axis_num) + lax.slice_in_dim(
        values, 0, extent - 1, axis=axis_num
    )


def spread_blocks(values, width):
    extent_a, extent_b, extent_c = values.shape
    wide = jnp.broadcast_to(
        values[:, None, :, None, :, None], (extent_a, width, extent_b, width, extent_c, width)
    )
    return wide.reshape(extent_a * width, extent_b * width, extent_c * width)


def moduli(substance_labels):
    shear_mod = jnp.where(
        substance_labels == 0, 3.0, jnp.where(substance_labels == 1, 2.0, 0.8)
    ).astype(jnp.float32)
    bulk_mod = jnp.where(
        substance_labels == 0, 5.0, jnp.where(substance_labels == 1, 4.0, 1.2)
    ).astype(jnp.float32)
    return (shear_mod, bulk_mod)


def face_term(element_values, axis_num):
    others = [other for other in (0, 1, 2) if other != axis_num]
    return shifted_diff(shifted_sum(shifted_sum(element_values, others[0]), others[1]), axis_num)


def element_state(node_vel, props):
    grad_x = 0.25 * shifted_diff(shifted_sum(shifted_sum(node_vel, 2), 3), 1)
    grad_y = 0.25 * shifted_diff(shifted_sum(shifted_sum(node_vel, 1), 3), 2)
    grad_z = 0.25 * shifted_diff(shifted_sum(shifted_sum(node_vel, 1), 2), 3)
    yield_eff = props[6]
    shear_mod = props[7]
    bulk_mod = props[8]
    strain_xx = TIME_STEP * grad_x[0]
    strain_yy = TIME_STEP * grad_y[1]
    strain_zz = TIME_STEP * grad_z[2]
    strain_xy = TIME_STEP * (0.5 * (grad_y[0] + grad_x[1]))
    strain_yz = TIME_STEP * (0.5 * (grad_z[1] + grad_y[2]))
    strain_xz = TIME_STEP * (0.5 * (grad_z[0] + grad_x[2]))
    volume = strain_xx + strain_yy + strain_zz
    vol_third = volume / 3.0
    trial_xx = props[0] + 2.0 * shear_mod * (strain_xx - vol_third) + bulk_mod * volume
    trial_yy = props[1] + 2.0 * shear_mod * (strain_yy - vol_third) + bulk_mod * volume
    trial_zz = props[2] + 2.0 * shear_mod * (strain_zz - vol_third) + bulk_mod * volume
    trial_xy = props[3] + 2.0 * shear_mod * strain_xy
    trial_yz = props[4] + 2.0 * shear_mod * strain_yz
    trial_xz = props[5] + 2.0 * shear_mod * strain_xz
    pressure = (trial_xx + trial_yy + trial_zz) / 3.0
    dev_xx = trial_xx - pressure
    dev_yy = trial_yy - pressure
    dev_zz = trial_zz - pressure
    second = (
        dev_xx * dev_xx
        + dev_yy * dev_yy
        + dev_zz * dev_zz
        + 2.0 * (trial_xy * trial_xy + trial_yz * trial_yz + trial_xz * trial_xz)
    )
    equivalent = jnp.sqrt(1.5 * second)
    flow_stress = yield_eff + FRICTION * jnp.maximum(-pressure, 0.0)
    excess = equivalent - flow_stress
    active = excess > 0.0
    plastic_rate = jnp.maximum(excess, 0.0) / (3.0 * shear_mod + VISCOSITY / TIME_STEP)
    scale_back = jnp.where(
        active, 1.0 - 3.0 * shear_mod * plastic_rate / jnp.where(active, equivalent, 1.0), 1.0
    )
    updated = jnp.stack(
        [
            pressure + scale_back * dev_xx,
            pressure + scale_back * dev_yy,
            pressure + scale_back * dev_zz,
            scale_back * trial_xy,
            scale_back * trial_yz,
            scale_back * trial_xz,
        ]
    )
    heat_local = (
        HEAT_SCALE * TAYLOR_QUINNEY * (equivalent - 3.0 * shear_mod * plastic_rate) * plastic_rate
    )
    return (updated, heat_local)


def node_forces(updated):
    force_x = face_term(updated[0], 0) + face_term(updated[3], 1) + face_term(updated[5], 2)
    force_y = face_term(updated[3], 0) + face_term(updated[1], 1) + face_term(updated[4], 2)
    force_z = face_term(updated[5], 0) + face_term(updated[4], 1) + face_term(updated[2], 2)
    return -0.25 * jnp.stack([force_x, force_y, force_z])


def mechanics(padded, corner_weights_diagonal):
    node_vel = padded[0:3]
    updated, heat_local = element_state(node_vel, padded[3:, :-1, :-1, :-1])
    force = node_forces(updated)
    corner_speed_later = node_vel[:, 1:-1, 1:-1, 1:-1] - TIME_STEP * force / corner_weights_diagonal
    return (corner_speed_later, updated[:, 1:, 1:, 1:], heat_local[1:, 1:, 1:])


def stencil(values, padded, matrix_main_entries):
    beside = padded[2:, 1:-1, 1:-1] + padded[:-2, 1:-1, 1:-1]
    beside = beside + padded[1:-1, 2:, 1:-1] + padded[1:-1, :-2, 1:-1]
    beside = beside + padded[1:-1, 1:-1, 2:] + padded[1:-1, 1:-1, :-2]
    return matrix_main_entries * values - beside


def diffuse_thermal_once(values, matrix_main_entries):
    haloed = extended(values, (("gx", 0), (("gy", "gz"), 1)), 1)
    padded = jnp.pad(haloed, ((0, 0), (0, 0), (1, 1)))
    return stencil(values, padded, matrix_main_entries)


def polynomial_relaxation(
    brick_warmth_prior,
    caloric_capacity_per_timestep,
    plastic_work_heating_rise,
    diffuse_thermal_field,
    inward_cell_flags,
):
    center_value = 0.5 * (UPPER_BOUND + LOWER_BOUND)
    half_width = 0.5 * (UPPER_BOUND - LOWER_BOUND)
    ratio_sig = center_value / half_width
    matrix_main_entries = 6.0 + caloric_capacity_per_timestep
    linear_system_target = (
        caloric_capacity_per_timestep * brick_warmth_prior + plastic_work_heating_rise
    )
    implicit_kelvin_result = brick_warmth_prior
    equation_misfit = (
        linear_system_target - diffuse_thermal_field(implicit_kelvin_result, matrix_main_entries)
    ) * inward_cell_flags
    weight_now = 1.0 / ratio_sig
    search_direction = equation_misfit / center_value
    for sweep_index in range(SWEEPS):
        implicit_kelvin_result = implicit_kelvin_result + search_direction
        if sweep_index + 1 < SWEEPS:
            equation_misfit = (
                equation_misfit - diffuse_thermal_field(search_direction, matrix_main_entries)
            ) * inward_cell_flags
            weight_next = 1.0 / (2.0 * ratio_sig - weight_now)
            search_direction = (
                weight_next * weight_now * search_direction
                + 2.0 * weight_next / half_width * equation_misfit
            )
            weight_now = weight_next
    return implicit_kelvin_result


def body(
    corner_speed_prior,
    brick_stress_tensor_now,
    compact_onset_strength,
    corner_weights_diagonal,
    substance_labels,
    brick_warmth_prior,
    caloric_capacity_per_timestep,
):
    z_index = lax.axis_index("gz")
    local_mat = lax.dynamic_slice_in_dim(substance_labels, z_index * ZB, ZB, 1)
    shear_blk, bulk_blk = moduli(local_mat)
    powder_cells = spread_blocks(local_mat, BS) == 2
    yield_eff = jnp.where(powder_cells, compact_onset_strength, ELASTIC_YIELD)
    stacked = jnp.concatenate(
        [
            corner_speed_prior,
            brick_stress_tensor_now,
            yield_eff[None],
            spread_blocks(shear_blk, BS)[None],
            spread_blocks(bulk_blk, BS)[None],
        ],
        axis=0,
    )
    padded = extended(stacked, (("gx", 1), ("gy", 3), ("gz", 2)), 1)
    corner_speed_later, projected_brick_stress_tensor, heat_local = mechanics(
        padded, corner_weights_diagonal
    )
    moved = lax.all_to_all(heat_local, "gz", split_axis=2, concat_axis=1, tiled=True)
    plastic_work_heating_rise = jnp.transpose(moved, (0, 2, 1))
    diffused_kelvin_field = polynomial_relaxation(
        brick_warmth_prior,
        caloric_capacity_per_timestep,
        plastic_work_heating_rise,
        diffuse_thermal_once,
        1.0,
    )
    return (corner_speed_later, projected_brick_stress_tensor, diffused_kelvin_field)


LANES = 128
VELS = 3
FIELDS = 11
SLOT = 4
RING = 12
PLANES = 14
MAIN = RING * 2 * BS
VMEM_BYTES = 48 * 1024 * 1024


def two_rounds_fit(mesh):
    return mesh.shape["gx"] == 2 and mesh.shape["gy"] == 2 and mesh.shape["gz"] == 8


def by_shape(*args):
    fits = args[0].shape[1:] == (BS, ZB * BS, LANES // 2) and args[5].shape == (BS, BS, LANES)
    return (two_round_body if fits else body)(*args)


def iota(shape, dim):
    return lax.broadcasted_iota(jnp.int32, shape, dim)


def place(q):
    return MAIN + RING * q if q < 5 else 2 * LANES + RING * (q - 5)


NODES = 2 * LANES + 2 * RING


def bulk_of(shear_mod):
    return jnp.where(
        shear_mod == 3.0,
        5.0,
        jnp.where(shear_mod == 2.0, 4.0, jnp.where(shear_mod == 0.0, 0.0, 1.2)),
    )


def own_labels(labels):
    second, press = labels.shape
    rows = ZB * BS
    first = lax.axis_index("gz") * ZB
    pick = iota((rows, press), 1) == first + iota((rows, press), 0) // BS
    spread = iota((second, LANES), 0) == (iota((second, LANES), 1) // BS) % second
    picked = lax.dot_general(
        pick.astype(jnp.float32),
        labels.astype(jnp.float32),
        (((1,), (1,)), ((), ())),
        preferred_element_type=jnp.float32,
    )
    return jnp.dot(picked, spread.astype(jnp.float32), preferred_element_type=jnp.float32)


FACE = (
    [(field, i) for field in range(VELS) for i in range(3)]
    + [(field, i) for field in range(VELS, 10) for i in range(2)]
    + [(10, 0)]
)
FACE_TILES = len(FACE) // 2 * ZB
PLANE = ZB * BS


def slot_at(lane, field, first):
    where = lax.rem(lane + (2 * LANES - SLOT * field) - first, LANES)
    return where < 3


def pack_kernel(
    labels, vel, stress, onset, warmth, capacity,
    wide, shear_out, face, columns, corner, warmth_out, capacity_out,
    own, own_labels_in, sems,
):
    lower_x = lax.axis_index("gx") == 0
    lower_y = lax.axis_index("gy") == 0
    deep = jnp.where(lower_x, BS - 3, 0)
    shallow = jnp.where(lower_x, BS - 2, 0)
    edge = jnp.where(lower_x, BS - 1, 0)
    copies = [
        pltpu.make_async_copy(*pair, sems.at[n])
        for n, pair in enumerate(
            (
                (labels, own_labels_in),
                (vel, own.at[pl.ds(0, VELS)]),
                (onset, own.at[9]),
                (stress, own.at[pl.ds(VELS, 6)]),
                (warmth.at[pl.ds(deep, 3)], face.at[pl.ds(FACE_TILES, 3)]),
                (capacity.at[edge], face.at[FACE_TILES + 3]),
                (warmth, warmth_out),
                (capacity, capacity_out),
            )
        )
    ]
    for copy in copies:
        copy.start()
    lane = iota((PLANE, LANES), 1)
    half = LANES // 2
    copies[0].wait()
    material = own_labels(own_labels_in[0])
    shear_mod = jnp.where(material == 0.0, 3.0, jnp.where(material == 1.0, 2.0, 0.8))
    shear_out[...] = shear_mod
    copies[1].wait()
    copies[2].wait()
    for field in range(VELS):
        wide[pl.ds(field * BS * PLANE, BS * PLANE), 0:half] = own[field].reshape(BS * PLANE, half)
    powder = material[:, 0:half] == 2.0
    for x in range(BS):
        at = pl.ds((9 * BS + x) * PLANE, PLANE)
        wide[at, 0:half] = jnp.where(powder, own[9, x], ELASTIC_YIELD)
    def read(field, x):
        if field == 10:
            return shear_mod
        return wide[pl.ds(pl.multiple_of((field * BS + x) * PLANE, PLANE), PLANE), :]

    first = jnp.where(lower_y, half - 3, 0)
    insides = [slot_at(lane, field, first) for field in range(FIELDS)]

    def pack_columns(fields, x, packed):
        for field in fields:
            turned = read(field, x)
            if field:
                turned = pltpu.roll(turned, SLOT * field, 1)
            packed = jnp.where(insides[field], turned, packed)
        columns[x] = packed

    for x in range(BS):
        pack_columns((0, 1, 2, 9, 10), x, jnp.zeros((PLANE, LANES), jnp.float32))
    copies[3].wait()
    for field in range(VELS, 9):
        wide[pl.ds(field * BS * PLANE, BS * PLANE), 0:half] = own[field].reshape(BS * PLANE, half)
    for pair in range(len(FACE) // 2):
        one, two = (
            read(field, (deep if field < VELS else shallow) + i)
            for field, i in FACE[2 * pair : 2 * pair + 2]
        )
        joined = jnp.where(lane < half, one, pltpu.roll(two, half, 1))
        face[2 * pair] = joined[:BS]
        face[2 * pair + 1] = joined[BS:]
    for x in range(BS):
        pack_columns(range(VELS, 9), x, columns[x])
    for i in range(3):
        corner[i] = columns[deep + i]
    for copy in copies[4:]:
        copy.wait()


def warmth_plane(j, warmth, face):
    upper_x = lax.axis_index("gx") == 1
    if j < 3:
        return jnp.where(upper_x, face[FACE_TILES + j], 0.0)
    if j < 11:
        return warmth[j - 3]
    return jnp.where(upper_x, 0.0, face[FACE_TILES + j - 11])


def capacity_plane(j, capacity, face):
    upper_x = lax.axis_index("gx") == 1
    if 3 <= j < 11:
        return capacity[j - 3]
    if j == 2 or j == 11:
        return jnp.where(upper_x == (j == 2), face[FACE_TILES + 3], 0.0)
    return jnp.zeros((BS, LANES), jnp.float32)


def stress_terms(shear_mod):
    bulk_mod = bulk_of(shear_mod)
    return (
        0.5 * TIME_STEP * shear_mod,
        0.25 * TIME_STEP * (bulk_mod - 2.0 / 3.0 * shear_mod),
        3.0 * shear_mod,
        1.0 / (3.0 * shear_mod + VISCOSITY / TIME_STEP),
    )


def strained(before, grads, terms):
    twice, volume_term = terms[0], terms[1]
    volume = volume_term * (grads[0] + grads[1] + grads[2])
    return [
        before[k] + twice * grads[k] + (volume if k < 3 else 0.0) for k in range(6)
    ]


def returned(trial, yield_eff, terms):
    shear_thrice, slope = terms[2], terms[3]
    pressure = (trial[0] + trial[1] + trial[2]) * (1.0 / 3.0)
    dev = [trial[k] - pressure for k in range(3)]
    second = (
        dev[0] * dev[0]
        + dev[1] * dev[1]
        + dev[2] * dev[2]
        + 2.0 * (trial[3] * trial[3] + trial[4] * trial[4] + trial[5] * trial[5])
    )
    equivalent = jnp.sqrt(1.5 * second)
    excess = equivalent - (yield_eff + FRICTION * jnp.maximum(-pressure, 0.0))
    active = excess > 0.0
    rate = jnp.maximum(excess, 0.0) * slope
    drop = shear_thrice * rate
    scale = jnp.where(active, 1.0 - drop / jnp.where(active, equivalent, 1.0), 1.0)
    heat = HEAT_SCALE * TAYLOR_QUINNEY * (equivalent - drop) * rate
    updated = [pressure + scale * dev[k] for k in range(3)] + [
        scale * trial[k] for k in range(3, 6)
    ]
    return updated, heat


def six(gx, gp, gs):
    return [
        gx[0],
        gp[1],
        gs[2],
        0.5 * (gp[0] + gx[1]),
        0.5 * (gs[1] + gp[2]),
        0.5 * (gs[0] + gx[2]),
    ]


LAYERS = 14


RIM_PAIRS = RING // 2
RIM_ROWS = RIM_PAIRS * BS


def rim_kernel(warmth, capacity, face, rim_out, twin_out):
    even = lax.rem(lax.axis_index("gz"), 2) == 0
    sub = iota((BS, LANES), 0)
    ups, downs = [], []
    for j in range(1, RING + 1):
        u = warmth_plane(j, warmth, face)
        c = capacity_plane(j, capacity, face)
        ups.append(jnp.where(sub > 4, u, pltpu.roll(c, 5, 0)))
        downs.append(jnp.where(sub < 3, u, pltpu.roll(c, 3, 0)))
    for m in range(RIM_PAIRS):
        at = pl.ds(m * BS, BS)
        up = jnp.where(sub < 4, pltpu.roll(ups[2 * m], 4, 0), ups[2 * m + 1])
        down = jnp.where(sub < 4, downs[2 * m], pltpu.roll(downs[2 * m + 1], 4, 0))
        rim_out[at, :] = jnp.where(even, down, up)
        twin_out[at, :] = jnp.where(even, up, down)


def heat_kernel(
    wide, shear, rim, rim_twin, face, columns, corner,
    chunks_out, even_out, odd_out, updated_out, partial_out,
    ext, stacked, chunks, sem,
):
    upper_x = lax.axis_index("gx") == 1
    upper_y = lax.axis_index("gy") == 1
    even = lax.rem(lax.axis_index("gz"), 2) == 0
    rows = PLANE
    half = LANES // 2
    lane = iota((rows, LANES), 1)
    first = jnp.where(upper_y, LANES - 3, half)
    beside = (lane >= first) & (lane < first + 3)
    faces = {key: at for at, key in enumerate(FACE)}

    def joined(field, plane, side):
        side = pltpu.roll(side, (half - SLOT * field) % LANES, 1)
        return jnp.where(lane < half, plane, jnp.where(beside, side, 0.0))

    def far(field, i, side):
        at = faces[field, i]
        pair = at // 2
        plane = jnp.concatenate([face[2 * pair], face[2 * pair + 1]], axis=0)
        return joined(field, pltpu.roll(plane, half, 1) if at % 2 else plane, side)

    def layer(field, j):
        if 3 <= j < 11:
            at = (field * BS + j - 3) * rows
            return joined(field, wide[pl.ds(at, rows), :], columns[j - 3])
        side = corner[j] if j < 3 else corner[j - 11]
        i = j - 11 if j >= 11 else j if field < VELS else j - 1
        plane = far(field, i, side)
        return jnp.where(upper_x, plane, 0.0) if j < 3 else jnp.where(upper_x, 0.0, plane)

    for field in range(10):
        for j in range(1, LAYERS if field < VELS else LAYERS - 1):
            ext[pl.ds((field * LAYERS + j) * rows, rows), :] = layer(field, j)
    outer = far(10, 0, corner[1])
    shears = [
        jnp.where(upper_x, outer, 0.0),
        joined(10, shear[...], columns[0]),
        jnp.where(upper_x, 0.0, outer),
    ]

    row = iota((rows, LANES), 0)

    def across(field, press):
        at = (field * LAYERS + 1) * rows + press
        return ext[pl.ds(at, rows, stride=rows), :]

    def parts(press, sign):
        terms = []
        for c in range(VELS):
            here = across(c, press)
            aside = pltpu.roll(here, LANES - 1, 1)
            total, change = here + aside, aside - here
            nxt = pltpu.roll(total, rows - 1, 0)
            both = nxt + total
            terms.append((nxt - total, sign * both, change + pltpu.roll(change, rows - 1, 0)))
        return six(*[[terms[c][d] for c in range(VELS)] for d in range(3)])

    last = rows - 1
    shear_row = [shears[block][last:, :] for block in range(3)]
    shear_mod = jnp.where(row < 2, shear_row[0], jnp.where(row < 10, shear_row[1], shear_row[2]))
    trial = strained(
        [across(VELS + k, last) for k in range(6)], parts(last, -1.0), stress_terms(shear_mod)
    )
    for q, plane in enumerate(trial + [across(9, last), shear_mod]):
        partial_out[q] = plane
    for k, plane in enumerate(parts(0, 1.0)):
        partial_out[8 + k] = plane

    sub = iota((BS, LANES), 0)
    for q in range(7):
        stacked[pl.ds(place(q), RING), :] = partial_out[q, pl.ds(0, RING), :]
    for c in range(VELS):
        stacked[pl.ds(NODES + (RING + 1) * c, RING + 1), :] = across(c, 0)[: RING + 1]

    def read(field, j):
        return ext[pl.ds((field * LAYERS + j) * rows, rows), :]

    def node_terms(j):
        terms = []
        for c in range(VELS):
            here = read(c, j)
            above = jnp.where(row == rows - 1, 0.0, pltpu.roll(here, rows - 1, 0))
            total, change = here + above, above - here
            aside = pltpu.roll(total, LANES - 1, 1)
            terms.append((total + aside, aside - total, change + pltpu.roll(change, LANES - 1, 1)))
        return terms

    materials = [stress_terms(plane) for plane in shears]
    before = node_terms(1)
    for a in range(RING):
        after = node_terms(a + 2)
        grads = six(
            [after[c][0] - before[c][0] for c in range(VELS)],
            [after[c][2] + before[c][2] for c in range(VELS)],
            [after[c][1] + before[c][1] for c in range(VELS)],
        )
        block = 0 if a < 2 else 1 if a < 10 else 2
        material = materials[block]
        trial = strained([read(VELS + k, a + 1) for k in range(6)], grads, material)
        updated, heat = returned(trial, read(9, a + 1), material)
        stacked[pl.ds(a * rows, rows), :] = jnp.where(row == rows - 1, shears[block], heat)
        if 1 <= a < 10:
            for k in range(6):
                updated_out[k, a - 1] = updated[k]
        before = after
    turned = jnp.transpose(stacked[...])
    for g in range(chunks.shape[0]):
        here, after, before = (
            turned[at % LANES : at % LANES + BS, :] for at in (g * BS, g * BS + BS, g * BS - BS)
        )
        for t in range(2):
            chunks[g, pl.ds(t * BS, BS), :] = here[:, t * LANES : (t + 1) * LANES]
        sides = [
            jnp.where(
                sub < 4,
                after[:, t * LANES : (t + 1) * LANES],
                before[:, t * LANES : (t + 1) * LANES],
            )
            for t in range(3)
        ]
        inner = jnp.where(sub < 4, pltpu.roll(sides[1], 2, 0), pltpu.roll(sides[1], 6, 0))
        chunks[g, pl.ds(2 * BS, BS), :] = jnp.where((sub < 2) | (sub > 5), sides[0], inner)
        chunks[g, pl.ds(3 * BS, BS), :] = jnp.where(
            lane[:BS] < half, here[:, 2 * LANES :], pltpu.roll(sides[2], half, 1)
        )
    copy = pltpu.make_async_copy(chunks, chunks_out, sem)
    copy.start()

    def fill(up_ref, down_ref):
        for q in range(8):
            up_ref[pl.ds(RIM_ROWS + NEAR * q, NEAR), :] = partial_out[q, pl.ds(1, NEAR), :]
        for k in range(6):
            down_ref[pl.ds(RIM_ROWS + NEAR * k, NEAR), :] = partial_out[8 + k, pl.ds(1, NEAR), :]
        for ref, count in ((up_ref, 8), (down_ref, 6)):
            rest = EDGE_ALL - RIM_ROWS - NEAR * count
            ref[pl.ds(EDGE_ALL - rest, rest), :] = jnp.zeros((rest, LANES), jnp.float32)
        even_out[pl.ds(0, RIM_ROWS), :] = rim_twin[...]
        odd_out[pl.ds(0, RIM_ROWS), :] = rim[...]

    @pl.when(even)
    def _():
        fill(even_out, odd_out)

    @pl.when(jnp.logical_not(even))
    def _():
        fill(odd_out, even_out)

    copy.wait()


NEAR = BS + 1
EDGE_ALL = RIM_ROWS + 8 * NEAR + BS


def corrected(planes, sign):
    rows = PLANE
    total, change, press = [], [], []
    for plane in planes:
        aside = pltpu.roll(plane, 1, 1)
        total.append(plane + aside)
        change.append(plane - aside)
        press.append(sign * (plane + aside))
    forces = []
    for kx, kp, ks in FORCE_TERMS:
        both = press[kp] + change[ks]
        forces.append(
            total[kx] - pltpu.roll(total[kx], 1, 0) + both + pltpu.roll(both, 1, 0)
        )
    return forces


FORCE_TERMS = ((0, 3, 5), (3, 1, 4), (5, 4, 2))


def gather_kernel(chunks, heats_out):
    groups = lax.axis_size("gz")
    rows = PLANE
    lane = iota((rows, LANES), 1)
    group = lane // rows
    sub = iota((BS, LANES), 0)

    sources = [[], [], []]
    for g in range(groups):
        tiles = [chunks[g, pl.ds(t * BS, BS), :] for t in range(4)]
        inner = jnp.where(sub < 4, pltpu.roll(tiles[2], 6, 0), pltpu.roll(tiles[2], 2, 0))
        outer = pltpu.roll(tiles[3], LANES // 2, 1)
        for t, pair in enumerate(((tiles[0], tiles[2]), (tiles[1], inner), (tiles[3], outer))):
            sources[t].append(jnp.concatenate(pair, axis=0))

    heats = []
    for t, count in ((0, 8), (1, 4)):
        turned = []
        for k in range(groups):
            mixed = sources[t][k]
            for b in range(1, count):
                mixed = jnp.where(group == b, sources[t][(b + k) % groups], mixed)
            turned.append(pltpu.roll(mixed, k * rows, 1) if k else mixed)
        for b in range(count):
            heat = turned[(0 - b) % groups]
            for g in range(1, groups):
                heat = jnp.where(group == g, turned[(g - b) % groups], heat)
            heats.append(heat)

    def spread(position, width, first):
        tile, at = divmod(position, LANES)
        plane = jnp.zeros((rows, LANES), jnp.float32)
        for g in range(first, groups):
            to = (g - first) * rows
            inside = (lane >= to) & (lane < to + width)
            plane = jnp.where(inside, pltpu.roll(sources[tile][g], (to - at) % LANES, 1), plane)
        return plane

    place_in = lane % rows
    trial = [spread(place(k), RING, 0) for k in range(6)]
    yield_eff = spread(place(6), RING, 0)
    shear_mod = jnp.zeros((rows, LANES), jnp.float32)
    for a in range(RING):
        turned = pltpu.roll(heats[a], (a - rows + 1) % LANES, 1)
        shear_mod = jnp.where(place_in == a, turned, shear_mod)
    gx, gp, gs = [], [], []
    for c in range(VELS):
        here = spread(NODES + (RING + 1) * c, RING + 1, 1)
        aside = pltpu.roll(here, rows - 1, 0)
        total, change = here + aside, aside - here
        nxt = pltpu.roll(total, LANES - 1, 1)
        gx.append(nxt - total)
        gp.append(nxt + total)
        gs.append(change + pltpu.roll(change, LANES - 1, 1))
    terms = stress_terms(shear_mod)
    seam = returned(strained(trial, six(gx, gp, gs), terms), yield_eff, terms)[1]
    for a in range(RING):
        heats_out[a] = jnp.where(
            place_in == rows - 1, pltpu.roll(seam, rows - 1 - a, 1), heats[a]
        )


def force_kernel(updated, vel, mass, base_out):
    rows = PLANE
    row = iota((rows, LANES), 0)

    def element_terms(j):
        terms = []
        for k in range(6):
            here = jnp.where(row == rows - 1, 0.0, updated[k, j])
            prev = pltpu.roll(here, 1, 0)
            total, change = here + prev, here - prev
            aside = pltpu.roll(total, 1, 1)
            terms.append((total + aside, total - aside, change + pltpu.roll(change, 1, 1)))
        return terms

    before = element_terms(0)
    for x in range(BS):
        after = element_terms(x + 1)
        weights = 0.25 * TIME_STEP / mass[x]
        for c, (kx, kp, ks) in enumerate(FORCE_TERMS):
            force = (
                (after[kx][0] - before[kx][0])
                + (after[kp][2] + before[kp][2])
                + (after[ks][1] + before[ks][1])
            )
            base_out[c, x] = vel[c, x] + force[:, : LANES // 2] * weights
        before = after


def finish_kernel(
    heats, base, updated, partial, mass, warmth, capacity, face, odd_in, even_in,
    vel_hbm, stress_hbm, out_hbm,
    vel_out, stress_out, out, top, low_force, high_force, sems,
):
    upper_x = lax.axis_index("gx") == 1
    at_z = lax.axis_index("gz")
    even = lax.rem(at_z, 2) == 0
    groups = lax.axis_size("gz")
    rows = PLANE
    half = LANES // 2
    at_flat = lax.axis_index("gy") * groups + at_z
    last = lax.axis_size("gy") * groups - 1
    has_above = at_z < groups - 1
    has_below = at_z > 0
    lane = iota((rows, LANES), 1)
    row = iota((rows, LANES), 0)
    sub = iota((BS, LANES), 0)

    def below_plane(q):
        at = pl.ds(RIM_ROWS + NEAR * q - 1, rows)
        return jnp.where(has_below, jnp.where(even, odd_in[at, :], even_in[at, :]), 0.0)

    def above_plane(k):
        at = pl.ds(RIM_ROWS + NEAR * k - 1, rows)
        return jnp.where(has_above, jnp.where(even, even_in[at, :], odd_in[at, :]), 0.0)

    terms = stress_terms(partial[7])
    trial = strained([partial[k] for k in range(6)], [above_plane(k) for k in range(6)], terms)
    uppermost = returned(trial, partial[6], terms)[0]
    for k, plane in enumerate(uppermost):
        top[k] = plane
    for c, plane in enumerate(corrected(uppermost, 1.0)):
        high_force[c] = plane
    terms = stress_terms(below_plane(7))
    trial = strained([below_plane(k) for k in range(6)], [partial[8 + k] for k in range(6)], terms)
    for c, plane in enumerate(corrected(returned(trial, below_plane(6), terms)[0], -1.0)):
        low_force[c] = plane
    for x in range(BS):
        at = pl.ds(x + 2, 1)
        weights = 0.25 * TIME_STEP / mass[x]
        for k in range(6):
            plane = jnp.where(row == rows - 1, top[k, at, :], updated[k, x + 1])
            stress_out[k, x] = plane[:, :half]
        for c in range(VELS):
            force = jnp.where(
                row == 0, low_force[c, at, :], jnp.where(row == rows - 1, high_force[c, at, :], 0.0)
            )
            vel_out[c, x] = base[c, x] + force[:, :half] * weights
    copies = [
        pltpu.make_async_copy(*pair, sems.at[n])
        for n, pair in enumerate(((vel_out, vel_hbm), (stress_out, stress_hbm), (out, out_hbm)))
    ]
    copies[0].start()
    copies[1].start()

    above, below = at_flat < last, at_flat > 0
    u_rows = (row < BS) | ((row < BS + 3) & above) | ((row >= rows - 3) & below)
    d_rows = (row < BS) | ((row < BS + 2) & above) | ((row >= rows - 2) & below)
    us, caps = [], []
    for j in range(14):
        at = pl.ds(min(max(j - 1, 0), RING - 1) // 2 * BS, BS)
        low = jnp.where(even, odd_in[at, :], even_in[at, :])
        high = jnp.where(even, even_in[at, :], odd_in[at, :])
        if j % 2:
            low = pltpu.roll(low, 4, 0)
        else:
            high = pltpu.roll(high, 4, 0)
        side = jnp.where(sub < 4, high, low)
        u = jnp.concatenate([warmth_plane(j, warmth, face), side], axis=0)
        us.append(jnp.where(u_rows, u, 0.0))
        side = jnp.where(sub < 4, pltpu.roll(high, 5, 0), pltpu.roll(low, 3, 0))
        caps.append(6.0 + jnp.concatenate([capacity_plane(j, capacity, face), side], axis=0))

    def around(fields, a):
        here = fields[a]
        total = fields[a - 1] + fields[a + 1]
        total = total + pltpu.roll(here, 1, 0) + pltpu.roll(here, rows - 1, 0)
        total = total + jnp.where(lane == 0, 0.0, pltpu.roll(here, 1, 1))
        return total + jnp.where(lane == LANES - 1, 0.0, pltpu.roll(here, LANES - 1, 1))

    def inside(a):
        if a < 2:
            return d_rows & upper_x
        if a >= 10:
            return d_rows & jnp.logical_not(upper_x)
        return d_rows

    theta = 0.5 * (UPPER_BOUND + LOWER_BOUND)
    half_width = 0.5 * (UPPER_BOUND - LOWER_BOUND)
    sig = theta / half_width
    weight_now = 1.0 / sig
    misfit, step, total = {}, {}, {}
    for a in range(RING):
        misfit[a] = heats[a] - 6.0 * us[a + 1] + around(us, a + 1)
        step[a] = jnp.where(inside(a), misfit[a] * (1.0 / theta), 0.0)
        total[a] = us[a + 1] + step[a]
    for sweep in range(1, SWEEPS):
        weight_next = 1.0 / (2.0 * sig - weight_now)
        new_misfit, new_step = {}, {}
        for a in range(sweep, RING - sweep):
            new_misfit[a] = misfit[a] - caps[a + 1] * step[a] + around(step, a)
            moved = (weight_next * weight_now) * step[a] + (
                2.0 * weight_next / half_width
            ) * new_misfit[a]
            new_step[a] = jnp.where(inside(a), moved, 0.0)
            total[a] = total[a] + new_step[a]
        misfit, step, weight_now = new_misfit, new_step, weight_next
    for x in range(BS):
        out[x] = total[x + 2][:BS]
    copies[2].start()
    for copy in copies:
        copy.wait()


def f32(*shape):
    return jax.ShapeDtypeStruct(shape, jnp.float32)


def call(kernel, out_shape, *args, scratch=(), far_in=False, far_out=0):
    moved = 4 * sum(a.size for a in args) + 4 * sum(o.size for o in jax.tree.leaves(out_shape))
    hbm, vmem = (pl.BlockSpec(memory_space=space) for space in (pltpu.HBM, pltpu.VMEM))
    return pl.pallas_call(
        kernel,
        out_shape=out_shape,
        in_specs=[hbm if far_in else vmem] * len(args),
        out_specs=tuple(hbm if n < far_out else vmem for n in range(len(out_shape))),
        scratch_shapes=scratch,
        compiler_params=pltpu.CompilerParams(vmem_limit_bytes=VMEM_BYTES),
        cost_estimate=pl.CostEstimate(flops=0, bytes_accessed=moved, transcendentals=0),
    )(*args)


def room(*shape):
    return pltpu.VMEM(shape, jnp.float32)


def paired(count, first):
    pairs = []
    for i in range(first, count - 1, 2):
        pairs += [(i, i + 1), (i + 1, i)]
    return pairs


def two_round_body(
    corner_speed_prior,
    brick_stress_tensor_now,
    compact_onset_strength,
    corner_weights_diagonal,
    substance_labels,
    brick_warmth_prior,
    caloric_capacity_per_timestep,
):
    rows = PLANE
    groups = lax.axis_size("gz")
    chain = groups * lax.axis_size("gy")
    labels = jnp.transpose(substance_labels, (0, 2, 1))
    raw = (
        labels,
        corner_speed_prior,
        brick_stress_tensor_now,
        compact_onset_strength,
        brick_warmth_prior,
        caloric_capacity_per_timestep,
    )
    raw = [pltpu.with_memory_space_constraint(array, pltpu.HBM) for array in raw]
    second = compact_onset_strength.shape[-1]
    wide, shear, face, columns, corner, warmth, capacity = call(
        pack_kernel,
        (
            f32(10 * BS * rows, LANES),
            f32(rows, LANES),
            f32(FACE_TILES + 4, BS, LANES),
            f32(BS, rows, LANES),
            f32(3, rows, LANES),
            f32(*brick_warmth_prior.shape),
            f32(*brick_warmth_prior.shape),
        ),
        *raw,
        far_in=True,
        scratch=(
            room(10, BS, rows, second),
            pltpu.VMEM(labels.shape, jnp.int32),
            pltpu.SemaphoreType.DMA((len(raw) + 2,)),
        ),
    )
    face = lax.ppermute(face, "gx", [(0, 1), (1, 0)])
    columns = lax.ppermute(columns, "gy", [(0, 1), (1, 0)])
    corner = lax.ppermute(corner, ("gx", "gy"), [(0, 3), (3, 0), (1, 2), (2, 1)])
    rim, twin = call(
        rim_kernel, (f32(RIM_ROWS, LANES), f32(RIM_ROWS, LANES)), warmth, capacity, face
    )
    chunks, even, odd, updated, partial = call(
        heat_kernel,
        (
            f32(groups, 4 * BS, LANES),
            f32(EDGE_ALL, LANES),
            f32(EDGE_ALL, LANES),
            f32(6, BS + 1, rows, LANES),
            f32(PLANES, rows, LANES),
        ),
        wide,
        shear,
        rim,
        twin,
        face,
        columns,
        corner,
        scratch=(
            room((10 * LAYERS + 3) * rows, LANES),
            room(3 * LANES, LANES),
            room(groups, 4 * BS, LANES),
            pltpu.SemaphoreType.DMA,
        ),
        far_out=1,
    )
    chunks = lax.all_to_all(chunks, "gz", split_axis=0, concat_axis=0, tiled=True)
    odd = lax.ppermute(odd, ("gy", "gz"), paired(chain, 1))
    even = lax.ppermute(even, "gz", paired(groups, 0))
    (base,) = call(
        force_kernel,
        (f32(*corner_speed_prior.shape),),
        updated,
        corner_speed_prior,
        corner_weights_diagonal,
    )
    (heats,) = call(gather_kernel, (f32(RING, rows, LANES),), chunks)
    odd, even, heats, base = lax.optimization_barrier((odd, even, heats, base))
    results = (corner_speed_prior.shape, brick_stress_tensor_now.shape, brick_warmth_prior.shape)
    return call(
        finish_kernel,
        tuple(f32(*shape) for shape in results),
        heats,
        base,
        updated,
        partial,
        corner_weights_diagonal,
        warmth,
        capacity,
        face,
        odd,
        even,
        scratch=(
            *[room(*shape) for shape in results],
            room(6, rows, LANES),
            room(VELS, rows, LANES),
            room(VELS, rows, LANES),
            pltpu.SemaphoreType.DMA((3,)),
        ),
        far_out=3,
    )


def solution(mesh):
    placed = (
        P(None, "gx", "gz", "gy"),
        P(None, "gx", "gz", "gy"),
        P("gx", "gz", "gy"),
        P("gx", "gz", "gy"),
        P("gx", None, "gy"),
        P("gx", ("gy", "gz"), None),
        P("gx", ("gy", "gz"), None),
    )
    return jax.shard_map(
        by_shape if two_rounds_fit(mesh) else body,
        mesh=mesh,
        in_specs=placed,
        out_specs=(
            P(None, "gx", "gz", "gy"),
            P(None, "gx", "gz", "gy"),
            P("gx", ("gy", "gz"), None),
        ),
        check_vma=False,
    )
```

```python
import jax
import jax.numpy as jnp
from jax import lax
from jax.experimental import pallas as pl
from jax.experimental.pallas import tpu as pltpu
from jax.sharding import PartitionSpec as P

BS = 8
ZB = 2
SWEEPS = 3


TIME_STEP = 0.2
VISCOSITY = 0.4
FRICTION = 0.5
TAYLOR_QUINNEY = 0.9
HEAT_SCALE = 5.0
ELASTIC_YIELD = 10000.0
LOWER_BOUND = 0.5
UPPER_BOUND = 16.0


def extended(cells, sides, width):
    for axis, dim in sides:
        count = lax.axis_size(axis)
        ends = count - 1
        head = lax.slice_in_dim(cells, 0, width, axis=dim)
        tail = lax.slice_in_dim(cells, cells.shape[dim] - width, cells.shape[dim], axis=dim)
        cells = jnp.concatenate(
            [
                lax.ppermute(tail, axis, [(i, (i + 1) % count) for i in range(ends)]),
                cells,
                lax.ppermute(head, axis, [((i + 1) % count, i) for i in range(ends)]),
            ],
            axis=dim,
        )
    return cells


def shifted_diff(values, axis_num):
    extent = values.shape[axis_num]
    return lax.slice_in_dim(values, 1, extent, axis=axis_num) - lax.slice_in_dim(
        values, 0, extent - 1, axis=axis_num
    )


def shifted_sum(values, axis_num):
    extent = values.shape[axis_num]
    return lax.slice_in_dim(values, 1, extent, axis=axis_num) + lax.slice_in_dim(
        values, 0, extent - 1, axis=axis_num
    )


def spread_blocks(values, width):
    extent_a, extent_b, extent_c = values.shape
    wide = jnp.broadcast_to(
        values[:, None, :, None, :, None], (extent_a, width, extent_b, width, extent_c, width)
    )
    return wide.reshape(extent_a * width, extent_b * width, extent_c * width)


def moduli(substance_labels):
    shear_mod = jnp.where(
        substance_labels == 0, 3.0, jnp.where(substance_labels == 1, 2.0, 0.8)
    ).astype(jnp.float32)
    bulk_mod = jnp.where(
        substance_labels == 0, 5.0, jnp.where(substance_labels == 1, 4.0, 1.2)
    ).astype(jnp.float32)
    return (shear_mod, bulk_mod)


def face_term(element_values, axis_num):
    others = [other for other in (0, 1, 2) if other != axis_num]
    return shifted_diff(shifted_sum(shifted_sum(element_values, others[0]), others[1]), axis_num)


def element_state(node_vel, props):
    grad_x = 0.25 * shifted_diff(shifted_sum(shifted_sum(node_vel, 2), 3), 1)
    grad_y = 0.25 * shifted_diff(shifted_sum(shifted_sum(node_vel, 1), 3), 2)
    grad_z = 0.25 * shifted_diff(shifted_sum(shifted_sum(node_vel, 1), 2), 3)
    yield_eff = props[6]
    shear_mod = props[7]
    bulk_mod = props[8]
    strain_xx = TIME_STEP * grad_x[0]
    strain_yy = TIME_STEP * grad_y[1]
    strain_zz = TIME_STEP * grad_z[2]
    strain_xy = TIME_STEP * (0.5 * (grad_y[0] + grad_x[1]))
    strain_yz = TIME_STEP * (0.5 * (grad_z[1] + grad_y[2]))
    strain_xz = TIME_STEP * (0.5 * (grad_z[0] + grad_x[2]))
    volume = strain_xx + strain_yy + strain_zz
    vol_third = volume / 3.0
    trial_xx = props[0] + 2.0 * shear_mod * (strain_xx - vol_third) + bulk_mod * volume
    trial_yy = props[1] + 2.0 * shear_mod * (strain_yy - vol_third) + bulk_mod * volume
    trial_zz = props[2] + 2.0 * shear_mod * (strain_zz - vol_third) + bulk_mod * volume
    trial_xy = props[3] + 2.0 * shear_mod * strain_xy
    trial_yz = props[4] + 2.0 * shear_mod * strain_yz
    trial_xz = props[5] + 2.0 * shear_mod * strain_xz
    pressure = (trial_xx + trial_yy + trial_zz) / 3.0
    dev_xx = trial_xx - pressure
    dev_yy = trial_yy - pressure
    dev_zz = trial_zz - pressure
    second = (
        dev_xx * dev_xx
        + dev_yy * dev_yy
        + dev_zz * dev_zz
        + 2.0 * (trial_xy * trial_xy + trial_yz * trial_yz + trial_xz * trial_xz)
    )
    equivalent = jnp.sqrt(1.5 * second)
    flow_stress = yield_eff + FRICTION * jnp.maximum(-pressure, 0.0)
    excess = equivalent - flow_stress
    active = excess > 0.0
    plastic_rate = jnp.maximum(excess, 0.0) / (3.0 * shear_mod + VISCOSITY / TIME_STEP)
    scale_back = jnp.where(
        active, 1.0 - 3.0 * shear_mod * plastic_rate / jnp.where(active, equivalent, 1.0), 1.0
    )
    updated = jnp.stack(
        [
            pressure + scale_back * dev_xx,
            pressure + scale_back * dev_yy,
            pressure + scale_back * dev_zz,
            scale_back * trial_xy,
            scale_back * trial_yz,
            scale_back * trial_xz,
        ]
    )
    heat_local = (
        HEAT_SCALE * TAYLOR_QUINNEY * (equivalent - 3.0 * shear_mod * plastic_rate) * plastic_rate
    )
    return (updated, heat_local)


def node_forces(updated):
    force_x = face_term(updated[0], 0) + face_term(updated[3], 1) + face_term(updated[5], 2)
    force_y = face_term(updated[3], 0) + face_term(updated[1], 1) + face_term(updated[4], 2)
    force_z = face_term(updated[5], 0) + face_term(updated[4], 1) + face_term(updated[2], 2)
    return -0.25 * jnp.stack([force_x, force_y, force_z])


def mechanics(padded, corner_weights_diagonal):
    node_vel = padded[0:3]
    updated, heat_local = element_state(node_vel, padded[3:, :-1, :-1, :-1])
    force = node_forces(updated)
    corner_speed_later = node_vel[:, 1:-1, 1:-1, 1:-1] - TIME_STEP * force / corner_weights_diagonal
    return (corner_speed_later, updated[:, 1:, 1:, 1:], heat_local[1:, 1:, 1:])


def stencil(values, padded, matrix_main_entries):
    beside = padded[2:, 1:-1, 1:-1] + padded[:-2, 1:-1, 1:-1]
    beside = beside + padded[1:-1, 2:, 1:-1] + padded[1:-1, :-2, 1:-1]
    beside = beside + padded[1:-1, 1:-1, 2:] + padded[1:-1, 1:-1, :-2]
    return matrix_main_entries * values - beside


def diffuse_thermal_once(values, matrix_main_entries):
    haloed = extended(values, (("gx", 0), (("gy", "gz"), 1)), 1)
    padded = jnp.pad(haloed, ((0, 0), (0, 0), (1, 1)))
    return stencil(values, padded, matrix_main_entries)


def polynomial_relaxation(
    brick_warmth_prior,
    caloric_capacity_per_timestep,
    plastic_work_heating_rise,
    diffuse_thermal_field,
    inward_cell_flags,
):
    center_value = 0.5 * (UPPER_BOUND + LOWER_BOUND)
    half_width = 0.5 * (UPPER_BOUND - LOWER_BOUND)
    ratio_sig = center_value / half_width
    matrix_main_entries = 6.0 + caloric_capacity_per_timestep
    linear_system_target = (
        caloric_capacity_per_timestep * brick_warmth_prior + plastic_work_heating_rise
    )
    implicit_kelvin_result = brick_warmth_prior
    equation_misfit = (
        linear_system_target - diffuse_thermal_field(implicit_kelvin_result, matrix_main_entries)
    ) * inward_cell_flags
    weight_now = 1.0 / ratio_sig
    search_direction = equation_misfit / center_value
    for sweep_index in range(SWEEPS):
        implicit_kelvin_result = implicit_kelvin_result + search_direction
        if sweep_index + 1 < SWEEPS:
            equation_misfit = (
                equation_misfit - diffuse_thermal_field(search_direction, matrix_main_entries)
            ) * inward_cell_flags
            weight_next = 1.0 / (2.0 * ratio_sig - weight_now)
            search_direction = (
                weight_next * weight_now * search_direction
                + 2.0 * weight_next / half_width * equation_misfit
            )
            weight_now = weight_next
    return implicit_kelvin_result


def body(
    corner_speed_prior,
    brick_stress_tensor_now,
    compact_onset_strength,
    corner_weights_diagonal,
    substance_labels,
    brick_warmth_prior,
    caloric_capacity_per_timestep,
):
    z_index = lax.axis_index("gz")
    local_mat = lax.dynamic_slice_in_dim(substance_labels, z_index * ZB, ZB, 1)
    shear_blk, bulk_blk = moduli(local_mat)
    powder_cells = spread_blocks(local_mat, BS) == 2
    yield_eff = jnp.where(powder_cells, compact_onset_strength, ELASTIC_YIELD)
    stacked = jnp.concatenate(
        [
            corner_speed_prior,
            brick_stress_tensor_now,
            yield_eff[None],
            spread_blocks(shear_blk, BS)[None],
            spread_blocks(bulk_blk, BS)[None],
        ],
        axis=0,
    )
    padded = extended(stacked, (("gx", 1), ("gy", 3), ("gz", 2)), 1)
    corner_speed_later, projected_brick_stress_tensor, heat_local = mechanics(
        padded, corner_weights_diagonal
    )
    moved = lax.all_to_all(heat_local, "gz", split_axis=2, concat_axis=1, tiled=True)
    plastic_work_heating_rise = jnp.transpose(moved, (0, 2, 1))
    diffused_kelvin_field = polynomial_relaxation(
        brick_warmth_prior,
        caloric_capacity_per_timestep,
        plastic_work_heating_rise,
        diffuse_thermal_once,
        1.0,
    )
    return (corner_speed_later, projected_brick_stress_tensor, diffused_kelvin_field)


LANES = 128
VELS = 3
FIELDS = 11
SLOT = 4
RING = 12
PLANES = 14
MAIN = RING * 2 * BS
VMEM_BYTES = 48 * 1024 * 1024


def two_rounds_fit(mesh):
    return mesh.shape["gx"] == 2 and mesh.shape["gy"] == 2 and mesh.shape["gz"] == 8


def by_shape(*args):
    fits = args[0].shape[1:] == (BS, ZB * BS, LANES // 2) and args[5].shape == (BS, BS, LANES)
    return (two_round_body if fits else body)(*args)


def iota(shape, dim):
    return lax.broadcasted_iota(jnp.int32, shape, dim)


def place(q):
    return MAIN + RING * q if q < 5 else 2 * LANES + RING * (q - 5)


NODES = 2 * LANES + 2 * RING


def bulk_of(shear_mod):
    return jnp.where(
        shear_mod == 3.0,
        5.0,
        jnp.where(shear_mod == 2.0, 4.0, jnp.where(shear_mod == 0.0, 0.0, 1.2)),
    )


def own_labels(labels):
    second, press = labels.shape
    rows = ZB * BS
    first = lax.axis_index("gz") * ZB
    pick = iota((rows, press), 1) == first + iota((rows, press), 0) // BS
    spread = iota((second, LANES), 0) == (iota((second, LANES), 1) // BS) % second
    picked = lax.dot_general(
        pick.astype(jnp.float32),
        labels.astype(jnp.float32),
        (((1,), (1,)), ((), ())),
        preferred_element_type=jnp.float32,
    )
    return jnp.dot(picked, spread.astype(jnp.float32), preferred_element_type=jnp.float32)


FACE = (
    [(field, i) for field in range(VELS) for i in range(3)]
    + [(field, i) for field in range(VELS, 10) for i in range(2)]
    + [(10, 0)]
)
FACE_TILES = len(FACE) // 2 * ZB
PLANE = ZB * BS


def slot_at(lane, field, first):
    where = lax.rem(lane + (2 * LANES - SLOT * field) - first, LANES)
    return where < 3


def pack_kernel(
    labels, vel, stress, onset, warmth, capacity,
    wide, shear_out, face, columns, corner, warmth_out, capacity_out,
    own, own_labels_in, sems,
):
    lower_x = lax.axis_index("gx") == 0
    lower_y = lax.axis_index("gy") == 0
    deep = jnp.where(lower_x, BS - 3, 0)
    shallow = jnp.where(lower_x, BS - 2, 0)
    edge = jnp.where(lower_x, BS - 1, 0)
    copies = [
        pltpu.make_async_copy(*pair, sems.at[n])
        for n, pair in enumerate(
            (
                (labels, own_labels_in),
                (vel, own.at[pl.ds(0, VELS)]),
                (onset, own.at[9]),
                (stress, own.at[pl.ds(VELS, 6)]),
                (warmth.at[pl.ds(deep, 3)], face.at[pl.ds(FACE_TILES, 3)]),
                (capacity.at[edge], face.at[FACE_TILES + 3]),
                (warmth, warmth_out),
                (capacity, capacity_out),
            )
        )
    ]
    for copy in copies:
        copy.start()
    lane = iota((PLANE, LANES), 1)
    half = LANES // 2
    copies[0].wait()
    material = own_labels(own_labels_in[0])
    shear_mod = jnp.where(material == 0.0, 3.0, jnp.where(material == 1.0, 2.0, 0.8))
    shear_out[...] = shear_mod
    copies[1].wait()
    copies[2].wait()
    for field in range(VELS):
        wide[pl.ds(field * BS * PLANE, BS * PLANE), 0:half] = own[field].reshape(BS * PLANE, half)
    powder = material[:, 0:half] == 2.0
    for x in range(BS):
        at = pl.ds((9 * BS + x) * PLANE, PLANE)
        wide[at, 0:half] = jnp.where(powder, own[9, x], ELASTIC_YIELD)
    def read(field, x):
        if field == 10:
            return shear_mod
        return wide[pl.ds(pl.multiple_of((field * BS + x) * PLANE, PLANE), PLANE), :]

    first = jnp.where(lower_y, half - 3, 0)
    insides = [slot_at(lane, field, first) for field in range(FIELDS)]

    def pack_columns(fields, x, packed):
        for field in fields:
            turned = read(field, x)
            if field:
                turned = pltpu.roll(turned, SLOT * field, 1)
            packed = jnp.where(insides[field], turned, packed)
        columns[x] = packed

    for x in range(BS):
        pack_columns((0, 1, 2, 9, 10), x, jnp.zeros((PLANE, LANES), jnp.float32))
    copies[3].wait()
    for field in range(VELS, 9):
        wide[pl.ds(field * BS * PLANE, BS * PLANE), 0:half] = own[field].reshape(BS * PLANE, half)
    for pair in range(len(FACE) // 2):
        one, two = (
            read(field, (deep if field < VELS else shallow) + i)
            for field, i in FACE[2 * pair : 2 * pair + 2]
        )
        joined = jnp.where(lane < half, one, pltpu.roll(two, half, 1))
        face[2 * pair] = joined[:BS]
        face[2 * pair + 1] = joined[BS:]
    for x in range(BS):
        pack_columns(range(VELS, 9), x, columns[x])
    for i in range(3):
        corner[i] = columns[deep + i]
    for copy in copies[4:]:
        copy.wait()


def warmth_plane(j, warmth, face):
    upper_x = lax.axis_index("gx") == 1
    if j < 3:
        return jnp.where(upper_x, face[FACE_TILES + j], 0.0)
    if j < 11:
        return warmth[j - 3]
    return jnp.where(upper_x, 0.0, face[FACE_TILES + j - 11])


def capacity_plane(j, capacity, face):
    upper_x = lax.axis_index("gx") == 1
    if 3 <= j < 11:
        return capacity[j - 3]
    if j == 2 or j == 11:
        return jnp.where(upper_x == (j == 2), face[FACE_TILES + 3], 0.0)
    return jnp.zeros((BS, LANES), jnp.float32)


def stress_terms(shear_mod):
    bulk_mod = bulk_of(shear_mod)
    return (
        0.5 * TIME_STEP * shear_mod,
        0.25 * TIME_STEP * (bulk_mod - 2.0 / 3.0 * shear_mod),
        3.0 * shear_mod,
        1.0 / (3.0 * shear_mod + VISCOSITY / TIME_STEP),
    )


def strained(before, grads, terms):
    twice, volume_term = terms[0], terms[1]
    volume = volume_term * (grads[0] + grads[1] + grads[2])
    return [
        before[k] + twice * grads[k] + (volume if k < 3 else 0.0) for k in range(6)
    ]


def returned(trial, yield_eff, terms):
    shear_thrice, slope = terms[2], terms[3]
    pressure = (trial[0] + trial[1] + trial[2]) * (1.0 / 3.0)
    dev = [trial[k] - pressure for k in range(3)]
    second = (
        dev[0] * dev[0]
        + dev[1] * dev[1]
        + dev[2] * dev[2]
        + 2.0 * (trial[3] * trial[3] + trial[4] * trial[4] + trial[5] * trial[5])
    )
    equivalent = jnp.sqrt(1.5 * second)
    excess = equivalent - (yield_eff + FRICTION * jnp.maximum(-pressure, 0.0))
    active = excess > 0.0
    rate = jnp.maximum(excess, 0.0) * slope
    drop = shear_thrice * rate
    scale = jnp.where(active, 1.0 - drop / jnp.where(active, equivalent, 1.0), 1.0)
    heat = HEAT_SCALE * TAYLOR_QUINNEY * (equivalent - drop) * rate
    updated = [pressure + scale * dev[k] for k in range(3)] + [
        scale * trial[k] for k in range(3, 6)
    ]
    return updated, heat


def six(gx, gp, gs):
    return [
        gx[0],
        gp[1],
        gs[2],
        0.5 * (gp[0] + gx[1]),
        0.5 * (gs[1] + gp[2]),
        0.5 * (gs[0] + gx[2]),
    ]


LAYERS = 14


def block_of(a):
    return 0 if a < 2 else 1 if a < 10 else 2


def layers(ext, shears, first, end):
    rows = PLANE
    row = iota((rows, LANES), 0)

    def read(field, j):
        return ext[pl.ds((field * LAYERS + j) * rows, rows), :]

    def node_terms(j):
        terms = []
        for c in range(VELS):
            here = read(c, j)
            above = jnp.where(row == rows - 1, 0.0, pltpu.roll(here, rows - 1, 0))
            total, change = here + above, above - here
            aside = pltpu.roll(total, LANES - 1, 1)
            terms.append((total + aside, aside - total, change + pltpu.roll(change, LANES - 1, 1)))
        return terms

    materials = [stress_terms(plane) for plane in shears]
    before = node_terms(first + 1)
    for a in range(first, end):
        after = node_terms(a + 2)
        grads = six(
            [after[c][0] - before[c][0] for c in range(VELS)],
            [after[c][2] + before[c][2] for c in range(VELS)],
            [after[c][1] + before[c][1] for c in range(VELS)],
        )
        material = materials[block_of(a)]
        trial = strained([read(VELS + k, a + 1) for k in range(6)], grads, material)
        yield (a, *returned(trial, read(9, a + 1), material))
        before = after


RIM_PAIRS = RING // 2
RIM_ROWS = RIM_PAIRS * BS


def rim_kernel(warmth, capacity, face, rim_out, twin_out):
    even = lax.rem(lax.axis_index("gz"), 2) == 0
    sub = iota((BS, LANES), 0)
    ups, downs = [], []
    for j in range(1, RING + 1):
        u = warmth_plane(j, warmth, face)
        c = capacity_plane(j, capacity, face)
        ups.append(jnp.where(sub > 4, u, pltpu.roll(c, 5, 0)))
        downs.append(jnp.where(sub < 3, u, pltpu.roll(c, 3, 0)))
    for m in range(RIM_PAIRS):
        at = pl.ds(m * BS, BS)
        up = jnp.where(sub < 4, pltpu.roll(ups[2 * m], 4, 0), ups[2 * m + 1])
        down = jnp.where(sub < 4, downs[2 * m], pltpu.roll(downs[2 * m + 1], 4, 0))
        rim_out[at, :] = jnp.where(even, down, up)
        twin_out[at, :] = jnp.where(even, up, down)


def heat_kernel(
    wide, shear, rim, rim_twin, face, columns, corner,
    chunks_out, even_out, odd_out, ext, shears_out, partial_out,
    stacked, chunks, sem,
):
    upper_x = lax.axis_index("gx") == 1
    upper_y = lax.axis_index("gy") == 1
    even = lax.rem(lax.axis_index("gz"), 2) == 0
    rows = PLANE
    half = LANES // 2
    lane = iota((rows, LANES), 1)
    first = jnp.where(upper_y, LANES - 3, half)
    beside = (lane >= first) & (lane < first + 3)
    faces = {key: at for at, key in enumerate(FACE)}

    def joined(field, plane, side):
        side = pltpu.roll(side, (half - SLOT * field) % LANES, 1)
        return jnp.where(lane < half, plane, jnp.where(beside, side, 0.0))

    def far(field, i, side):
        at = faces[field, i]
        pair = at // 2
        plane = jnp.concatenate([face[2 * pair], face[2 * pair + 1]], axis=0)
        return joined(field, pltpu.roll(plane, half, 1) if at % 2 else plane, side)

    def layer(field, j):
        if 3 <= j < 11:
            at = (field * BS + j - 3) * rows
            return joined(field, wide[pl.ds(at, rows), :], columns[j - 3])
        side = corner[j] if j < 3 else corner[j - 11]
        i = j - 11 if j >= 11 else j if field < VELS else j - 1
        plane = far(field, i, side)
        return jnp.where(upper_x, plane, 0.0) if j < 3 else jnp.where(upper_x, 0.0, plane)

    for field in range(10):
        for j in range(1, LAYERS if field < VELS else LAYERS - 1):
            ext[pl.ds((field * LAYERS + j) * rows, rows), :] = layer(field, j)
    outer = far(10, 0, corner[1])
    shears = [
        jnp.where(upper_x, outer, 0.0),
        joined(10, shear[...], columns[0]),
        jnp.where(upper_x, 0.0, outer),
    ]
    for block in range(3):
        shears_out[block] = shears[block]

    row = iota((rows, LANES), 0)

    def across(field, press):
        at = (field * LAYERS + 1) * rows + press
        return ext[pl.ds(at, rows, stride=rows), :]

    def parts(press, sign):
        terms = []
        for c in range(VELS):
            here = across(c, press)
            aside = pltpu.roll(here, LANES - 1, 1)
            total, change = here + aside, aside - here
            nxt = pltpu.roll(total, rows - 1, 0)
            both = nxt + total
            terms.append((nxt - total, sign * both, change + pltpu.roll(change, rows - 1, 0)))
        return six(*[[terms[c][d] for c in range(VELS)] for d in range(3)])

    last = rows - 1
    shear_row = [shears[block][last:, :] for block in range(3)]
    shear_mod = jnp.where(row < 2, shear_row[0], jnp.where(row < 10, shear_row[1], shear_row[2]))
    trial = strained(
        [across(VELS + k, last) for k in range(6)], parts(last, -1.0), stress_terms(shear_mod)
    )
    for q, plane in enumerate(trial + [across(9, last), shear_mod]):
        partial_out[q] = plane
    for k, plane in enumerate(parts(0, 1.0)):
        partial_out[8 + k] = plane

    sub = iota((BS, LANES), 0)
    for q in range(7):
        stacked[pl.ds(place(q), RING), :] = partial_out[q, pl.ds(0, RING), :]
    for c in range(VELS):
        stacked[pl.ds(NODES + (RING + 1) * c, RING + 1), :] = across(c, 0)[: RING + 1]

    for a, updated, heat in layers(ext, shears, 0, RING):
        shear_mod = shears[block_of(a)]
        stacked[pl.ds(a * rows, rows), :] = jnp.where(row == rows - 1, shear_mod, heat)
    turned = jnp.transpose(stacked[...])
    for g in range(chunks.shape[0]):
        here, after, before = (
            turned[at % LANES : at % LANES + BS, :] for at in (g * BS, g * BS + BS, g * BS - BS)
        )
        for t in range(2):
            chunks[g, pl.ds(t * BS, BS), :] = here[:, t * LANES : (t + 1) * LANES]
        sides = [
            jnp.where(
                sub < 4,
                after[:, t * LANES : (t + 1) * LANES],
                before[:, t * LANES : (t + 1) * LANES],
            )
            for t in range(3)
        ]
        inner = jnp.where(sub < 4, pltpu.roll(sides[1], 2, 0), pltpu.roll(sides[1], 6, 0))
        chunks[g, pl.ds(2 * BS, BS), :] = jnp.where((sub < 2) | (sub > 5), sides[0], inner)
        chunks[g, pl.ds(3 * BS, BS), :] = jnp.where(
            lane[:BS] < half, here[:, 2 * LANES :], pltpu.roll(sides[2], half, 1)
        )
    copy = pltpu.make_async_copy(chunks, chunks_out, sem)
    copy.start()

    def fill(up_ref, down_ref):
        for q in range(8):
            up_ref[pl.ds(RIM_ROWS + NEAR * q, NEAR), :] = partial_out[q, pl.ds(1, NEAR), :]
        for k in range(6):
            down_ref[pl.ds(RIM_ROWS + NEAR * k, NEAR), :] = partial_out[8 + k, pl.ds(1, NEAR), :]
        for ref, count in ((up_ref, 8), (down_ref, 6)):
            rest = EDGE_ALL - RIM_ROWS - NEAR * count
            ref[pl.ds(EDGE_ALL - rest, rest), :] = jnp.zeros((rest, LANES), jnp.float32)
        even_out[pl.ds(0, RIM_ROWS), :] = rim_twin[...]
        odd_out[pl.ds(0, RIM_ROWS), :] = rim[...]

    @pl.when(even)
    def _():
        fill(even_out, odd_out)

    @pl.when(jnp.logical_not(even))
    def _():
        fill(odd_out, even_out)

    copy.wait()


NEAR = BS + 1
EDGE_ALL = RIM_ROWS + 8 * NEAR + BS


def corrected(planes, sign):
    rows = PLANE
    total, change, press = [], [], []
    for plane in planes:
        aside = pltpu.roll(plane, 1, 1)
        total.append(plane + aside)
        change.append(plane - aside)
        press.append(sign * (plane + aside))
    forces = []
    for kx, kp, ks in FORCE_TERMS:
        both = press[kp] + change[ks]
        forces.append(
            total[kx] - pltpu.roll(total[kx], 1, 0) + both + pltpu.roll(both, 1, 0)
        )
    return forces


FORCE_TERMS = ((0, 3, 5), (3, 1, 4), (5, 4, 2))


def gather_kernel(chunks, heats_out):
    groups = lax.axis_size("gz")
    rows = PLANE
    lane = iota((rows, LANES), 1)
    group = lane // rows
    sub = iota((BS, LANES), 0)

    sources = [[], [], []]
    for g in range(groups):
        tiles = [chunks[g, pl.ds(t * BS, BS), :] for t in range(4)]
        inner = jnp.where(sub < 4, pltpu.roll(tiles[2], 6, 0), pltpu.roll(tiles[2], 2, 0))
        outer = pltpu.roll(tiles[3], LANES // 2, 1)
        for t, pair in enumerate(((tiles[0], tiles[2]), (tiles[1], inner), (tiles[3], outer))):
            sources[t].append(jnp.concatenate(pair, axis=0))

    heats = []
    for t, count in ((0, 8), (1, 4)):
        turned = []
        for k in range(groups):
            mixed = sources[t][k]
            for b in range(1, count):
                mixed = jnp.where(group == b, sources[t][(b + k) % groups], mixed)
            turned.append(pltpu.roll(mixed, k * rows, 1) if k else mixed)
        for b in range(count):
            heat = turned[(0 - b) % groups]
            for g in range(1, groups):
                heat = jnp.where(group == g, turned[(g - b) % groups], heat)
            heats.append(heat)

    def spread(position, width, first):
        tile, at = divmod(position, LANES)
        plane = jnp.zeros((rows, LANES), jnp.float32)
        for g in range(first, groups):
            to = (g - first) * rows
            inside = (lane >= to) & (lane < to + width)
            plane = jnp.where(inside, pltpu.roll(sources[tile][g], (to - at) % LANES, 1), plane)
        return plane

    place_in = lane % rows
    trial = [spread(place(k), RING, 0) for k in range(6)]
    yield_eff = spread(place(6), RING, 0)
    shear_mod = jnp.zeros((rows, LANES), jnp.float32)
    for a in range(RING):
        turned = pltpu.roll(heats[a], (a - rows + 1) % LANES, 1)
        shear_mod = jnp.where(place_in == a, turned, shear_mod)
    gx, gp, gs = [], [], []
    for c in range(VELS):
        here = spread(NODES + (RING + 1) * c, RING + 1, 1)
        aside = pltpu.roll(here, rows - 1, 0)
        total, change = here + aside, aside - here
        nxt = pltpu.roll(total, LANES - 1, 1)
        gx.append(nxt - total)
        gp.append(nxt + total)
        gs.append(change + pltpu.roll(change, LANES - 1, 1))
    terms = stress_terms(shear_mod)
    seam = returned(strained(trial, six(gx, gp, gs), terms), yield_eff, terms)[1]
    for a in range(RING):
        heats_out[a] = jnp.where(
            place_in == rows - 1, pltpu.roll(seam, rows - 1 - a, 1), heats[a]
        )


def force_kernel(ext, shears, vel, mass, base_out, updated_out):
    rows = PLANE
    row = iota((rows, LANES), 0)
    for a, updated, _ in layers(ext, [shears[block] for block in range(3)], 1, 10):
        for k in range(6):
            updated_out[k, a - 1] = updated[k]

    def element_terms(j):
        terms = []
        for k in range(6):
            here = jnp.where(row == rows - 1, 0.0, updated_out[k, j])
            prev = pltpu.roll(here, 1, 0)
            total, change = here + prev, here - prev
            aside = pltpu.roll(total, 1, 1)
            terms.append((total + aside, total - aside, change + pltpu.roll(change, 1, 1)))
        return terms

    before = element_terms(0)
    for x in range(BS):
        after = element_terms(x + 1)
        weights = 0.25 * TIME_STEP / mass[x]
        for c, (kx, kp, ks) in enumerate(FORCE_TERMS):
            force = (
                (after[kx][0] - before[kx][0])
                + (after[kp][2] + before[kp][2])
                + (after[ks][1] + before[ks][1])
            )
            base_out[c, x] = vel[c, x] + force[:, : LANES // 2] * weights
        before = after


def finish_kernel(
    heats, base, updated, partial, mass, warmth, capacity, face, odd_in, even_in,
    vel_hbm, stress_hbm, out_hbm,
    vel_out, stress_out, out, top, low_force, high_force, sems,
):
    upper_x = lax.axis_index("gx") == 1
    at_z = lax.axis_index("gz")
    even = lax.rem(at_z, 2) == 0
    groups = lax.axis_size("gz")
    rows = PLANE
    half = LANES // 2
    at_flat = lax.axis_index("gy") * groups + at_z
    last = lax.axis_size("gy") * groups - 1
    has_above = at_z < groups - 1
    has_below = at_z > 0
    lane = iota((rows, LANES), 1)
    row = iota((rows, LANES), 0)
    sub = iota((BS, LANES), 0)

    def below_plane(q):
        at = pl.ds(RIM_ROWS + NEAR * q - 1, rows)
        return jnp.where(has_below, jnp.where(even, odd_in[at, :], even_in[at, :]), 0.0)

    def above_plane(k):
        at = pl.ds(RIM_ROWS + NEAR * k - 1, rows)
        return jnp.where(has_above, jnp.where(even, even_in[at, :], odd_in[at, :]), 0.0)

    terms = stress_terms(partial[7])
    trial = strained([partial[k] for k in range(6)], [above_plane(k) for k in range(6)], terms)
    uppermost = returned(trial, partial[6], terms)[0]
    for k, plane in enumerate(uppermost):
        top[k] = plane
    for c, plane in enumerate(corrected(uppermost, 1.0)):
        high_force[c] = plane
    terms = stress_terms(below_plane(7))
    trial = strained([below_plane(k) for k in range(6)], [partial[8 + k] for k in range(6)], terms)
    for c, plane in enumerate(corrected(returned(trial, below_plane(6), terms)[0], -1.0)):
        low_force[c] = plane
    for x in range(BS):
        at = pl.ds(x + 2, 1)
        weights = 0.25 * TIME_STEP / mass[x]
        for k in range(6):
            plane = jnp.where(row == rows - 1, top[k, at, :], updated[k, x + 1])
            stress_out[k, x] = plane[:, :half]
        for c in range(VELS):
            force = jnp.where(
                row == 0, low_force[c, at, :], jnp.where(row == rows - 1, high_force[c, at, :], 0.0)
            )
            vel_out[c, x] = base[c, x] + force[:, :half] * weights
    copies = [
        pltpu.make_async_copy(*pair, sems.at[n])
        for n, pair in enumerate(((vel_out, vel_hbm), (stress_out, stress_hbm), (out, out_hbm)))
    ]
    copies[0].start()
    copies[1].start()

    above, below = at_flat < last, at_flat > 0
    u_rows = (row < BS) | ((row < BS + 3) & above) | ((row >= rows - 3) & below)
    d_rows = (row < BS) | ((row < BS + 2) & above) | ((row >= rows - 2) & below)
    us, caps = [], []
    for j in range(14):
        at = pl.ds(min(max(j - 1, 0), RING - 1) // 2 * BS, BS)
        low = jnp.where(even, odd_in[at, :], even_in[at, :])
        high = jnp.where(even, even_in[at, :], odd_in[at, :])
        if j % 2:
            low = pltpu.roll(low, 4, 0)
        else:
            high = pltpu.roll(high, 4, 0)
        side = jnp.where(sub < 4, high, low)
        u = jnp.concatenate([warmth_plane(j, warmth, face), side], axis=0)
        us.append(jnp.where(u_rows, u, 0.0))
        side = jnp.where(sub < 4, pltpu.roll(high, 5, 0), pltpu.roll(low, 3, 0))
        caps.append(6.0 + jnp.concatenate([capacity_plane(j, capacity, face), side], axis=0))

    def around(fields, a):
        here = fields[a]
        total = fields[a - 1] + fields[a + 1]
        total = total + pltpu.roll(here, 1, 0) + pltpu.roll(here, rows - 1, 0)
        total = total + jnp.where(lane == 0, 0.0, pltpu.roll(here, 1, 1))
        return total + jnp.where(lane == LANES - 1, 0.0, pltpu.roll(here, LANES - 1, 1))

    def inside(a):
        if a < 2:
            return d_rows & upper_x
        if a >= 10:
            return d_rows & jnp.logical_not(upper_x)
        return d_rows

    theta = 0.5 * (UPPER_BOUND + LOWER_BOUND)
    half_width = 0.5 * (UPPER_BOUND - LOWER_BOUND)
    sig = theta / half_width
    weight_now = 1.0 / sig
    misfit, step, total = {}, {}, {}
    for a in range(RING):
        misfit[a] = heats[a] - 6.0 * us[a + 1] + around(us, a + 1)
        step[a] = jnp.where(inside(a), misfit[a] * (1.0 / theta), 0.0)
        total[a] = us[a + 1] + step[a]
    for sweep in range(1, SWEEPS):
        weight_next = 1.0 / (2.0 * sig - weight_now)
        new_misfit, new_step = {}, {}
        for a in range(sweep, RING - sweep):
            new_misfit[a] = misfit[a] - caps[a + 1] * step[a] + around(step, a)
            moved = (weight_next * weight_now) * step[a] + (
                2.0 * weight_next / half_width
            ) * new_misfit[a]
            new_step[a] = jnp.where(inside(a), moved, 0.0)
            total[a] = total[a] + new_step[a]
        misfit, step, weight_now = new_misfit, new_step, weight_next
    for x in range(BS):
        out[x] = total[x + 2][:BS]
    copies[2].start()
    for copy in copies:
        copy.wait()


def f32(*shape):
    return jax.ShapeDtypeStruct(shape, jnp.float32)


def call(kernel, out_shape, *args, scratch=(), far_in=False, far_out=0):
    moved = 4 * sum(a.size for a in args) + 4 * sum(o.size for o in jax.tree.leaves(out_shape))
    hbm, vmem = (pl.BlockSpec(memory_space=space) for space in (pltpu.HBM, pltpu.VMEM))
    return pl.pallas_call(
        kernel,
        out_shape=out_shape,
        in_specs=[hbm if far_in else vmem] * len(args),
        out_specs=tuple(hbm if n < far_out else vmem for n in range(len(out_shape))),
        scratch_shapes=scratch,
        compiler_params=pltpu.CompilerParams(vmem_limit_bytes=VMEM_BYTES),
        cost_estimate=pl.CostEstimate(flops=0, bytes_accessed=moved, transcendentals=0),
    )(*args)


def room(*shape):
    return pltpu.VMEM(shape, jnp.float32)


def paired(count, first):
    pairs = []
    for i in range(first, count - 1, 2):
        pairs += [(i, i + 1), (i + 1, i)]
    return pairs


def two_round_body(
    corner_speed_prior,
    brick_stress_tensor_now,
    compact_onset_strength,
    corner_weights_diagonal,
    substance_labels,
    brick_warmth_prior,
    caloric_capacity_per_timestep,
):
    rows = PLANE
    groups = lax.axis_size("gz")
    chain = groups * lax.axis_size("gy")
    labels = jnp.transpose(substance_labels, (0, 2, 1))
    raw = (
        labels,
        corner_speed_prior,
        brick_stress_tensor_now,
        compact_onset_strength,
        brick_warmth_prior,
        caloric_capacity_per_timestep,
    )
    raw = [pltpu.with_memory_space_constraint(array, pltpu.HBM) for array in raw]
    second = compact_onset_strength.shape[-1]
    wide, shear, face, columns, corner, warmth, capacity = call(
        pack_kernel,
        (
            f32(10 * BS * rows, LANES),
            f32(rows, LANES),
            f32(FACE_TILES + 4, BS, LANES),
            f32(BS, rows, LANES),
            f32(3, rows, LANES),
            f32(*brick_warmth_prior.shape),
            f32(*brick_warmth_prior.shape),
        ),
        *raw,
        far_in=True,
        scratch=(
            room(10, BS, rows, second),
            pltpu.VMEM(labels.shape, jnp.int32),
            pltpu.SemaphoreType.DMA((len(raw) + 2,)),
        ),
    )
    face = lax.ppermute(face, "gx", [(0, 1), (1, 0)])
    columns = lax.ppermute(columns, "gy", [(0, 1), (1, 0)])
    corner = lax.ppermute(corner, ("gx", "gy"), [(0, 3), (3, 0), (1, 2), (2, 1)])
    rim, twin = call(
        rim_kernel, (f32(RIM_ROWS, LANES), f32(RIM_ROWS, LANES)), warmth, capacity, face
    )
    chunks, even, odd, ext, shears, partial = call(
        heat_kernel,
        (
            f32(groups, 4 * BS, LANES),
            f32(EDGE_ALL, LANES),
            f32(EDGE_ALL, LANES),
            f32((10 * LAYERS + 3) * rows, LANES),
            f32(3, rows, LANES),
            f32(PLANES, rows, LANES),
        ),
        wide,
        shear,
        rim,
        twin,
        face,
        columns,
        corner,
        scratch=(
            room(3 * LANES, LANES),
            room(groups, 4 * BS, LANES),
            pltpu.SemaphoreType.DMA,
        ),
        far_out=1,
    )
    chunks = lax.all_to_all(chunks, "gz", split_axis=0, concat_axis=0, tiled=True)
    odd = lax.ppermute(odd, ("gy", "gz"), paired(chain, 1))
    even = lax.ppermute(even, "gz", paired(groups, 0))
    base, updated = call(
        force_kernel,
        (f32(*corner_speed_prior.shape), f32(6, BS + 1, rows, LANES)),
        ext,
        shears,
        corner_speed_prior,
        corner_weights_diagonal,
    )
    (heats,) = call(gather_kernel, (f32(RING, rows, LANES),), chunks)
    odd, even, heats, base = lax.optimization_barrier((odd, even, heats, base))
    results = (corner_speed_prior.shape, brick_stress_tensor_now.shape, brick_warmth_prior.shape)
    return call(
        finish_kernel,
        tuple(f32(*shape) for shape in results),
        heats,
        base,
        updated,
        partial,
        corner_weights_diagonal,
        warmth,
        capacity,
        face,
        odd,
        even,
        scratch=(
            *[room(*shape) for shape in results],
            room(6, rows, LANES),
            room(VELS, rows, LANES),
            room(VELS, rows, LANES),
            pltpu.SemaphoreType.DMA((3,)),
        ),
        far_out=3,
    )


def solution(mesh):
    placed = (
        P(None, "gx", "gz", "gy"),
        P(None, "gx", "gz", "gy"),
        P("gx", "gz", "gy"),
        P("gx", "gz", "gy"),
        P("gx", None, "gy"),
        P("gx", ("gy", "gz"), None),
        P("gx", ("gy", "gz"), None),
    )
    return jax.shard_map(
        by_shape if two_rounds_fit(mesh) else body,
        mesh=mesh,
        in_specs=placed,
        out_specs=(
            P(None, "gx", "gz", "gy"),
            P(None, "gx", "gz", "gy"),
            P("gx", ("gy", "gz"), None),
        ),
        check_vma=False,
    )
```

```python
import jax
import jax.numpy as jnp
from jax import lax
from jax.experimental import pallas as pl
from jax.experimental.pallas import tpu as pltpu
from jax.sharding import PartitionSpec as P

BS = 8
ZB = 2
SWEEPS = 3


TIME_STEP = 0.2
VISCOSITY = 0.4
FRICTION = 0.5
TAYLOR_QUINNEY = 0.9
HEAT_SCALE = 5.0
ELASTIC_YIELD = 10000.0
LOWER_BOUND = 0.5
UPPER_BOUND = 16.0


def extended(cells, sides, width):
    for axis, dim in sides:
        count = lax.axis_size(axis)
        ends = count - 1
        head = lax.slice_in_dim(cells, 0, width, axis=dim)
        tail = lax.slice_in_dim(cells, cells.shape[dim] - width, cells.shape[dim], axis=dim)
        cells = jnp.concatenate(
            [
                lax.ppermute(tail, axis, [(i, (i + 1) % count) for i in range(ends)]),
                cells,
                lax.ppermute(head, axis, [((i + 1) % count, i) for i in range(ends)]),
            ],
            axis=dim,
        )
    return cells


def shifted_diff(values, axis_num):
    extent = values.shape[axis_num]
    return lax.slice_in_dim(values, 1, extent, axis=axis_num) - lax.slice_in_dim(
        values, 0, extent - 1, axis=axis_num
    )


def shifted_sum(values, axis_num):
    extent = values.shape[axis_num]
    return lax.slice_in_dim(values, 1, extent, axis=axis_num) + lax.slice_in_dim(
        values, 0, extent - 1, axis=axis_num
    )


def spread_blocks(values, width):
    extent_a, extent_b, extent_c = values.shape
    wide = jnp.broadcast_to(
        values[:, None, :, None, :, None], (extent_a, width, extent_b, width, extent_c, width)
    )
    return wide.reshape(extent_a * width, extent_b * width, extent_c * width)


def moduli(substance_labels):
    shear_mod = jnp.where(
        substance_labels == 0, 3.0, jnp.where(substance_labels == 1, 2.0, 0.8)
    ).astype(jnp.float32)
    bulk_mod = jnp.where(
        substance_labels == 0, 5.0, jnp.where(substance_labels == 1, 4.0, 1.2)
    ).astype(jnp.float32)
    return (shear_mod, bulk_mod)


def face_term(element_values, axis_num):
    others = [other for other in (0, 1, 2) if other != axis_num]
    return shifted_diff(shifted_sum(shifted_sum(element_values, others[0]), others[1]), axis_num)


def element_state(node_vel, props):
    grad_x = 0.25 * shifted_diff(shifted_sum(shifted_sum(node_vel, 2), 3), 1)
    grad_y = 0.25 * shifted_diff(shifted_sum(shifted_sum(node_vel, 1), 3), 2)
    grad_z = 0.25 * shifted_diff(shifted_sum(shifted_sum(node_vel, 1), 2), 3)
    yield_eff = props[6]
    shear_mod = props[7]
    bulk_mod = props[8]
    strain_xx = TIME_STEP * grad_x[0]
    strain_yy = TIME_STEP * grad_y[1]
    strain_zz = TIME_STEP * grad_z[2]
    strain_xy = TIME_STEP * (0.5 * (grad_y[0] + grad_x[1]))
    strain_yz = TIME_STEP * (0.5 * (grad_z[1] + grad_y[2]))
    strain_xz = TIME_STEP * (0.5 * (grad_z[0] + grad_x[2]))
    volume = strain_xx + strain_yy + strain_zz
    vol_third = volume / 3.0
    trial_xx = props[0] + 2.0 * shear_mod * (strain_xx - vol_third) + bulk_mod * volume
    trial_yy = props[1] + 2.0 * shear_mod * (strain_yy - vol_third) + bulk_mod * volume
    trial_zz = props[2] + 2.0 * shear_mod * (strain_zz - vol_third) + bulk_mod * volume
    trial_xy = props[3] + 2.0 * shear_mod * strain_xy
    trial_yz = props[4] + 2.0 * shear_mod * strain_yz
    trial_xz = props[5] + 2.0 * shear_mod * strain_xz
    pressure = (trial_xx + trial_yy + trial_zz) / 3.0
    dev_xx = trial_xx - pressure
    dev_yy = trial_yy - pressure
    dev_zz = trial_zz - pressure
    second = (
        dev_xx * dev_xx
        + dev_yy * dev_yy
        + dev_zz * dev_zz
        + 2.0 * (trial_xy * trial_xy + trial_yz * trial_yz + trial_xz * trial_xz)
    )
    equivalent = jnp.sqrt(1.5 * second)
    flow_stress = yield_eff + FRICTION * jnp.maximum(-pressure, 0.0)
    excess = equivalent - flow_stress
    active = excess > 0.0
    plastic_rate = jnp.maximum(excess, 0.0) / (3.0 * shear_mod + VISCOSITY / TIME_STEP)
    scale_back = jnp.where(
        active, 1.0 - 3.0 * shear_mod * plastic_rate / jnp.where(active, equivalent, 1.0), 1.0
    )
    updated = jnp.stack(
        [
            pressure + scale_back * dev_xx,
            pressure + scale_back * dev_yy,
            pressure + scale_back * dev_zz,
            scale_back * trial_xy,
            scale_back * trial_yz,
            scale_back * trial_xz,
        ]
    )
    heat_local = (
        HEAT_SCALE * TAYLOR_QUINNEY * (equivalent - 3.0 * shear_mod * plastic_rate) * plastic_rate
    )
    return (updated, heat_local)


def node_forces(updated):
    force_x = face_term(updated[0], 0) + face_term(updated[3], 1) + face_term(updated[5], 2)
    force_y = face_term(updated[3], 0) + face_term(updated[1], 1) + face_term(updated[4], 2)
    force_z = face_term(updated[5], 0) + face_term(updated[4], 1) + face_term(updated[2], 2)
    return -0.25 * jnp.stack([force_x, force_y, force_z])


def mechanics(padded, corner_weights_diagonal):
    node_vel = padded[0:3]
    updated, heat_local = element_state(node_vel, padded[3:, :-1, :-1, :-1])
    force = node_forces(updated)
    corner_speed_later = node_vel[:, 1:-1, 1:-1, 1:-1] - TIME_STEP * force / corner_weights_diagonal
    return (corner_speed_later, updated[:, 1:, 1:, 1:], heat_local[1:, 1:, 1:])


def stencil(values, padded, matrix_main_entries):
    beside = padded[2:, 1:-1, 1:-1] + padded[:-2, 1:-1, 1:-1]
    beside = beside + padded[1:-1, 2:, 1:-1] + padded[1:-1, :-2, 1:-1]
    beside = beside + padded[1:-1, 1:-1, 2:] + padded[1:-1, 1:-1, :-2]
    return matrix_main_entries * values - beside


def diffuse_thermal_once(values, matrix_main_entries):
    haloed = extended(values, (("gx", 0), (("gy", "gz"), 1)), 1)
    padded = jnp.pad(haloed, ((0, 0), (0, 0), (1, 1)))
    return stencil(values, padded, matrix_main_entries)


def polynomial_relaxation(
    brick_warmth_prior,
    caloric_capacity_per_timestep,
    plastic_work_heating_rise,
    diffuse_thermal_field,
    inward_cell_flags,
):
    center_value = 0.5 * (UPPER_BOUND + LOWER_BOUND)
    half_width = 0.5 * (UPPER_BOUND - LOWER_BOUND)
    ratio_sig = center_value / half_width
    matrix_main_entries = 6.0 + caloric_capacity_per_timestep
    linear_system_target = (
        caloric_capacity_per_timestep * brick_warmth_prior + plastic_work_heating_rise
    )
    implicit_kelvin_result = brick_warmth_prior
    equation_misfit = (
        linear_system_target - diffuse_thermal_field(implicit_kelvin_result, matrix_main_entries)
    ) * inward_cell_flags
    weight_now = 1.0 / ratio_sig
    search_direction = equation_misfit / center_value
    for sweep_index in range(SWEEPS):
        implicit_kelvin_result = implicit_kelvin_result + search_direction
        if sweep_index + 1 < SWEEPS:
            equation_misfit = (
                equation_misfit - diffuse_thermal_field(search_direction, matrix_main_entries)
            ) * inward_cell_flags
            weight_next = 1.0 / (2.0 * ratio_sig - weight_now)
            search_direction = (
                weight_next * weight_now * search_direction
                + 2.0 * weight_next / half_width * equation_misfit
            )
            weight_now = weight_next
    return implicit_kelvin_result


def body(
    corner_speed_prior,
    brick_stress_tensor_now,
    compact_onset_strength,
    corner_weights_diagonal,
    substance_labels,
    brick_warmth_prior,
    caloric_capacity_per_timestep,
):
    z_index = lax.axis_index("gz")
    local_mat = lax.dynamic_slice_in_dim(substance_labels, z_index * ZB, ZB, 1)
    shear_blk, bulk_blk = moduli(local_mat)
    powder_cells = spread_blocks(local_mat, BS) == 2
    yield_eff = jnp.where(powder_cells, compact_onset_strength, ELASTIC_YIELD)
    stacked = jnp.concatenate(
        [
            corner_speed_prior,
            brick_stress_tensor_now,
            yield_eff[None],
            spread_blocks(shear_blk, BS)[None],
            spread_blocks(bulk_blk, BS)[None],
        ],
        axis=0,
    )
    padded = extended(stacked, (("gx", 1), ("gy", 3), ("gz", 2)), 1)
    corner_speed_later, projected_brick_stress_tensor, heat_local = mechanics(
        padded, corner_weights_diagonal
    )
    moved = lax.all_to_all(heat_local, "gz", split_axis=2, concat_axis=1, tiled=True)
    plastic_work_heating_rise = jnp.transpose(moved, (0, 2, 1))
    diffused_kelvin_field = polynomial_relaxation(
        brick_warmth_prior,
        caloric_capacity_per_timestep,
        plastic_work_heating_rise,
        diffuse_thermal_once,
        1.0,
    )
    return (corner_speed_later, projected_brick_stress_tensor, diffused_kelvin_field)


LANES = 128
VELS = 3
FIELDS = 11
SLOT = 4
RING = 12
PLANES = 14
MAIN = RING * 2 * BS
VMEM_BYTES = 48 * 1024 * 1024


def two_rounds_fit(mesh):
    return mesh.shape["gx"] == 2 and mesh.shape["gy"] == 2 and mesh.shape["gz"] == 8


def by_shape(*args):
    fits = args[0].shape[1:] == (BS, ZB * BS, LANES // 2) and args[5].shape == (BS, BS, LANES)
    return (two_round_body if fits else body)(*args)


def iota(shape, dim):
    return lax.broadcasted_iota(jnp.int32, shape, dim)


def place(q):
    return MAIN + RING * q if q < 5 else 2 * LANES + RING * (q - 5)


NODES = 2 * LANES + 2 * RING


def bulk_of(shear_mod):
    return jnp.where(
        shear_mod == 3.0,
        5.0,
        jnp.where(shear_mod == 2.0, 4.0, jnp.where(shear_mod == 0.0, 0.0, 1.2)),
    )


def own_labels(labels):
    second, press = labels.shape
    rows = ZB * BS
    first = lax.axis_index("gz") * ZB
    pick = iota((rows, press), 1) == first + iota((rows, press), 0) // BS
    spread = iota((second, LANES), 0) == (iota((second, LANES), 1) // BS) % second
    picked = lax.dot_general(
        pick.astype(jnp.float32),
        labels.astype(jnp.float32),
        (((1,), (1,)), ((), ())),
        preferred_element_type=jnp.float32,
    )
    return jnp.dot(picked, spread.astype(jnp.float32), preferred_element_type=jnp.float32)


FACE = (
    [(field, i) for field in range(VELS) for i in range(3)]
    + [(field, i) for field in range(VELS, 10) for i in range(2)]
    + [(10, 0)]
)
FACE_TILES = len(FACE) // 2 * ZB
PLANE = ZB * BS


def slot_at(lane, field, first):
    where = lax.rem(lane + (2 * LANES - SLOT * field) - first, LANES)
    return where < 3


def pack_kernel(
    labels, vel, stress, onset, warmth, capacity,
    wide, shear_out, face, columns, corner, warmth_out, capacity_out,
    own, own_labels_in, sems,
):
    lower_x = lax.axis_index("gx") == 0
    lower_y = lax.axis_index("gy") == 0
    deep = jnp.where(lower_x, BS - 3, 0)
    shallow = jnp.where(lower_x, BS - 2, 0)
    edge = jnp.where(lower_x, BS - 1, 0)
    copies = [
        pltpu.make_async_copy(*pair, sems.at[n])
        for n, pair in enumerate(
            (
                (labels, own_labels_in),
                (vel, own.at[pl.ds(0, VELS)]),
                (onset, own.at[9]),
                (stress, own.at[pl.ds(VELS, 6)]),
                (warmth.at[pl.ds(deep, 3)], face.at[pl.ds(FACE_TILES, 3)]),
                (capacity.at[edge], face.at[FACE_TILES + 3]),
                (warmth, warmth_out),
                (capacity, capacity_out),
            )
        )
    ]
    for copy in copies:
        copy.start()
    lane = iota((PLANE, LANES), 1)
    half = LANES // 2
    copies[0].wait()
    material = own_labels(own_labels_in[0])
    shear_mod = jnp.where(material == 0.0, 3.0, jnp.where(material == 1.0, 2.0, 0.8))
    shear_out[...] = shear_mod
    copies[1].wait()
    copies[2].wait()
    for field in range(VELS):
        wide[pl.ds(field * BS * PLANE, BS * PLANE), 0:half] = own[field].reshape(BS * PLANE, half)
    powder = material[:, 0:half] == 2.0
    for x in range(BS):
        at = pl.ds((9 * BS + x) * PLANE, PLANE)
        wide[at, 0:half] = jnp.where(powder, own[9, x], ELASTIC_YIELD)
    def read(field, x):
        if field == 10:
            return shear_mod
        return wide[pl.ds(pl.multiple_of((field * BS + x) * PLANE, PLANE), PLANE), :]

    first = jnp.where(lower_y, half - 3, 0)
    insides = [slot_at(lane, field, first) for field in range(FIELDS)]

    def pack_columns(fields, x, packed):
        for field in fields:
            turned = read(field, x)
            if field:
                turned = pltpu.roll(turned, SLOT * field, 1)
            packed = jnp.where(insides[field], turned, packed)
        columns[x] = packed

    for x in range(BS):
        pack_columns((0, 1, 2, 9, 10), x, jnp.zeros((PLANE, LANES), jnp.float32))
    copies[3].wait()
    for field in range(VELS, 9):
        wide[pl.ds(field * BS * PLANE, BS * PLANE), 0:half] = own[field].reshape(BS * PLANE, half)
    for pair in range(len(FACE) // 2):
        one, two = (
            read(field, (deep if field < VELS else shallow) + i)
            for field, i in FACE[2 * pair : 2 * pair + 2]
        )
        joined = jnp.where(lane < half, one, pltpu.roll(two, half, 1))
        face[2 * pair] = joined[:BS]
        face[2 * pair + 1] = joined[BS:]
    for x in range(BS):
        pack_columns(range(VELS, 9), x, columns[x])
    for i in range(3):
        corner[i] = columns[deep + i]
    for copy in copies[4:]:
        copy.wait()


def warmth_plane(j, warmth, face):
    upper_x = lax.axis_index("gx") == 1
    if j < 3:
        return jnp.where(upper_x, face[FACE_TILES + j], 0.0)
    if j < 11:
        return warmth[j - 3]
    return jnp.where(upper_x, 0.0, face[FACE_TILES + j - 11])


def capacity_plane(j, capacity, face):
    upper_x = lax.axis_index("gx") == 1
    if 3 <= j < 11:
        return capacity[j - 3]
    if j == 2 or j == 11:
        return jnp.where(upper_x == (j == 2), face[FACE_TILES + 3], 0.0)
    return jnp.zeros((BS, LANES), jnp.float32)


def stress_terms(shear_mod):
    bulk_mod = bulk_of(shear_mod)
    return (
        0.5 * TIME_STEP * shear_mod,
        0.25 * TIME_STEP * (bulk_mod - 2.0 / 3.0 * shear_mod),
        3.0 * shear_mod,
        1.0 / (3.0 * shear_mod + VISCOSITY / TIME_STEP),
    )


def strained(before, grads, terms):
    twice, volume_term = terms[0], terms[1]
    volume = volume_term * (grads[0] + grads[1] + grads[2])
    return [
        before[k] + twice * grads[k] + (volume if k < 3 else 0.0) for k in range(6)
    ]


def returned(trial, yield_eff, terms):
    shear_thrice, slope = terms[2], terms[3]
    pressure = (trial[0] + trial[1] + trial[2]) * (1.0 / 3.0)
    dev = [trial[k] - pressure for k in range(3)]
    second = (
        dev[0] * dev[0]
        + dev[1] * dev[1]
        + dev[2] * dev[2]
        + 2.0 * (trial[3] * trial[3] + trial[4] * trial[4] + trial[5] * trial[5])
    )
    equivalent = jnp.sqrt(1.5 * second)
    excess = equivalent - (yield_eff + FRICTION * jnp.maximum(-pressure, 0.0))
    active = excess > 0.0
    rate = jnp.maximum(excess, 0.0) * slope
    drop = shear_thrice * rate
    scale = jnp.where(active, 1.0 - drop / jnp.where(active, equivalent, 1.0), 1.0)
    heat = HEAT_SCALE * TAYLOR_QUINNEY * (equivalent - drop) * rate
    updated = [pressure + scale * dev[k] for k in range(3)] + [
        scale * trial[k] for k in range(3, 6)
    ]
    return updated, heat


def six(gx, gp, gs):
    return [
        gx[0],
        gp[1],
        gs[2],
        0.5 * (gp[0] + gx[1]),
        0.5 * (gs[1] + gp[2]),
        0.5 * (gs[0] + gx[2]),
    ]


LAYERS = 14


def block_of(a):
    return 0 if a < 2 else 1 if a < 10 else 2


def layers(ext, shears, first, end):
    rows = PLANE
    row = iota((rows, LANES), 0)

    def read(field, j):
        return ext[pl.ds((field * LAYERS + j) * rows, rows), :]

    def node_terms(j):
        terms = []
        for c in range(VELS):
            here = read(c, j)
            above = jnp.where(row == rows - 1, 0.0, pltpu.roll(here, rows - 1, 0))
            total, change = here + above, above - here
            aside = pltpu.roll(total, LANES - 1, 1)
            terms.append((total + aside, aside - total, change + pltpu.roll(change, LANES - 1, 1)))
        return terms

    materials = [stress_terms(plane) for plane in shears]
    before = node_terms(first + 1)
    for a in range(first, end):
        after = node_terms(a + 2)
        grads = six(
            [after[c][0] - before[c][0] for c in range(VELS)],
            [after[c][2] + before[c][2] for c in range(VELS)],
            [after[c][1] + before[c][1] for c in range(VELS)],
        )
        material = materials[block_of(a)]
        trial = strained([read(VELS + k, a + 1) for k in range(6)], grads, material)
        yield (a, *returned(trial, read(9, a + 1), material))
        before = after


RIM_PAIRS = RING // 2
RIM_ROWS = RIM_PAIRS * BS


def rim_kernel(warmth, capacity, face, rim_out, twin_out):
    even = lax.rem(lax.axis_index("gz"), 2) == 0
    sub = iota((BS, LANES), 0)
    ups, downs = [], []
    for j in range(1, RING + 1):
        u = warmth_plane(j, warmth, face)
        c = capacity_plane(j, capacity, face)
        ups.append(jnp.where(sub > 4, u, pltpu.roll(c, 5, 0)))
        downs.append(jnp.where(sub < 3, u, pltpu.roll(c, 3, 0)))
    for m in range(RIM_PAIRS):
        at = pl.ds(m * BS, BS)
        up = jnp.where(sub < 4, pltpu.roll(ups[2 * m], 4, 0), ups[2 * m + 1])
        down = jnp.where(sub < 4, downs[2 * m], pltpu.roll(downs[2 * m + 1], 4, 0))
        rim_out[at, :] = jnp.where(even, down, up)
        twin_out[at, :] = jnp.where(even, up, down)


def heat_kernel(
    wide, shear, rim, rim_twin, face, columns, corner,
    chunks_out, even_out, odd_out, ext, shears_out, partial_out,
    stacked, chunks, sem,
):
    upper_x = lax.axis_index("gx") == 1
    upper_y = lax.axis_index("gy") == 1
    even = lax.rem(lax.axis_index("gz"), 2) == 0
    rows = PLANE
    half = LANES // 2
    lane = iota((rows, LANES), 1)
    first = jnp.where(upper_y, LANES - 3, half)
    beside = (lane >= first) & (lane < first + 3)
    faces = {key: at for at, key in enumerate(FACE)}

    def joined(field, plane, side):
        side = pltpu.roll(side, (half - SLOT * field) % LANES, 1)
        return jnp.where(lane < half, plane, jnp.where(beside, side, 0.0))

    def far(field, i, side):
        at = faces[field, i]
        pair = at // 2
        plane = jnp.concatenate([face[2 * pair], face[2 * pair + 1]], axis=0)
        return joined(field, pltpu.roll(plane, half, 1) if at % 2 else plane, side)

    def layer(field, j):
        if 3 <= j < 11:
            at = (field * BS + j - 3) * rows
            return joined(field, wide[pl.ds(at, rows), :], columns[j - 3])
        side = corner[j] if j < 3 else corner[j - 11]
        i = j - 11 if j >= 11 else j if field < VELS else j - 1
        plane = far(field, i, side)
        return jnp.where(upper_x, plane, 0.0) if j < 3 else jnp.where(upper_x, 0.0, plane)

    for field in range(10):
        for j in range(1, LAYERS if field < VELS else LAYERS - 1):
            ext[pl.ds((field * LAYERS + j) * rows, rows), :] = layer(field, j)
    outer = far(10, 0, corner[1])
    shears = [
        jnp.where(upper_x, outer, 0.0),
        joined(10, shear[...], columns[0]),
        jnp.where(upper_x, 0.0, outer),
    ]
    for block in range(3):
        shears_out[block] = shears[block]

    row = iota((rows, LANES), 0)

    def across(field, press):
        at = (field * LAYERS + 1) * rows + press
        return ext[pl.ds(at, rows, stride=rows), :]

    def parts(press, sign):
        terms = []
        for c in range(VELS):
            here = across(c, press)
            aside = pltpu.roll(here, LANES - 1, 1)
            total, change = here + aside, aside - here
            nxt = pltpu.roll(total, rows - 1, 0)
            both = nxt + total
            terms.append((nxt - total, sign * both, change + pltpu.roll(change, rows - 1, 0)))
        return six(*[[terms[c][d] for c in range(VELS)] for d in range(3)])

    last = rows - 1
    shear_row = [shears[block][last:, :] for block in range(3)]
    shear_mod = jnp.where(row < 2, shear_row[0], jnp.where(row < 10, shear_row[1], shear_row[2]))
    trial = strained(
        [across(VELS + k, last) for k in range(6)], parts(last, -1.0), stress_terms(shear_mod)
    )
    for q, plane in enumerate(trial + [across(9, last), shear_mod]):
        partial_out[q] = plane
    for k, plane in enumerate(parts(0, 1.0)):
        partial_out[8 + k] = plane

    sub = iota((BS, LANES), 0)
    for q in range(7):
        stacked[pl.ds(place(q), RING), :] = partial_out[q, pl.ds(0, RING), :]
    for c in range(VELS):
        stacked[pl.ds(NODES + (RING + 1) * c, RING + 1), :] = across(c, 0)[: RING + 1]

    for a, updated, heat in layers(ext, shears, 0, RING):
        shear_mod = shears[block_of(a)]
        stacked[pl.ds(a * rows, rows), :] = jnp.where(row == rows - 1, shear_mod, heat)
    turned = jnp.transpose(stacked[...])
    for g in range(chunks.shape[0]):
        here, after, before = (
            turned[at % LANES : at % LANES + BS, :] for at in (g * BS, g * BS + BS, g * BS - BS)
        )
        for t in range(2):
            chunks[g, pl.ds(t * BS, BS), :] = here[:, t * LANES : (t + 1) * LANES]
        sides = [
            jnp.where(
                sub < 4,
                after[:, t * LANES : (t + 1) * LANES],
                before[:, t * LANES : (t + 1) * LANES],
            )
            for t in range(3)
        ]
        inner = jnp.where(sub < 4, pltpu.roll(sides[1], 2, 0), pltpu.roll(sides[1], 6, 0))
        chunks[g, pl.ds(2 * BS, BS), :] = jnp.where((sub < 2) | (sub > 5), sides[0], inner)
        chunks[g, pl.ds(3 * BS, BS), :] = jnp.where(
            lane[:BS] < half, here[:, 2 * LANES :], pltpu.roll(sides[2], half, 1)
        )
    copy = pltpu.make_async_copy(chunks, chunks_out, sem)
    copy.start()

    def fill(up_ref, down_ref):
        for q in range(8):
            up_ref[pl.ds(RIM_ROWS + NEAR * q, NEAR), :] = partial_out[q, pl.ds(1, NEAR), :]
        for k in range(6):
            down_ref[pl.ds(RIM_ROWS + NEAR * k, NEAR), :] = partial_out[8 + k, pl.ds(1, NEAR), :]
        for ref, count in ((up_ref, 8), (down_ref, 6)):
            rest = EDGE_ALL - RIM_ROWS - NEAR * count
            ref[pl.ds(EDGE_ALL - rest, rest), :] = jnp.zeros((rest, LANES), jnp.float32)
        even_out[pl.ds(0, RIM_ROWS), :] = rim_twin[...]
        odd_out[pl.ds(0, RIM_ROWS), :] = rim[...]

    @pl.when(even)
    def _():
        fill(even_out, odd_out)

    @pl.when(jnp.logical_not(even))
    def _():
        fill(odd_out, even_out)

    copy.wait()


NEAR = BS + 1
EDGE_ALL = RIM_ROWS + 8 * NEAR + BS


def corrected(planes, sign):
    rows = PLANE
    total, change, press = [], [], []
    for plane in planes:
        aside = pltpu.roll(plane, 1, 1)
        total.append(plane + aside)
        change.append(plane - aside)
        press.append(sign * (plane + aside))
    forces = []
    for kx, kp, ks in FORCE_TERMS:
        both = press[kp] + change[ks]
        forces.append(
            total[kx] - pltpu.roll(total[kx], 1, 0) + both + pltpu.roll(both, 1, 0)
        )
    return forces


FORCE_TERMS = ((0, 3, 5), (3, 1, 4), (5, 4, 2))


def gather_kernel(chunks, heats_out):
    groups = lax.axis_size("gz")
    rows = PLANE
    lane = iota((rows, LANES), 1)
    group = lane // rows
    sub = iota((BS, LANES), 0)

    sources = [[], [], []]
    for g in range(groups):
        tiles = [chunks[g, pl.ds(t * BS, BS), :] for t in range(4)]
        inner = jnp.where(sub < 4, pltpu.roll(tiles[2], 6, 0), pltpu.roll(tiles[2], 2, 0))
        outer = pltpu.roll(tiles[3], LANES // 2, 1)
        for t, pair in enumerate(((tiles[0], tiles[2]), (tiles[1], inner), (tiles[3], outer))):
            sources[t].append(jnp.concatenate(pair, axis=0))

    heats = []
    for t, count in ((0, 8), (1, 4)):
        turned = []
        for k in range(groups):
            mixed = sources[t][k]
            for b in range(1, count):
                mixed = jnp.where(group == b, sources[t][(b + k) % groups], mixed)
            turned.append(pltpu.roll(mixed, k * rows, 1) if k else mixed)
        for b in range(count):
            heat = turned[(0 - b) % groups]
            for g in range(1, groups):
                heat = jnp.where(group == g, turned[(g - b) % groups], heat)
            heats.append(heat)

    def spread(position, width, first):
        tile, at = divmod(position, LANES)
        plane = jnp.zeros((rows, LANES), jnp.float32)
        for g in range(first, groups):
            to = (g - first) * rows
            inside = (lane >= to) & (lane < to + width)
            plane = jnp.where(inside, pltpu.roll(sources[tile][g], (to - at) % LANES, 1), plane)
        return plane

    place_in = lane % rows
    trial = [spread(place(k), RING, 0) for k in range(6)]
    yield_eff = spread(place(6), RING, 0)
    shear_mod = jnp.zeros((rows, LANES), jnp.float32)
    for a in range(RING):
        turned = pltpu.roll(heats[a], (a - rows + 1) % LANES, 1)
        shear_mod = jnp.where(place_in == a, turned, shear_mod)
    gx, gp, gs = [], [], []
    for c in range(VELS):
        here = spread(NODES + (RING + 1) * c, RING + 1, 1)
        aside = pltpu.roll(here, rows - 1, 0)
        total, change = here + aside, aside - here
        nxt = pltpu.roll(total, LANES - 1, 1)
        gx.append(nxt - total)
        gp.append(nxt + total)
        gs.append(change + pltpu.roll(change, LANES - 1, 1))
    terms = stress_terms(shear_mod)
    seam = returned(strained(trial, six(gx, gp, gs), terms), yield_eff, terms)[1]
    for a in range(RING):
        heats_out[a] = jnp.where(
            place_in == rows - 1, pltpu.roll(seam, rows - 1 - a, 1), heats[a]
        )


def force_kernel(ext, shears, vel, mass, stress_hbm, base_out, updated_out, low, sem):
    rows = PLANE
    row = iota((rows, LANES), 0)
    for a, updated, _ in layers(ext, [shears[block] for block in range(3)], 1, 10):
        for k in range(6):
            updated_out[k, a - 1] = updated[k]
            if a > 1:
                low[k, a - 2] = updated[k][:BS, : LANES // 2]
    copy = pltpu.make_async_copy(low, stress_hbm.at[:, :, pl.ds(0, BS), :], sem)
    copy.start()

    def element_terms(j):
        terms = []
        for k in range(6):
            here = jnp.where(row == rows - 1, 0.0, updated_out[k, j])
            prev = pltpu.roll(here, 1, 0)
            total, change = here + prev, here - prev
            aside = pltpu.roll(total, 1, 1)
            terms.append((total + aside, total - aside, change + pltpu.roll(change, 1, 1)))
        return terms

    before = element_terms(0)
    for x in range(BS):
        after = element_terms(x + 1)
        weights = 0.25 * TIME_STEP / mass[x]
        for c, (kx, kp, ks) in enumerate(FORCE_TERMS):
            force = (
                (after[kx][0] - before[kx][0])
                + (after[kp][2] + before[kp][2])
                + (after[ks][1] + before[ks][1])
            )
            base_out[c, x] = vel[c, x] + force[:, : LANES // 2] * weights
        before = after
    copy.wait()


def finish_kernel(
    heats, base, updated, partial, mass, warmth, capacity, face, odd_in, even_in, _,
    vel_hbm, stress_hbm, out_hbm,
    vel_out, stress_out, out, top, low_force, high_force, sems,
):
    upper_x = lax.axis_index("gx") == 1
    at_z = lax.axis_index("gz")
    even = lax.rem(at_z, 2) == 0
    groups = lax.axis_size("gz")
    rows = PLANE
    half = LANES // 2
    at_flat = lax.axis_index("gy") * groups + at_z
    last = lax.axis_size("gy") * groups - 1
    has_above = at_z < groups - 1
    has_below = at_z > 0
    lane = iota((rows, LANES), 1)
    row = iota((rows, LANES), 0)
    sub = iota((BS, LANES), 0)

    def below_plane(q):
        at = pl.ds(RIM_ROWS + NEAR * q - 1, rows)
        return jnp.where(has_below, jnp.where(even, odd_in[at, :], even_in[at, :]), 0.0)

    def above_plane(k):
        at = pl.ds(RIM_ROWS + NEAR * k - 1, rows)
        return jnp.where(has_above, jnp.where(even, even_in[at, :], odd_in[at, :]), 0.0)

    terms = stress_terms(partial[7])
    trial = strained([partial[k] for k in range(6)], [above_plane(k) for k in range(6)], terms)
    uppermost = returned(trial, partial[6], terms)[0]
    for k, plane in enumerate(uppermost):
        top[k] = plane
    for c, plane in enumerate(corrected(uppermost, 1.0)):
        high_force[c] = plane
    terms = stress_terms(below_plane(7))
    trial = strained([below_plane(k) for k in range(6)], [partial[8 + k] for k in range(6)], terms)
    for c, plane in enumerate(corrected(returned(trial, below_plane(6), terms)[0], -1.0)):
        low_force[c] = plane
    for x in range(BS):
        at = pl.ds(x + 2, 1)
        weights = 0.25 * TIME_STEP / mass[x]
        for k in range(6):
            plane = jnp.where(sub == BS - 1, top[k, at, :], updated[k, x + 1][BS:])
            stress_out[k, x] = plane[:, :half]
        for c in range(VELS):
            force = jnp.where(
                row == 0, low_force[c, at, :], jnp.where(row == rows - 1, high_force[c, at, :], 0.0)
            )
            vel_out[c, x] = base[c, x] + force[:, :half] * weights
    copies = [
        pltpu.make_async_copy(*pair, sems.at[n])
        for n, pair in enumerate((
                (vel_out, vel_hbm),
                (stress_out, stress_hbm.at[:, :, pl.ds(BS, BS), :]),
                (out, out_hbm),
            ))
    ]
    copies[0].start()
    copies[1].start()

    above, below = at_flat < last, at_flat > 0
    u_rows = (row < BS) | ((row < BS + 3) & above) | ((row >= rows - 3) & below)
    d_rows = (row < BS) | ((row < BS + 2) & above) | ((row >= rows - 2) & below)
    us, caps = [], []
    for j in range(14):
        at = pl.ds(min(max(j - 1, 0), RING - 1) // 2 * BS, BS)
        low = jnp.where(even, odd_in[at, :], even_in[at, :])
        high = jnp.where(even, even_in[at, :], odd_in[at, :])
        if j % 2:
            low = pltpu.roll(low, 4, 0)
        else:
            high = pltpu.roll(high, 4, 0)
        side = jnp.where(sub < 4, high, low)
        u = jnp.concatenate([warmth_plane(j, warmth, face), side], axis=0)
        us.append(jnp.where(u_rows, u, 0.0))
        side = jnp.where(sub < 4, pltpu.roll(high, 5, 0), pltpu.roll(low, 3, 0))
        caps.append(6.0 + jnp.concatenate([capacity_plane(j, capacity, face), side], axis=0))

    def around(fields, a):
        here = fields[a]
        total = fields[a - 1] + fields[a + 1]
        total = total + pltpu.roll(here, 1, 0) + pltpu.roll(here, rows - 1, 0)
        total = total + jnp.where(lane == 0, 0.0, pltpu.roll(here, 1, 1))
        return total + jnp.where(lane == LANES - 1, 0.0, pltpu.roll(here, LANES - 1, 1))

    def inside(a):
        if a < 2:
            return d_rows & upper_x
        if a >= 10:
            return d_rows & jnp.logical_not(upper_x)
        return d_rows

    theta = 0.5 * (UPPER_BOUND + LOWER_BOUND)
    half_width = 0.5 * (UPPER_BOUND - LOWER_BOUND)
    sig = theta / half_width
    weight_now = 1.0 / sig
    misfit, step, total = {}, {}, {}
    for a in range(RING):
        misfit[a] = heats[a] - 6.0 * us[a + 1] + around(us, a + 1)
        step[a] = jnp.where(inside(a), misfit[a] * (1.0 / theta), 0.0)
        total[a] = us[a + 1] + step[a]
    for sweep in range(1, SWEEPS):
        weight_next = 1.0 / (2.0 * sig - weight_now)
        new_misfit, new_step = {}, {}
        for a in range(sweep, RING - sweep):
            new_misfit[a] = misfit[a] - caps[a + 1] * step[a] + around(step, a)
            moved = (weight_next * weight_now) * step[a] + (
                2.0 * weight_next / half_width
            ) * new_misfit[a]
            new_step[a] = jnp.where(inside(a), moved, 0.0)
            total[a] = total[a] + new_step[a]
        misfit, step, weight_now = new_misfit, new_step, weight_next
    for x in range(BS):
        out[x] = total[x + 2][:BS]
    copies[2].start()
    for copy in copies:
        copy.wait()


def f32(*shape):
    return jax.ShapeDtypeStruct(shape, jnp.float32)


def call(kernel, out_shape, *args, scratch=(), far_in=False, far_out=0, onto=None):
    moved = 4 * sum(a.size for a in args) + 4 * sum(o.size for o in jax.tree.leaves(out_shape))
    hbm, vmem = (pl.BlockSpec(memory_space=space) for space in (pltpu.HBM, pltpu.VMEM))
    return pl.pallas_call(
        kernel,
        out_shape=out_shape,
        in_specs=[hbm if far_in or n == onto else vmem for n in range(len(args))],
        input_output_aliases={} if onto is None else {onto: 1},
        out_specs=tuple(hbm if n < far_out else vmem for n in range(len(out_shape))),
        scratch_shapes=scratch,
        compiler_params=pltpu.CompilerParams(vmem_limit_bytes=VMEM_BYTES),
        cost_estimate=pl.CostEstimate(flops=0, bytes_accessed=moved, transcendentals=0),
    )(*args)


def room(*shape):
    return pltpu.VMEM(shape, jnp.float32)


def paired(count, first):
    pairs = []
    for i in range(first, count - 1, 2):
        pairs += [(i, i + 1), (i + 1, i)]
    return pairs


def two_round_body(
    corner_speed_prior,
    brick_stress_tensor_now,
    compact_onset_strength,
    corner_weights_diagonal,
    substance_labels,
    brick_warmth_prior,
    caloric_capacity_per_timestep,
):
    rows = PLANE
    groups = lax.axis_size("gz")
    chain = groups * lax.axis_size("gy")
    labels = jnp.transpose(substance_labels, (0, 2, 1))
    raw = (
        labels,
        corner_speed_prior,
        brick_stress_tensor_now,
        compact_onset_strength,
        brick_warmth_prior,
        caloric_capacity_per_timestep,
    )
    raw = [pltpu.with_memory_space_constraint(array, pltpu.HBM) for array in raw]
    second = compact_onset_strength.shape[-1]
    wide, shear, face, columns, corner, warmth, capacity = call(
        pack_kernel,
        (
            f32(10 * BS * rows, LANES),
            f32(rows, LANES),
            f32(FACE_TILES + 4, BS, LANES),
            f32(BS, rows, LANES),
            f32(3, rows, LANES),
            f32(*brick_warmth_prior.shape),
            f32(*brick_warmth_prior.shape),
        ),
        *raw,
        far_in=True,
        scratch=(
            room(10, BS, rows, second),
            pltpu.VMEM(labels.shape, jnp.int32),
            pltpu.SemaphoreType.DMA((len(raw) + 2,)),
        ),
    )
    face = lax.ppermute(face, "gx", [(0, 1), (1, 0)])
    columns = lax.ppermute(columns, "gy", [(0, 1), (1, 0)])
    corner = lax.ppermute(corner, ("gx", "gy"), [(0, 3), (3, 0), (1, 2), (2, 1)])
    rim, twin = call(
        rim_kernel, (f32(RIM_ROWS, LANES), f32(RIM_ROWS, LANES)), warmth, capacity, face
    )
    chunks, even, odd, ext, shears, partial = call(
        heat_kernel,
        (
            f32(groups, 4 * BS, LANES),
            f32(EDGE_ALL, LANES),
            f32(EDGE_ALL, LANES),
            f32((10 * LAYERS + 3) * rows, LANES),
            f32(3, rows, LANES),
            f32(PLANES, rows, LANES),
        ),
        wide,
        shear,
        rim,
        twin,
        face,
        columns,
        corner,
        scratch=(
            room(3 * LANES, LANES),
            room(groups, 4 * BS, LANES),
            pltpu.SemaphoreType.DMA,
        ),
        far_out=1,
    )
    chunks = lax.all_to_all(chunks, "gz", split_axis=0, concat_axis=0, tiled=True)
    odd = lax.ppermute(odd, ("gy", "gz"), paired(chain, 1))
    even = lax.ppermute(even, "gz", paired(groups, 0))
    stress, base, updated = call(
        force_kernel,
        (f32(*brick_stress_tensor_now.shape), f32(*corner_speed_prior.shape), f32(6, BS + 1, rows, LANES)),
        ext,
        shears,
        corner_speed_prior,
        corner_weights_diagonal,
        scratch=(room(6, BS, BS, second), pltpu.SemaphoreType.DMA),
        far_out=1,
    )
    (heats,) = call(gather_kernel, (f32(RING, rows, LANES),), chunks)
    odd, even, heats, base = lax.optimization_barrier((odd, even, heats, base))
    results = (corner_speed_prior.shape, brick_stress_tensor_now.shape, brick_warmth_prior.shape)
    return call(
        finish_kernel,
        tuple(f32(*shape) for shape in results),
        heats,
        base,
        updated,
        partial,
        corner_weights_diagonal,
        warmth,
        capacity,
        face,
        odd,
        even,
        stress,
        onto=10,
        scratch=(
            room(*results[0]),
            room(6, BS, BS, second),
            room(*results[2]),
            room(6, rows, LANES),
            room(VELS, rows, LANES),
            room(VELS, rows, LANES),
            pltpu.SemaphoreType.DMA((3,)),
        ),
        far_out=3,
    )


def solution(mesh):
    placed = (
        P(None, "gx", "gz", "gy"),
        P(None, "gx", "gz", "gy"),
        P("gx", "gz", "gy"),
        P("gx", "gz", "gy"),
        P("gx", None, "gy"),
        P("gx", ("gy", "gz"), None),
        P("gx", ("gy", "gz"), None),
    )
    return jax.shard_map(
        by_shape if two_rounds_fit(mesh) else body,
        mesh=mesh,
        in_specs=placed,
        out_specs=(
            P(None, "gx", "gz", "gy"),
            P(None, "gx", "gz", "gy"),
            P("gx", ("gy", "gz"), None),
        ),
        check_vma=False,
    )
```

```python
import jax
import jax.numpy as jnp
from jax import lax
from jax.experimental import pallas as pl
from jax.experimental.pallas import tpu as pltpu
from jax.sharding import PartitionSpec as P

BS = 8
ZB = 2
SWEEPS = 3


TIME_STEP = 0.2
VISCOSITY = 0.4
FRICTION = 0.5
TAYLOR_QUINNEY = 0.9
HEAT_SCALE = 5.0
ELASTIC_YIELD = 10000.0
LOWER_BOUND = 0.5
UPPER_BOUND = 16.0


def extended(cells, sides, width):
    for axis, dim in sides:
        count = lax.axis_size(axis)
        ends = count - 1
        head = lax.slice_in_dim(cells, 0, width, axis=dim)
        tail = lax.slice_in_dim(cells, cells.shape[dim] - width, cells.shape[dim], axis=dim)
        cells = jnp.concatenate(
            [
                lax.ppermute(tail, axis, [(i, (i + 1) % count) for i in range(ends)]),
                cells,
                lax.ppermute(head, axis, [((i + 1) % count, i) for i in range(ends)]),
            ],
            axis=dim,
        )
    return cells


def shifted_diff(values, axis_num):
    extent = values.shape[axis_num]
    return lax.slice_in_dim(values, 1, extent, axis=axis_num) - lax.slice_in_dim(
        values, 0, extent - 1, axis=axis_num
    )


def shifted_sum(values, axis_num):
    extent = values.shape[axis_num]
    return lax.slice_in_dim(values, 1, extent, axis=axis_num) + lax.slice_in_dim(
        values, 0, extent - 1, axis=axis_num
    )


def spread_blocks(values, width):
    extent_a, extent_b, extent_c = values.shape
    wide = jnp.broadcast_to(
        values[:, None, :, None, :, None], (extent_a, width, extent_b, width, extent_c, width)
    )
    return wide.reshape(extent_a * width, extent_b * width, extent_c * width)


def moduli(substance_labels):
    shear_mod = jnp.where(
        substance_labels == 0, 3.0, jnp.where(substance_labels == 1, 2.0, 0.8)
    ).astype(jnp.float32)
    bulk_mod = jnp.where(
        substance_labels == 0, 5.0, jnp.where(substance_labels == 1, 4.0, 1.2)
    ).astype(jnp.float32)
    return (shear_mod, bulk_mod)


def face_term(element_values, axis_num):
    others = [other for other in (0, 1, 2) if other != axis_num]
    return shifted_diff(shifted_sum(shifted_sum(element_values, others[0]), others[1]), axis_num)


def element_state(node_vel, props):
    grad_x = 0.25 * shifted_diff(shifted_sum(shifted_sum(node_vel, 2), 3), 1)
    grad_y = 0.25 * shifted_diff(shifted_sum(shifted_sum(node_vel, 1), 3), 2)
    grad_z = 0.25 * shifted_diff(shifted_sum(shifted_sum(node_vel, 1), 2), 3)
    yield_eff = props[6]
    shear_mod = props[7]
    bulk_mod = props[8]
    strain_xx = TIME_STEP * grad_x[0]
    strain_yy = TIME_STEP * grad_y[1]
    strain_zz = TIME_STEP * grad_z[2]
    strain_xy = TIME_STEP * (0.5 * (grad_y[0] + grad_x[1]))
    strain_yz = TIME_STEP * (0.5 * (grad_z[1] + grad_y[2]))
    strain_xz = TIME_STEP * (0.5 * (grad_z[0] + grad_x[2]))
    volume = strain_xx + strain_yy + strain_zz
    vol_third = volume / 3.0
    trial_xx = props[0] + 2.0 * shear_mod * (strain_xx - vol_third) + bulk_mod * volume
    trial_yy = props[1] + 2.0 * shear_mod * (strain_yy - vol_third) + bulk_mod * volume
    trial_zz = props[2] + 2.0 * shear_mod * (strain_zz - vol_third) + bulk_mod * volume
    trial_xy = props[3] + 2.0 * shear_mod * strain_xy
    trial_yz = props[4] + 2.0 * shear_mod * strain_yz
    trial_xz = props[5] + 2.0 * shear_mod * strain_xz
    pressure = (trial_xx + trial_yy + trial_zz) / 3.0
    dev_xx = trial_xx - pressure
    dev_yy = trial_yy - pressure
    dev_zz = trial_zz - pressure
    second = (
        dev_xx * dev_xx
        + dev_yy * dev_yy
        + dev_zz * dev_zz
        + 2.0 * (trial_xy * trial_xy + trial_yz * trial_yz + trial_xz * trial_xz)
    )
    equivalent = jnp.sqrt(1.5 * second)
    flow_stress = yield_eff + FRICTION * jnp.maximum(-pressure, 0.0)
    excess = equivalent - flow_stress
    active = excess > 0.0
    plastic_rate = jnp.maximum(excess, 0.0) / (3.0 * shear_mod + VISCOSITY / TIME_STEP)
    scale_back = jnp.where(
        active, 1.0 - 3.0 * shear_mod * plastic_rate / jnp.where(active, equivalent, 1.0), 1.0
    )
    updated = jnp.stack(
        [
            pressure + scale_back * dev_xx,
            pressure + scale_back * dev_yy,
            pressure + scale_back * dev_zz,
            scale_back * trial_xy,
            scale_back * trial_yz,
            scale_back * trial_xz,
        ]
    )
    heat_local = (
        HEAT_SCALE * TAYLOR_QUINNEY * (equivalent - 3.0 * shear_mod * plastic_rate) * plastic_rate
    )
    return (updated, heat_local)


def node_forces(updated):
    force_x = face_term(updated[0], 0) + face_term(updated[3], 1) + face_term(updated[5], 2)
    force_y = face_term(updated[3], 0) + face_term(updated[1], 1) + face_term(updated[4], 2)
    force_z = face_term(updated[5], 0) + face_term(updated[4], 1) + face_term(updated[2], 2)
    return -0.25 * jnp.stack([force_x, force_y, force_z])


def mechanics(padded, corner_weights_diagonal):
    node_vel = padded[0:3]
    updated, heat_local = element_state(node_vel, padded[3:, :-1, :-1, :-1])
    force = node_forces(updated)
    corner_speed_later = node_vel[:, 1:-1, 1:-1, 1:-1] - TIME_STEP * force / corner_weights_diagonal
    return (corner_speed_later, updated[:, 1:, 1:, 1:], heat_local[1:, 1:, 1:])


def stencil(values, padded, matrix_main_entries):
    beside = padded[2:, 1:-1, 1:-1] + padded[:-2, 1:-1, 1:-1]
    beside = beside + padded[1:-1, 2:, 1:-1] + padded[1:-1, :-2, 1:-1]
    beside = beside + padded[1:-1, 1:-1, 2:] + padded[1:-1, 1:-1, :-2]
    return matrix_main_entries * values - beside


def diffuse_thermal_once(values, matrix_main_entries):
    haloed = extended(values, (("gx", 0), (("gy", "gz"), 1)), 1)
    padded = jnp.pad(haloed, ((0, 0), (0, 0), (1, 1)))
    return stencil(values, padded, matrix_main_entries)


def polynomial_relaxation(
    brick_warmth_prior,
    caloric_capacity_per_timestep,
    plastic_work_heating_rise,
    diffuse_thermal_field,
    inward_cell_flags,
):
    center_value = 0.5 * (UPPER_BOUND + LOWER_BOUND)
    half_width = 0.5 * (UPPER_BOUND - LOWER_BOUND)
    ratio_sig = center_value / half_width
    matrix_main_entries = 6.0 + caloric_capacity_per_timestep
    linear_system_target = (
        caloric_capacity_per_timestep * brick_warmth_prior + plastic_work_heating_rise
    )
    implicit_kelvin_result = brick_warmth_prior
    equation_misfit = (
        linear_system_target - diffuse_thermal_field(implicit_kelvin_result, matrix_main_entries)
    ) * inward_cell_flags
    weight_now = 1.0 / ratio_sig
    search_direction = equation_misfit / center_value
    for sweep_index in range(SWEEPS):
        implicit_kelvin_result = implicit_kelvin_result + search_direction
        if sweep_index + 1 < SWEEPS:
            equation_misfit = (
                equation_misfit - diffuse_thermal_field(search_direction, matrix_main_entries)
            ) * inward_cell_flags
            weight_next = 1.0 / (2.0 * ratio_sig - weight_now)
            search_direction = (
                weight_next * weight_now * search_direction
                + 2.0 * weight_next / half_width * equation_misfit
            )
            weight_now = weight_next
    return implicit_kelvin_result


def body(
    corner_speed_prior,
    brick_stress_tensor_now,
    compact_onset_strength,
    corner_weights_diagonal,
    substance_labels,
    brick_warmth_prior,
    caloric_capacity_per_timestep,
):
    z_index = lax.axis_index("gz")
    local_mat = lax.dynamic_slice_in_dim(substance_labels, z_index * ZB, ZB, 1)
    shear_blk, bulk_blk = moduli(local_mat)
    powder_cells = spread_blocks(local_mat, BS) == 2
    yield_eff = jnp.where(powder_cells, compact_onset_strength, ELASTIC_YIELD)
    stacked = jnp.concatenate(
        [
            corner_speed_prior,
            brick_stress_tensor_now,
            yield_eff[None],
            spread_blocks(shear_blk, BS)[None],
            spread_blocks(bulk_blk, BS)[None],
        ],
        axis=0,
    )
    padded = extended(stacked, (("gx", 1), ("gy", 3), ("gz", 2)), 1)
    corner_speed_later, projected_brick_stress_tensor, heat_local = mechanics(
        padded, corner_weights_diagonal
    )
    moved = lax.all_to_all(heat_local, "gz", split_axis=2, concat_axis=1, tiled=True)
    plastic_work_heating_rise = jnp.transpose(moved, (0, 2, 1))
    diffused_kelvin_field = polynomial_relaxation(
        brick_warmth_prior,
        caloric_capacity_per_timestep,
        plastic_work_heating_rise,
        diffuse_thermal_once,
        1.0,
    )
    return (corner_speed_later, projected_brick_stress_tensor, diffused_kelvin_field)


LANES = 128
VELS = 3
FIELDS = 11
SLOT = 4
RING = 12
PLANES = 14
MAIN = RING * 2 * BS
VMEM_BYTES = 48 * 1024 * 1024


def two_rounds_fit(mesh):
    return mesh.shape["gx"] == 2 and mesh.shape["gy"] == 2 and mesh.shape["gz"] == 8


def by_shape(*args):
    fits = args[0].shape[1:] == (BS, ZB * BS, LANES // 2) and args[5].shape == (BS, BS, LANES)
    return (two_round_body if fits else body)(*args)


def iota(shape, dim):
    return lax.broadcasted_iota(jnp.int32, shape, dim)


def place(q):
    return MAIN + RING * q if q < 5 else 2 * LANES + RING * (q - 5)


NODES = 2 * LANES + 2 * RING


def bulk_of(shear_mod):
    return jnp.where(
        shear_mod == 3.0,
        5.0,
        jnp.where(shear_mod == 2.0, 4.0, jnp.where(shear_mod == 0.0, 0.0, 1.2)),
    )


def own_labels(labels):
    second, press = labels.shape
    rows = ZB * BS
    first = lax.axis_index("gz") * ZB
    pick = iota((rows, press), 1) == first + iota((rows, press), 0) // BS
    spread = iota((second, LANES), 0) == (iota((second, LANES), 1) // BS) % second
    picked = lax.dot_general(
        pick.astype(jnp.float32),
        labels.astype(jnp.float32),
        (((1,), (1,)), ((), ())),
        preferred_element_type=jnp.float32,
    )
    return jnp.dot(picked, spread.astype(jnp.float32), preferred_element_type=jnp.float32)


FACE = (
    [(field, i) for field in range(VELS) for i in range(3)]
    + [(field, i) for field in range(VELS, 10) for i in range(2)]
    + [(10, 0)]
)
FACE_TILES = len(FACE) // 2 * ZB
PLANE = ZB * BS


def slot_at(lane, field, first):
    where = lax.rem(lane + (2 * LANES - SLOT * field) - first, LANES)
    return where < 3


def pack_kernel(
    labels, vel, stress, onset, warmth, capacity,
    wide, shear_out, face, columns, corner, warmth_out, capacity_out,
    own, own_labels_in, sems,
):
    lower_x = lax.axis_index("gx") == 0
    lower_y = lax.axis_index("gy") == 0
    deep = jnp.where(lower_x, BS - 3, 0)
    shallow = jnp.where(lower_x, BS - 2, 0)
    edge = jnp.where(lower_x, BS - 1, 0)
    copies = [
        pltpu.make_async_copy(*pair, sems.at[n])
        for n, pair in enumerate(
            (
                (labels, own_labels_in),
                (vel, own.at[pl.ds(0, VELS)]),
                (onset, own.at[9]),
                (stress, own.at[pl.ds(VELS, 6)]),
                (warmth.at[pl.ds(deep, 3)], face.at[pl.ds(FACE_TILES, 3)]),
                (capacity.at[edge], face.at[FACE_TILES + 3]),
                (warmth, warmth_out),
                (capacity, capacity_out),
            )
        )
    ]
    for copy in copies:
        copy.start()
    lane = iota((PLANE, LANES), 1)
    half = LANES // 2
    copies[0].wait()
    material = own_labels(own_labels_in[0])
    shear_mod = jnp.where(material == 0.0, 3.0, jnp.where(material == 1.0, 2.0, 0.8))
    shear_out[...] = shear_mod
    copies[1].wait()
    copies[2].wait()
    for field in range(VELS):
        wide[pl.ds(field * BS * PLANE, BS * PLANE), 0:half] = own[field].reshape(BS * PLANE, half)
    powder = material[:, 0:half] == 2.0
    for x in range(BS):
        at = pl.ds((9 * BS + x) * PLANE, PLANE)
        wide[at, 0:half] = jnp.where(powder, own[9, x], ELASTIC_YIELD)
    def read(field, x):
        if field == 10:
            return shear_mod
        return wide[pl.ds(pl.multiple_of((field * BS + x) * PLANE, PLANE), PLANE), :]

    first = jnp.where(lower_y, half - 3, 0)
    insides = [slot_at(lane, field, first) for field in range(FIELDS)]

    def pack_columns(fields, x, packed):
        for field in fields:
            turned = read(field, x)
            if field:
                turned = pltpu.roll(turned, SLOT * field, 1)
            packed = jnp.where(insides[field], turned, packed)
        columns[x] = packed

    for x in range(BS):
        pack_columns((0, 1, 2, 9, 10), x, jnp.zeros((PLANE, LANES), jnp.float32))
    copies[3].wait()
    for field in range(VELS, 9):
        wide[pl.ds(field * BS * PLANE, BS * PLANE), 0:half] = own[field].reshape(BS * PLANE, half)
    for pair in range(len(FACE) // 2):
        one, two = (
            read(field, (deep if field < VELS else shallow) + i)
            for field, i in FACE[2 * pair : 2 * pair + 2]
        )
        joined = jnp.where(lane < half, one, pltpu.roll(two, half, 1))
        face[2 * pair] = joined[:BS]
        face[2 * pair + 1] = joined[BS:]
    for x in range(BS):
        pack_columns(range(VELS, 9), x, columns[x])
    for i in range(3):
        corner[i] = columns[deep + i]
    for copy in copies[4:]:
        copy.wait()


def warmth_plane(j, warmth, face):
    upper_x = lax.axis_index("gx") == 1
    if j < 3:
        return jnp.where(upper_x, face[FACE_TILES + j], 0.0)
    if j < 11:
        return warmth[j - 3]
    return jnp.where(upper_x, 0.0, face[FACE_TILES + j - 11])


def capacity_plane(j, capacity, face):
    upper_x = lax.axis_index("gx") == 1
    if 3 <= j < 11:
        return capacity[j - 3]
    if j == 2 or j == 11:
        return jnp.where(upper_x == (j == 2), face[FACE_TILES + 3], 0.0)
    return jnp.zeros((BS, LANES), jnp.float32)


def stress_terms(shear_mod):
    bulk_mod = bulk_of(shear_mod)
    return (
        0.5 * TIME_STEP * shear_mod,
        0.25 * TIME_STEP * (bulk_mod - 2.0 / 3.0 * shear_mod),
        3.0 * shear_mod,
        1.0 / (3.0 * shear_mod + VISCOSITY / TIME_STEP),
    )


def strained(before, grads, terms):
    twice, volume_term = terms[0], terms[1]
    volume = volume_term * (grads[0] + grads[1] + grads[2])
    return [
        before[k] + twice * grads[k] + (volume if k < 3 else 0.0) for k in range(6)
    ]


def returned(trial, yield_eff, terms):
    shear_thrice, slope = terms[2], terms[3]
    pressure = (trial[0] + trial[1] + trial[2]) * (1.0 / 3.0)
    dev = [trial[k] - pressure for k in range(3)]
    second = (
        dev[0] * dev[0]
        + dev[1] * dev[1]
        + dev[2] * dev[2]
        + 2.0 * (trial[3] * trial[3] + trial[4] * trial[4] + trial[5] * trial[5])
    )
    equivalent = jnp.sqrt(1.5 * second)
    excess = equivalent - (yield_eff + FRICTION * jnp.maximum(-pressure, 0.0))
    active = excess > 0.0
    rate = jnp.maximum(excess, 0.0) * slope
    drop = shear_thrice * rate
    scale = jnp.where(active, 1.0 - drop / jnp.where(active, equivalent, 1.0), 1.0)
    heat = HEAT_SCALE * TAYLOR_QUINNEY * (equivalent - drop) * rate
    updated = [pressure + scale * dev[k] for k in range(3)] + [
        scale * trial[k] for k in range(3, 6)
    ]
    return updated, heat


def six(gx, gp, gs):
    return [
        gx[0],
        gp[1],
        gs[2],
        0.5 * (gp[0] + gx[1]),
        0.5 * (gs[1] + gp[2]),
        0.5 * (gs[0] + gx[2]),
    ]


LAYERS = 14


def block_of(a):
    return 0 if a < 2 else 1 if a < 10 else 2


def layers(ext, shears, first, end):
    rows = PLANE
    row = iota((rows, LANES), 0)

    def read(field, j):
        return ext[pl.ds((field * LAYERS + j) * rows, rows), :]

    def node_terms(j):
        terms = []
        for c in range(VELS):
            here = read(c, j)
            above = jnp.where(row == rows - 1, 0.0, pltpu.roll(here, rows - 1, 0))
            total, change = here + above, above - here
            aside = pltpu.roll(total, LANES - 1, 1)
            terms.append((total + aside, aside - total, change + pltpu.roll(change, LANES - 1, 1)))
        return terms

    materials = [stress_terms(plane) for plane in shears]
    before = node_terms(first + 1)
    for a in range(first, end):
        after = node_terms(a + 2)
        grads = six(
            [after[c][0] - before[c][0] for c in range(VELS)],
            [after[c][2] + before[c][2] for c in range(VELS)],
            [after[c][1] + before[c][1] for c in range(VELS)],
        )
        material = materials[block_of(a)]
        trial = strained([read(VELS + k, a + 1) for k in range(6)], grads, material)
        yield (a, *returned(trial, read(9, a + 1), material))
        before = after


RIM_PAIRS = RING // 2
RIM_ROWS = RIM_PAIRS * BS


def rim_kernel(warmth, capacity, face, rim_out, twin_out):
    even = lax.rem(lax.axis_index("gz"), 2) == 0
    sub = iota((BS, LANES), 0)
    ups, downs = [], []
    for j in range(1, RING + 1):
        u = warmth_plane(j, warmth, face)
        c = capacity_plane(j, capacity, face)
        ups.append(jnp.where(sub > 4, u, pltpu.roll(c, 5, 0)))
        downs.append(jnp.where(sub < 3, u, pltpu.roll(c, 3, 0)))
    for m in range(RIM_PAIRS):
        at = pl.ds(m * BS, BS)
        up = jnp.where(sub < 4, pltpu.roll(ups[2 * m], 4, 0), ups[2 * m + 1])
        down = jnp.where(sub < 4, downs[2 * m], pltpu.roll(downs[2 * m + 1], 4, 0))
        rim_out[at, :] = jnp.where(even, down, up)
        twin_out[at, :] = jnp.where(even, up, down)


def heat_kernel(
    wide, shear, rim, rim_twin, face, columns, corner,
    chunks_out, even_out, odd_out, ext, shears_out, partial_out,
    stacked, chunks, sem,
):
    upper_x = lax.axis_index("gx") == 1
    upper_y = lax.axis_index("gy") == 1
    even = lax.rem(lax.axis_index("gz"), 2) == 0
    rows = PLANE
    half = LANES // 2
    lane = iota((rows, LANES), 1)
    first = jnp.where(upper_y, LANES - 3, half)
    beside = (lane >= first) & (lane < first + 3)
    faces = {key: at for at, key in enumerate(FACE)}

    def joined(field, plane, side):
        side = pltpu.roll(side, (half - SLOT * field) % LANES, 1)
        return jnp.where(lane < half, plane, jnp.where(beside, side, 0.0))

    def far(field, i, side):
        at = faces[field, i]
        pair = at // 2
        plane = jnp.concatenate([face[2 * pair], face[2 * pair + 1]], axis=0)
        return joined(field, pltpu.roll(plane, half, 1) if at % 2 else plane, side)

    def layer(field, j):
        if 3 <= j < 11:
            at = (field * BS + j - 3) * rows
            return joined(field, wide[pl.ds(at, rows), :], columns[j - 3])
        side = corner[j] if j < 3 else corner[j - 11]
        i = j - 11 if j >= 11 else j if field < VELS else j - 1
        plane = far(field, i, side)
        return jnp.where(upper_x, plane, 0.0) if j < 3 else jnp.where(upper_x, 0.0, plane)

    for field in range(10):
        for j in range(1, LAYERS if field < VELS else LAYERS - 1):
            ext[pl.ds((field * LAYERS + j) * rows, rows), :] = layer(field, j)
    outer = far(10, 0, corner[1])
    shears = [
        jnp.where(upper_x, outer, 0.0),
        joined(10, shear[...], columns[0]),
        jnp.where(upper_x, 0.0, outer),
    ]
    for block in range(3):
        shears_out[block] = shears[block]

    row = iota((rows, LANES), 0)

    def across(field, press):
        at = (field * LAYERS + 1) * rows + press
        return ext[pl.ds(at, rows, stride=rows), :]

    def parts(press, sign):
        terms = []
        for c in range(VELS):
            here = across(c, press)
            aside = pltpu.roll(here, LANES - 1, 1)
            total, change = here + aside, aside - here
            nxt = pltpu.roll(total, rows - 1, 0)
            both = nxt + total
            terms.append((nxt - total, sign * both, change + pltpu.roll(change, rows - 1, 0)))
        return six(*[[terms[c][d] for c in range(VELS)] for d in range(3)])

    last = rows - 1
    shear_row = [shears[block][last:, :] for block in range(3)]
    shear_mod = jnp.where(row < 2, shear_row[0], jnp.where(row < 10, shear_row[1], shear_row[2]))
    trial = strained(
        [across(VELS + k, last) for k in range(6)], parts(last, -1.0), stress_terms(shear_mod)
    )
    for q, plane in enumerate(trial + [across(9, last), shear_mod]):
        partial_out[q] = plane
    for k, plane in enumerate(parts(0, 1.0)):
        partial_out[8 + k] = plane

    sub = iota((BS, LANES), 0)
    for q in range(7):
        stacked[pl.ds(place(q), RING), :] = partial_out[q, pl.ds(0, RING), :]
    for c in range(VELS):
        stacked[pl.ds(NODES + (RING + 1) * c, RING + 1), :] = across(c, 0)[: RING + 1]

    for a, updated, heat in layers(ext, shears, 0, RING):
        shear_mod = shears[block_of(a)]
        stacked[pl.ds(a * rows, rows), :] = jnp.where(row == rows - 1, shear_mod, heat)
    turned = jnp.transpose(stacked[...])
    for g in range(chunks.shape[0]):
        here, after, before = (
            turned[at % LANES : at % LANES + BS, :] for at in (g * BS, g * BS + BS, g * BS - BS)
        )
        for t in range(2):
            chunks[g, pl.ds(t * BS, BS), :] = here[:, t * LANES : (t + 1) * LANES]
        sides = [
            jnp.where(
                sub < 4,
                after[:, t * LANES : (t + 1) * LANES],
                before[:, t * LANES : (t + 1) * LANES],
            )
            for t in range(3)
        ]
        inner = jnp.where(sub < 4, pltpu.roll(sides[1], 2, 0), pltpu.roll(sides[1], 6, 0))
        chunks[g, pl.ds(2 * BS, BS), :] = jnp.where((sub < 2) | (sub > 5), sides[0], inner)
        chunks[g, pl.ds(3 * BS, BS), :] = jnp.where(
            lane[:BS] < half, here[:, 2 * LANES :], pltpu.roll(sides[2], half, 1)
        )
    copy = pltpu.make_async_copy(chunks, chunks_out, sem)
    copy.start()

    def fill(up_ref, down_ref):
        for q in range(8):
            up_ref[pl.ds(RIM_ROWS + NEAR * q, NEAR), :] = partial_out[q, pl.ds(1, NEAR), :]
        for k in range(6):
            down_ref[pl.ds(RIM_ROWS + NEAR * k, NEAR), :] = partial_out[8 + k, pl.ds(1, NEAR), :]
        for ref, count in ((up_ref, 8), (down_ref, 6)):
            rest = EDGE_ALL - RIM_ROWS - NEAR * count
            ref[pl.ds(EDGE_ALL - rest, rest), :] = jnp.zeros((rest, LANES), jnp.float32)
        even_out[pl.ds(0, RIM_ROWS), :] = rim_twin[...]
        odd_out[pl.ds(0, RIM_ROWS), :] = rim[...]

    @pl.when(even)
    def _():
        fill(even_out, odd_out)

    @pl.when(jnp.logical_not(even))
    def _():
        fill(odd_out, even_out)

    copy.wait()


NEAR = BS + 1
EDGE_ALL = RIM_ROWS + 8 * NEAR + BS


def corrected(planes, sign):
    rows = PLANE
    total, change, press = [], [], []
    for plane in planes:
        aside = pltpu.roll(plane, 1, 1)
        total.append(plane + aside)
        change.append(plane - aside)
        press.append(sign * (plane + aside))
    forces = []
    for kx, kp, ks in FORCE_TERMS:
        both = press[kp] + change[ks]
        forces.append(
            total[kx] - pltpu.roll(total[kx], 1, 0) + both + pltpu.roll(both, 1, 0)
        )
    return forces


FORCE_TERMS = ((0, 3, 5), (3, 1, 4), (5, 4, 2))


def gather_kernel(chunks, heats_out):
    groups = lax.axis_size("gz")
    rows = PLANE
    lane = iota((rows, LANES), 1)
    group = lane // rows
    sub = iota((BS, LANES), 0)

    sources = [[], [], []]
    for g in range(groups):
        tiles = [chunks[g, pl.ds(t * BS, BS), :] for t in range(4)]
        inner = jnp.where(sub < 4, pltpu.roll(tiles[2], 6, 0), pltpu.roll(tiles[2], 2, 0))
        outer = pltpu.roll(tiles[3], LANES // 2, 1)
        for t, pair in enumerate(((tiles[0], tiles[2]), (tiles[1], inner), (tiles[3], outer))):
            sources[t].append(jnp.concatenate(pair, axis=0))

    heats = []
    for t, count in ((0, 8), (1, 4)):
        turned = []
        for k in range(groups):
            mixed = sources[t][k]
            for b in range(1, count):
                mixed = jnp.where(group == b, sources[t][(b + k) % groups], mixed)
            turned.append(pltpu.roll(mixed, k * rows, 1) if k else mixed)
        for b in range(count):
            heat = turned[(0 - b) % groups]
            for g in range(1, groups):
                heat = jnp.where(group == g, turned[(g - b) % groups], heat)
            heats.append(heat)

    def spread(position, width, first):
        tile, at = divmod(position, LANES)
        plane = jnp.zeros((rows, LANES), jnp.float32)
        for g in range(first, groups):
            to = (g - first) * rows
            inside = (lane >= to) & (lane < to + width)
            plane = jnp.where(inside, pltpu.roll(sources[tile][g], (to - at) % LANES, 1), plane)
        return plane

    place_in = lane % rows
    trial = [spread(place(k), RING, 0) for k in range(6)]
    yield_eff = spread(place(6), RING, 0)
    shear_mod = jnp.zeros((rows, LANES), jnp.float32)
    for a in range(RING):
        turned = pltpu.roll(heats[a], (a - rows + 1) % LANES, 1)
        shear_mod = jnp.where(place_in == a, turned, shear_mod)
    gx, gp, gs = [], [], []
    for c in range(VELS):
        here = spread(NODES + (RING + 1) * c, RING + 1, 1)
        aside = pltpu.roll(here, rows - 1, 0)
        total, change = here + aside, aside - here
        nxt = pltpu.roll(total, LANES - 1, 1)
        gx.append(nxt - total)
        gp.append(nxt + total)
        gs.append(change + pltpu.roll(change, LANES - 1, 1))
    terms = stress_terms(shear_mod)
    seam = returned(strained(trial, six(gx, gp, gs), terms), yield_eff, terms)[1]
    for a in range(RING):
        heats_out[a] = jnp.where(
            place_in == rows - 1, pltpu.roll(seam, rows - 1 - a, 1), heats[a]
        )


def force_kernel(ext, shears, vel, mass, stress_hbm, base_out, updated_out, low, sem):
    rows = PLANE
    row = iota((rows, LANES), 0)
    for a, updated, _ in layers(ext, [shears[block] for block in range(3)], 1, 10):
        for k in range(6):
            updated_out[k, a - 1] = updated[k]
            if a > 1:
                low[k, a - 2] = updated[k][:BS, : LANES // 2]
    copy = pltpu.make_async_copy(low, stress_hbm.at[:, :, pl.ds(0, BS), :], sem)
    copy.start()

    def element_terms(j):
        terms = []
        for k in range(6):
            here = jnp.where(row == rows - 1, 0.0, updated_out[k, j])
            prev = pltpu.roll(here, 1, 0)
            total, change = here + prev, here - prev
            aside = pltpu.roll(total, 1, 1)
            terms.append((total + aside, total - aside, change + pltpu.roll(change, 1, 1)))
        return terms

    before = element_terms(0)
    for x in range(BS):
        after = element_terms(x + 1)
        weights = 0.25 * TIME_STEP / mass[x]
        for c, (kx, kp, ks) in enumerate(FORCE_TERMS):
            force = (
                (after[kx][0] - before[kx][0])
                + (after[kp][2] + before[kp][2])
                + (after[ks][1] + before[ks][1])
            )
            base_out[c, x] = vel[c, x] + force[:, : LANES // 2] * weights
        before = after
    copy.wait()


def finish_kernel(
    heats, base, updated, partial, mass, warmth, capacity, face, odd_in, even_in, _,
    vel_hbm, stress_hbm, out_hbm,
    vel_out, stress_out, out, top, low_force, high_force, sems,
):
    upper_x = lax.axis_index("gx") == 1
    at_z = lax.axis_index("gz")
    even = lax.rem(at_z, 2) == 0
    groups = lax.axis_size("gz")
    rows = PLANE
    half = LANES // 2
    at_flat = lax.axis_index("gy") * groups + at_z
    last = lax.axis_size("gy") * groups - 1
    has_above = at_z < groups - 1
    has_below = at_z > 0
    lane = iota((rows, LANES), 1)
    row = iota((rows, LANES), 0)
    sub = iota((BS, LANES), 0)

    def below_plane(q):
        at = pl.ds(RIM_ROWS + NEAR * q - 1, rows)
        return jnp.where(has_below, jnp.where(even, odd_in[at, :], even_in[at, :]), 0.0)

    def above_plane(k):
        at = pl.ds(RIM_ROWS + NEAR * k - 1, rows)
        return jnp.where(has_above, jnp.where(even, even_in[at, :], odd_in[at, :]), 0.0)

    terms = stress_terms(partial[7])
    trial = strained([partial[k] for k in range(6)], [above_plane(k) for k in range(6)], terms)
    uppermost = returned(trial, partial[6], terms)[0]
    for k, plane in enumerate(uppermost):
        top[k] = plane
    copies = [
        pltpu.make_async_copy(*pair, sems.at[n])
        for n, pair in enumerate((
                (vel_out, vel_hbm),
                (stress_out, stress_hbm.at[:, :, pl.ds(BS, BS), :]),
                (out, out_hbm),
            ))
    ]
    for x in range(BS):
        for k in range(6):
            plane = jnp.where(sub == BS - 1, top[k, pl.ds(x + 2, 1), :], updated[k, x + 1][BS:])
            stress_out[k, x] = plane[:, :half]
    copies[1].start()
    for c, plane in enumerate(corrected(uppermost, 1.0)):
        high_force[c] = plane
    terms = stress_terms(below_plane(7))
    trial = strained([below_plane(k) for k in range(6)], [partial[8 + k] for k in range(6)], terms)
    for c, plane in enumerate(corrected(returned(trial, below_plane(6), terms)[0], -1.0)):
        low_force[c] = plane
    for x in range(BS):
        at = pl.ds(x + 2, 1)
        weights = 0.25 * TIME_STEP / mass[x]
        for c in range(VELS):
            force = jnp.where(
                row == 0, low_force[c, at, :], jnp.where(row == rows - 1, high_force[c, at, :], 0.0)
            )
            vel_out[c, x] = base[c, x] + force[:, :half] * weights
    copies[0].start()

    above, below = at_flat < last, at_flat > 0
    u_rows = (row < BS) | ((row < BS + 3) & above) | ((row >= rows - 3) & below)
    d_rows = (row < BS) | ((row < BS + 2) & above) | ((row >= rows - 2) & below)
    us, caps = [], []
    for j in range(14):
        at = pl.ds(min(max(j - 1, 0), RING - 1) // 2 * BS, BS)
        low = jnp.where(even, odd_in[at, :], even_in[at, :])
        high = jnp.where(even, even_in[at, :], odd_in[at, :])
        if j % 2:
            low = pltpu.roll(low, 4, 0)
        else:
            high = pltpu.roll(high, 4, 0)
        side = jnp.where(sub < 4, high, low)
        u = jnp.concatenate([warmth_plane(j, warmth, face), side], axis=0)
        us.append(jnp.where(u_rows, u, 0.0))
        side = jnp.where(sub < 4, pltpu.roll(high, 5, 0), pltpu.roll(low, 3, 0))
        caps.append(6.0 + jnp.concatenate([capacity_plane(j, capacity, face), side], axis=0))

    def around(fields, a):
        here = fields[a]
        total = fields[a - 1] + fields[a + 1]
        total = total + pltpu.roll(here, 1, 0) + pltpu.roll(here, rows - 1, 0)
        total = total + jnp.where(lane == 0, 0.0, pltpu.roll(here, 1, 1))
        return total + jnp.where(lane == LANES - 1, 0.0, pltpu.roll(here, LANES - 1, 1))

    def inside(a):
        if a < 2:
            return d_rows & upper_x
        if a >= 10:
            return d_rows & jnp.logical_not(upper_x)
        return d_rows

    theta = 0.5 * (UPPER_BOUND + LOWER_BOUND)
    half_width = 0.5 * (UPPER_BOUND - LOWER_BOUND)
    sig = theta / half_width
    weight_now = 1.0 / sig
    misfit, step, total = {}, {}, {}
    for a in range(RING):
        misfit[a] = heats[a] - 6.0 * us[a + 1] + around(us, a + 1)
        step[a] = jnp.where(inside(a), misfit[a] * (1.0 / theta), 0.0)
        total[a] = us[a + 1] + step[a]
    for sweep in range(1, SWEEPS):
        weight_next = 1.0 / (2.0 * sig - weight_now)
        new_misfit, new_step = {}, {}
        for a in range(sweep, RING - sweep):
            new_misfit[a] = misfit[a] - caps[a + 1] * step[a] + around(step, a)
            moved = (weight_next * weight_now) * step[a] + (
                2.0 * weight_next / half_width
            ) * new_misfit[a]
            new_step[a] = jnp.where(inside(a), moved, 0.0)
            total[a] = total[a] + new_step[a]
        misfit, step, weight_now = new_misfit, new_step, weight_next
    for x in range(BS):
        out[x] = total[x + 2][:BS]
    copies[2].start()
    for copy in copies:
        copy.wait()


def f32(*shape):
    return jax.ShapeDtypeStruct(shape, jnp.float32)


def call(kernel, out_shape, *args, scratch=(), far_in=False, far_out=0, onto=None):
    moved = 4 * sum(a.size for a in args) + 4 * sum(o.size for o in jax.tree.leaves(out_shape))
    hbm, vmem = (pl.BlockSpec(memory_space=space) for space in (pltpu.HBM, pltpu.VMEM))
    return pl.pallas_call(
        kernel,
        out_shape=out_shape,
        in_specs=[hbm if far_in or n == onto else vmem for n in range(len(args))],
        input_output_aliases={} if onto is None else {onto: 1},
        out_specs=tuple(hbm if n < far_out else vmem for n in range(len(out_shape))),
        scratch_shapes=scratch,
        compiler_params=pltpu.CompilerParams(vmem_limit_bytes=VMEM_BYTES),
        cost_estimate=pl.CostEstimate(flops=0, bytes_accessed=moved, transcendentals=0),
    )(*args)


def room(*shape):
    return pltpu.VMEM(shape, jnp.float32)


def paired(count, first):
    pairs = []
    for i in range(first, count - 1, 2):
        pairs += [(i, i + 1), (i + 1, i)]
    return pairs


def two_round_body(
    corner_speed_prior,
    brick_stress_tensor_now,
    compact_onset_strength,
    corner_weights_diagonal,
    substance_labels,
    brick_warmth_prior,
    caloric_capacity_per_timestep,
):
    rows = PLANE
    groups = lax.axis_size("gz")
    chain = groups * lax.axis_size("gy")
    labels = jnp.transpose(substance_labels, (0, 2, 1))
    raw = (
        labels,
        corner_speed_prior,
        brick_stress_tensor_now,
        compact_onset_strength,
        brick_warmth_prior,
        caloric_capacity_per_timestep,
    )
    raw = [pltpu.with_memory_space_constraint(array, pltpu.HBM) for array in raw]
    second = compact_onset_strength.shape[-1]
    wide, shear, face, columns, corner, warmth, capacity = call(
        pack_kernel,
        (
            f32(10 * BS * rows, LANES),
            f32(rows, LANES),
            f32(FACE_TILES + 4, BS, LANES),
            f32(BS, rows, LANES),
            f32(3, rows, LANES),
            f32(*brick_warmth_prior.shape),
            f32(*brick_warmth_prior.shape),
        ),
        *raw,
        far_in=True,
        scratch=(
            room(10, BS, rows, second),
            pltpu.VMEM(labels.shape, jnp.int32),
            pltpu.SemaphoreType.DMA((len(raw) + 2,)),
        ),
    )
    face = lax.ppermute(face, "gx", [(0, 1), (1, 0)])
    columns = lax.ppermute(columns, "gy", [(0, 1), (1, 0)])
    corner = lax.ppermute(corner, ("gx", "gy"), [(0, 3), (3, 0), (1, 2), (2, 1)])
    rim, twin = call(
        rim_kernel, (f32(RIM_ROWS, LANES), f32(RIM_ROWS, LANES)), warmth, capacity, face
    )
    chunks, even, odd, ext, shears, partial = call(
        heat_kernel,
        (
            f32(groups, 4 * BS, LANES),
            f32(EDGE_ALL, LANES),
            f32(EDGE_ALL, LANES),
            f32((10 * LAYERS + 3) * rows, LANES),
            f32(3, rows, LANES),
            f32(PLANES, rows, LANES),
        ),
        wide,
        shear,
        rim,
        twin,
        face,
        columns,
        corner,
        scratch=(
            room(3 * LANES, LANES),
            room(groups, 4 * BS, LANES),
            pltpu.SemaphoreType.DMA,
        ),
        far_out=1,
    )
    chunks = lax.all_to_all(chunks, "gz", split_axis=0, concat_axis=0, tiled=True)
    odd = lax.ppermute(odd, ("gy", "gz"), paired(chain, 1))
    even = lax.ppermute(even, "gz", paired(groups, 0))
    stress, base, updated = call(
        force_kernel,
        (f32(*brick_stress_tensor_now.shape), f32(*corner_speed_prior.shape), f32(6, BS + 1, rows, LANES)),
        ext,
        shears,
        corner_speed_prior,
        corner_weights_diagonal,
        scratch=(room(6, BS, BS, second), pltpu.SemaphoreType.DMA),
        far_out=1,
    )
    (heats,) = call(gather_kernel, (f32(RING, rows, LANES),), chunks)
    odd, even, heats, base = lax.optimization_barrier((odd, even, heats, base))
    results = (corner_speed_prior.shape, brick_stress_tensor_now.shape, brick_warmth_prior.shape)
    return call(
        finish_kernel,
        tuple(f32(*shape) for shape in results),
        heats,
        base,
        updated,
        partial,
        corner_weights_diagonal,
        warmth,
        capacity,
        face,
        odd,
        even,
        stress,
        onto=10,
        scratch=(
            room(*results[0]),
            room(6, BS, BS, second),
            room(*results[2]),
            room(6, rows, LANES),
            room(VELS, rows, LANES),
            room(VELS, rows, LANES),
            pltpu.SemaphoreType.DMA((3,)),
        ),
        far_out=3,
    )


def solution(mesh):
    placed = (
        P(None, "gx", "gz", "gy"),
        P(None, "gx", "gz", "gy"),
        P("gx", "gz", "gy"),
        P("gx", "gz", "gy"),
        P("gx", None, "gy"),
        P("gx", ("gy", "gz"), None),
        P("gx", ("gy", "gz"), None),
    )
    return jax.shard_map(
        by_shape if two_rounds_fit(mesh) else body,
        mesh=mesh,
        in_specs=placed,
        out_specs=(
            P(None, "gx", "gz", "gy"),
            P(None, "gx", "gz", "gy"),
            P("gx", ("gy", "gz"), None),
        ),
        check_vma=False,
    )
```

```python
import jax
import jax.numpy as jnp
from jax import lax
from jax.experimental import pallas as pl
from jax.experimental.pallas import tpu as pltpu
from jax.sharding import PartitionSpec as P

BS = 8
ZB = 2
SWEEPS = 3


TIME_STEP = 0.2
VISCOSITY = 0.4
FRICTION = 0.5
TAYLOR_QUINNEY = 0.9
HEAT_SCALE = 5.0
ELASTIC_YIELD = 10000.0
LOWER_BOUND = 0.5
UPPER_BOUND = 16.0


def extended(cells, sides, width):
    for axis, dim in sides:
        count = lax.axis_size(axis)
        ends = count - 1
        head = lax.slice_in_dim(cells, 0, width, axis=dim)
        tail = lax.slice_in_dim(cells, cells.shape[dim] - width, cells.shape[dim], axis=dim)
        cells = jnp.concatenate(
            [
                lax.ppermute(tail, axis, [(i, (i + 1) % count) for i in range(ends)]),
                cells,
                lax.ppermute(head, axis, [((i + 1) % count, i) for i in range(ends)]),
            ],
            axis=dim,
        )
    return cells


def shifted_diff(values, axis_num):
    extent = values.shape[axis_num]
    return lax.slice_in_dim(values, 1, extent, axis=axis_num) - lax.slice_in_dim(
        values, 0, extent - 1, axis=axis_num
    )


def shifted_sum(values, axis_num):
    extent = values.shape[axis_num]
    return lax.slice_in_dim(values, 1, extent, axis=axis_num) + lax.slice_in_dim(
        values, 0, extent - 1, axis=axis_num
    )


def spread_blocks(values, width):
    extent_a, extent_b, extent_c = values.shape
    wide = jnp.broadcast_to(
        values[:, None, :, None, :, None], (extent_a, width, extent_b, width, extent_c, width)
    )
    return wide.reshape(extent_a * width, extent_b * width, extent_c * width)


def moduli(substance_labels):
    shear_mod = jnp.where(
        substance_labels == 0, 3.0, jnp.where(substance_labels == 1, 2.0, 0.8)
    ).astype(jnp.float32)
    bulk_mod = jnp.where(
        substance_labels == 0, 5.0, jnp.where(substance_labels == 1, 4.0, 1.2)
    ).astype(jnp.float32)
    return (shear_mod, bulk_mod)


def face_term(element_values, axis_num):
    others = [other for other in (0, 1, 2) if other != axis_num]
    return shifted_diff(shifted_sum(shifted_sum(element_values, others[0]), others[1]), axis_num)


def element_state(node_vel, props):
    grad_x = 0.25 * shifted_diff(shifted_sum(shifted_sum(node_vel, 2), 3), 1)
    grad_y = 0.25 * shifted_diff(shifted_sum(shifted_sum(node_vel, 1), 3), 2)
    grad_z = 0.25 * shifted_diff(shifted_sum(shifted_sum(node_vel, 1), 2), 3)
    yield_eff = props[6]
    shear_mod = props[7]
    bulk_mod = props[8]
    strain_xx = TIME_STEP * grad_x[0]
    strain_yy = TIME_STEP * grad_y[1]
    strain_zz = TIME_STEP * grad_z[2]
    strain_xy = TIME_STEP * (0.5 * (grad_y[0] + grad_x[1]))
    strain_yz = TIME_STEP * (0.5 * (grad_z[1] + grad_y[2]))
    strain_xz = TIME_STEP * (0.5 * (grad_z[0] + grad_x[2]))
    volume = strain_xx + strain_yy + strain_zz
    vol_third = volume / 3.0
    trial_xx = props[0] + 2.0 * shear_mod * (strain_xx - vol_third) + bulk_mod * volume
    trial_yy = props[1] + 2.0 * shear_mod * (strain_yy - vol_third) + bulk_mod * volume
    trial_zz = props[2] + 2.0 * shear_mod * (strain_zz - vol_third) + bulk_mod * volume
    trial_xy = props[3] + 2.0 * shear_mod * strain_xy
    trial_yz = props[4] + 2.0 * shear_mod * strain_yz
    trial_xz = props[5] + 2.0 * shear_mod * strain_xz
    pressure = (trial_xx + trial_yy + trial_zz) / 3.0
    dev_xx = trial_xx - pressure
    dev_yy = trial_yy - pressure
    dev_zz = trial_zz - pressure
    second = (
        dev_xx * dev_xx
        + dev_yy * dev_yy
        + dev_zz * dev_zz
        + 2.0 * (trial_xy * trial_xy + trial_yz * trial_yz + trial_xz * trial_xz)
    )
    equivalent = jnp.sqrt(1.5 * second)
    flow_stress = yield_eff + FRICTION * jnp.maximum(-pressure, 0.0)
    excess = equivalent - flow_stress
    active = excess > 0.0
    plastic_rate = jnp.maximum(excess, 0.0) / (3.0 * shear_mod + VISCOSITY / TIME_STEP)
    scale_back = jnp.where(
        active, 1.0 - 3.0 * shear_mod * plastic_rate / jnp.where(active, equivalent, 1.0), 1.0
    )
    updated = jnp.stack(
        [
            pressure + scale_back * dev_xx,
            pressure + scale_back * dev_yy,
            pressure + scale_back * dev_zz,
            scale_back * trial_xy,
            scale_back * trial_yz,
            scale_back * trial_xz,
        ]
    )
    heat_local = (
        HEAT_SCALE * TAYLOR_QUINNEY * (equivalent - 3.0 * shear_mod * plastic_rate) * plastic_rate
    )
    return (updated, heat_local)


def node_forces(updated):
    force_x = face_term(updated[0], 0) + face_term(updated[3], 1) + face_term(updated[5], 2)
    force_y = face_term(updated[3], 0) + face_term(updated[1], 1) + face_term(updated[4], 2)
    force_z = face_term(updated[5], 0) + face_term(updated[4], 1) + face_term(updated[2], 2)
    return -0.25 * jnp.stack([force_x, force_y, force_z])


def mechanics(padded, corner_weights_diagonal):
    node_vel = padded[0:3]
    updated, heat_local = element_state(node_vel, padded[3:, :-1, :-1, :-1])
    force = node_forces(updated)
    corner_speed_later = node_vel[:, 1:-1, 1:-1, 1:-1] - TIME_STEP * force / corner_weights_diagonal
    return (corner_speed_later, updated[:, 1:, 1:, 1:], heat_local[1:, 1:, 1:])


def stencil(values, padded, matrix_main_entries):
    beside = padded[2:, 1:-1, 1:-1] + padded[:-2, 1:-1, 1:-1]
    beside = beside + padded[1:-1, 2:, 1:-1] + padded[1:-1, :-2, 1:-1]
    beside = beside + padded[1:-1, 1:-1, 2:] + padded[1:-1, 1:-1, :-2]
    return matrix_main_entries * values - beside


def diffuse_thermal_once(values, matrix_main_entries):
    haloed = extended(values, (("gx", 0), (("gy", "gz"), 1)), 1)
    padded = jnp.pad(haloed, ((0, 0), (0, 0), (1, 1)))
    return stencil(values, padded, matrix_main_entries)


def polynomial_relaxation(
    brick_warmth_prior,
    caloric_capacity_per_timestep,
    plastic_work_heating_rise,
    diffuse_thermal_field,
    inward_cell_flags,
):
    center_value = 0.5 * (UPPER_BOUND + LOWER_BOUND)
    half_width = 0.5 * (UPPER_BOUND - LOWER_BOUND)
    ratio_sig = center_value / half_width
    matrix_main_entries = 6.0 + caloric_capacity_per_timestep
    linear_system_target = (
        caloric_capacity_per_timestep * brick_warmth_prior + plastic_work_heating_rise
    )
    implicit_kelvin_result = brick_warmth_prior
    equation_misfit = (
        linear_system_target - diffuse_thermal_field(implicit_kelvin_result, matrix_main_entries)
    ) * inward_cell_flags
    weight_now = 1.0 / ratio_sig
    search_direction = equation_misfit / center_value
    for sweep_index in range(SWEEPS):
        implicit_kelvin_result = implicit_kelvin_result + search_direction
        if sweep_index + 1 < SWEEPS:
            equation_misfit = (
                equation_misfit - diffuse_thermal_field(search_direction, matrix_main_entries)
            ) * inward_cell_flags
            weight_next = 1.0 / (2.0 * ratio_sig - weight_now)
            search_direction = (
                weight_next * weight_now * search_direction
                + 2.0 * weight_next / half_width * equation_misfit
            )
            weight_now = weight_next
    return implicit_kelvin_result


def body(
    corner_speed_prior,
    brick_stress_tensor_now,
    compact_onset_strength,
    corner_weights_diagonal,
    substance_labels,
    brick_warmth_prior,
    caloric_capacity_per_timestep,
):
    z_index = lax.axis_index("gz")
    local_mat = lax.dynamic_slice_in_dim(substance_labels, z_index * ZB, ZB, 1)
    shear_blk, bulk_blk = moduli(local_mat)
    powder_cells = spread_blocks(local_mat, BS) == 2
    yield_eff = jnp.where(powder_cells, compact_onset_strength, ELASTIC_YIELD)
    stacked = jnp.concatenate(
        [
            corner_speed_prior,
            brick_stress_tensor_now,
            yield_eff[None],
            spread_blocks(shear_blk, BS)[None],
            spread_blocks(bulk_blk, BS)[None],
        ],
        axis=0,
    )
    padded = extended(stacked, (("gx", 1), ("gy", 3), ("gz", 2)), 1)
    corner_speed_later, projected_brick_stress_tensor, heat_local = mechanics(
        padded, corner_weights_diagonal
    )
    moved = lax.all_to_all(heat_local, "gz", split_axis=2, concat_axis=1, tiled=True)
    plastic_work_heating_rise = jnp.transpose(moved, (0, 2, 1))
    diffused_kelvin_field = polynomial_relaxation(
        brick_warmth_prior,
        caloric_capacity_per_timestep,
        plastic_work_heating_rise,
        diffuse_thermal_once,
        1.0,
    )
    return (corner_speed_later, projected_brick_stress_tensor, diffused_kelvin_field)


LANES = 128
VELS = 3
FIELDS = 11
SLOT = 4
RING = 12
PLANES = 14
MAIN = RING * 2 * BS
VMEM_BYTES = 48 * 1024 * 1024


def two_rounds_fit(mesh):
    return mesh.shape["gx"] == 2 and mesh.shape["gy"] == 2 and mesh.shape["gz"] == 8


def by_shape(*args):
    fits = args[0].shape[1:] == (BS, ZB * BS, LANES // 2) and args[5].shape == (BS, BS, LANES)
    return (two_round_body if fits else body)(*args)


def iota(shape, dim):
    return lax.broadcasted_iota(jnp.int32, shape, dim)


def place(q):
    return MAIN + RING * q if q < 5 else 2 * LANES + RING * (q - 5)


NODES = 2 * LANES + 2 * RING


def bulk_of(shear_mod):
    return jnp.where(
        shear_mod == 3.0,
        5.0,
        jnp.where(shear_mod == 2.0, 4.0, jnp.where(shear_mod == 0.0, 0.0, 1.2)),
    )


def own_labels(labels):
    second, press = labels.shape
    rows = ZB * BS
    first = lax.axis_index("gz") * ZB
    pick = iota((rows, press), 1) == first + iota((rows, press), 0) // BS
    spread = iota((second, LANES), 0) == (iota((second, LANES), 1) // BS) % second
    picked = lax.dot_general(
        pick.astype(jnp.float32),
        labels.astype(jnp.float32),
        (((1,), (1,)), ((), ())),
        preferred_element_type=jnp.float32,
    )
    return jnp.dot(picked, spread.astype(jnp.float32), preferred_element_type=jnp.float32)


FACE = (
    [(field, i) for field in range(VELS) for i in range(3)]
    + [(field, i) for field in range(VELS, 10) for i in range(2)]
    + [(10, 0)]
)
FACE_TILES = len(FACE) // 2 * ZB
PLANE = ZB * BS


def slot_at(lane, field, first):
    where = lax.rem(lane + (2 * LANES - SLOT * field) - first, LANES)
    return where < 3


def pack_kernel(
    labels, vel, stress, onset, warmth, capacity,
    wide, shear_out, face, columns, corner, warmth_out, capacity_out,
    own, own_labels_in, sems,
):
    lower_x = lax.axis_index("gx") == 0
    lower_y = lax.axis_index("gy") == 0
    deep = jnp.where(lower_x, BS - 3, 0)
    shallow = jnp.where(lower_x, BS - 2, 0)
    edge = jnp.where(lower_x, BS - 1, 0)
    copies = [
        pltpu.make_async_copy(*pair, sems.at[n])
        for n, pair in enumerate(
            (
                (labels, own_labels_in),
                (vel, own.at[pl.ds(0, VELS)]),
                (onset, own.at[9]),
                (stress, own.at[pl.ds(VELS, 6)]),
                (warmth.at[pl.ds(deep, 3)], face.at[pl.ds(FACE_TILES, 3)]),
                (capacity.at[edge], face.at[FACE_TILES + 3]),
                (warmth, warmth_out),
                (capacity, capacity_out),
            )
        )
    ]
    for copy in copies:
        copy.start()
    lane = iota((PLANE, LANES), 1)
    half = LANES // 2
    copies[0].wait()
    material = own_labels(own_labels_in[0])
    shear_mod = jnp.where(material == 0.0, 3.0, jnp.where(material == 1.0, 2.0, 0.8))
    shear_out[...] = shear_mod
    copies[1].wait()
    copies[2].wait()
    for field in range(VELS):
        wide[pl.ds(field * BS * PLANE, BS * PLANE), 0:half] = own[field].reshape(BS * PLANE, half)
    powder = material[:, 0:half] == 2.0
    for x in range(BS):
        at = pl.ds((9 * BS + x) * PLANE, PLANE)
        wide[at, 0:half] = jnp.where(powder, own[9, x], ELASTIC_YIELD)
    def read(field, x):
        if field == 10:
            return shear_mod
        return wide[pl.ds(pl.multiple_of((field * BS + x) * PLANE, PLANE), PLANE), :]

    first = jnp.where(lower_y, half - 3, 0)
    insides = [slot_at(lane, field, first) for field in range(FIELDS)]

    def pack_columns(fields, x, packed):
        for field in fields:
            turned = read(field, x)
            if field:
                turned = pltpu.roll(turned, SLOT * field, 1)
            packed = jnp.where(insides[field], turned, packed)
        columns[x] = packed

    for x in range(BS):
        pack_columns((0, 1, 2, 9, 10), x, jnp.zeros((PLANE, LANES), jnp.float32))
    copies[3].wait()
    for field in range(VELS, 9):
        wide[pl.ds(field * BS * PLANE, BS * PLANE), 0:half] = own[field].reshape(BS * PLANE, half)
    for pair in range(len(FACE) // 2):
        one, two = (
            read(field, (deep if field < VELS else shallow) + i)
            for field, i in FACE[2 * pair : 2 * pair + 2]
        )
        joined = jnp.where(lane < half, one, pltpu.roll(two, half, 1))
        face[2 * pair] = joined[:BS]
        face[2 * pair + 1] = joined[BS:]
    for x in range(BS):
        pack_columns(range(VELS, 9), x, columns[x])
    for i in range(3):
        corner[i] = columns[deep + i]
    for copy in copies[4:]:
        copy.wait()


def warmth_plane(j, warmth, face):
    upper_x = lax.axis_index("gx") == 1
    if j < 3:
        return jnp.where(upper_x, face[FACE_TILES + j], 0.0)
    if j < 11:
        return warmth[j - 3]
    return jnp.where(upper_x, 0.0, face[FACE_TILES + j - 11])


def capacity_plane(j, capacity, face):
    upper_x = lax.axis_index("gx") == 1
    if 3 <= j < 11:
        return capacity[j - 3]
    if j == 2 or j == 11:
        return jnp.where(upper_x == (j == 2), face[FACE_TILES + 3], 0.0)
    return jnp.zeros((BS, LANES), jnp.float32)


def stress_terms(shear_mod):
    bulk_mod = bulk_of(shear_mod)
    return (
        0.5 * TIME_STEP * shear_mod,
        0.25 * TIME_STEP * (bulk_mod - 2.0 / 3.0 * shear_mod),
        3.0 * shear_mod,
        1.0 / (3.0 * shear_mod + VISCOSITY / TIME_STEP),
    )


def strained(before, grads, terms):
    twice, volume_term = terms[0], terms[1]
    volume = volume_term * (grads[0] + grads[1] + grads[2])
    return [
        before[k] + twice * grads[k] + (volume if k < 3 else 0.0) for k in range(6)
    ]


def returned(trial, yield_eff, terms):
    shear_thrice, slope = terms[2], terms[3]
    pressure = (trial[0] + trial[1] + trial[2]) * (1.0 / 3.0)
    dev = [trial[k] - pressure for k in range(3)]
    second = (
        dev[0] * dev[0]
        + dev[1] * dev[1]
        + dev[2] * dev[2]
        + 2.0 * (trial[3] * trial[3] + trial[4] * trial[4] + trial[5] * trial[5])
    )
    equivalent = jnp.sqrt(1.5 * second)
    excess = equivalent - (yield_eff + FRICTION * jnp.maximum(-pressure, 0.0))
    active = excess > 0.0
    rate = jnp.maximum(excess, 0.0) * slope
    drop = shear_thrice * rate
    scale = jnp.where(active, 1.0 - drop / jnp.where(active, equivalent, 1.0), 1.0)
    heat = HEAT_SCALE * TAYLOR_QUINNEY * (equivalent - drop) * rate
    updated = [pressure + scale * dev[k] for k in range(3)] + [
        scale * trial[k] for k in range(3, 6)
    ]
    return updated, heat


def six(gx, gp, gs):
    return [
        gx[0],
        gp[1],
        gs[2],
        0.5 * (gp[0] + gx[1]),
        0.5 * (gs[1] + gp[2]),
        0.5 * (gs[0] + gx[2]),
    ]


LAYERS = 14


def block_of(a):
    return 0 if a < 2 else 1 if a < 10 else 2


def layers(ext, shears, first, end):
    rows = PLANE
    row = iota((rows, LANES), 0)

    def read(field, j):
        return ext[pl.ds((field * LAYERS + j) * rows, rows), :]

    def node_terms(j):
        terms = []
        for c in range(VELS):
            here = read(c, j)
            above = jnp.where(row == rows - 1, 0.0, pltpu.roll(here, rows - 1, 0))
            total, change = here + above, above - here
            aside = pltpu.roll(total, LANES - 1, 1)
            terms.append((total + aside, aside - total, change + pltpu.roll(change, LANES - 1, 1)))
        return terms

    materials = [stress_terms(plane) for plane in shears]
    before = node_terms(first + 1)
    for a in range(first, end):
        after = node_terms(a + 2)
        grads = six(
            [after[c][0] - before[c][0] for c in range(VELS)],
            [after[c][2] + before[c][2] for c in range(VELS)],
            [after[c][1] + before[c][1] for c in range(VELS)],
        )
        material = materials[block_of(a)]
        trial = strained([read(VELS + k, a + 1) for k in range(6)], grads, material)
        yield (a, *returned(trial, read(9, a + 1), material))
        before = after


RIM_PAIRS = RING // 2
RIM_ROWS = RIM_PAIRS * BS


def rim_kernel(warmth, capacity, face, rim_out, twin_out):
    even = lax.rem(lax.axis_index("gz"), 2) == 0
    sub = iota((BS, LANES), 0)
    ups, downs = [], []
    for j in range(1, RING + 1):
        u = warmth_plane(j, warmth, face)
        c = capacity_plane(j, capacity, face)
        ups.append(jnp.where(sub > 4, u, pltpu.roll(c, 5, 0)))
        downs.append(jnp.where(sub < 3, u, pltpu.roll(c, 3, 0)))
    for m in range(RIM_PAIRS):
        at = pl.ds(m * BS, BS)
        up = jnp.where(sub < 4, pltpu.roll(ups[2 * m], 4, 0), ups[2 * m + 1])
        down = jnp.where(sub < 4, downs[2 * m], pltpu.roll(downs[2 * m + 1], 4, 0))
        rim_out[at, :] = jnp.where(even, down, up)
        twin_out[at, :] = jnp.where(even, up, down)


def heat_kernel(
    wide, shear, rim, rim_twin, face, columns, corner,
    chunks_out, even_out, odd_out, ext, shears_out, partial_out,
    stacked, chunks, sem,
):
    upper_x = lax.axis_index("gx") == 1
    upper_y = lax.axis_index("gy") == 1
    even = lax.rem(lax.axis_index("gz"), 2) == 0
    rows = PLANE
    half = LANES // 2
    lane = iota((rows, LANES), 1)
    first = jnp.where(upper_y, LANES - 3, half)
    beside = (lane >= first) & (lane < first + 3)
    faces = {key: at for at, key in enumerate(FACE)}

    def joined(field, plane, side):
        side = pltpu.roll(side, (half - SLOT * field) % LANES, 1)
        return jnp.where(lane < half, plane, jnp.where(beside, side, 0.0))

    def far(field, i, side):
        at = faces[field, i]
        pair = at // 2
        plane = jnp.concatenate([face[2 * pair], face[2 * pair + 1]], axis=0)
        return joined(field, pltpu.roll(plane, half, 1) if at % 2 else plane, side)

    def layer(field, j):
        if 3 <= j < 11:
            at = (field * BS + j - 3) * rows
            return joined(field, wide[pl.ds(at, rows), :], columns[j - 3])
        side = corner[j] if j < 3 else corner[j - 11]
        i = j - 11 if j >= 11 else j if field < VELS else j - 1
        plane = far(field, i, side)
        return jnp.where(upper_x, plane, 0.0) if j < 3 else jnp.where(upper_x, 0.0, plane)

    for field in range(10):
        for j in range(1, LAYERS if field < VELS else LAYERS - 1):
            ext[pl.ds((field * LAYERS + j) * rows, rows), :] = layer(field, j)
    outer = far(10, 0, corner[1])
    shears = [
        jnp.where(upper_x, outer, 0.0),
        joined(10, shear[...], columns[0]),
        jnp.where(upper_x, 0.0, outer),
    ]
    for block in range(3):
        shears_out[block] = shears[block]

    row = iota((rows, LANES), 0)

    def across(field, press):
        at = (field * LAYERS + 1) * rows + press
        return ext[pl.ds(at, rows, stride=rows), :]

    def parts(press, sign):
        terms = []
        for c in range(VELS):
            here = across(c, press)
            aside = pltpu.roll(here, LANES - 1, 1)
            total, change = here + aside, aside - here
            nxt = pltpu.roll(total, rows - 1, 0)
            both = nxt + total
            terms.append((nxt - total, sign * both, change + pltpu.roll(change, rows - 1, 0)))
        return six(*[[terms[c][d] for c in range(VELS)] for d in range(3)])

    last = rows - 1
    shear_row = [shears[block][last:, :] for block in range(3)]
    shear_mod = jnp.where(row < 2, shear_row[0], jnp.where(row < 10, shear_row[1], shear_row[2]))
    trial = strained(
        [across(VELS + k, last) for k in range(6)], parts(last, -1.0), stress_terms(shear_mod)
    )
    for q, plane in enumerate(trial + [across(9, last), shear_mod]):
        partial_out[q] = plane
    for k, plane in enumerate(parts(0, 1.0)):
        partial_out[8 + k] = plane

    sub = iota((BS, LANES), 0)
    for q in range(7):
        stacked[pl.ds(place(q), RING), :] = partial_out[q, pl.ds(0, RING), :]
    for c in range(VELS):
        stacked[pl.ds(NODES + (RING + 1) * c, RING + 1), :] = across(c, 0)[: RING + 1]

    for a, updated, heat in layers(ext, shears, 0, RING):
        shear_mod = shears[block_of(a)]
        stacked[pl.ds(a * rows, rows), :] = jnp.where(row == rows - 1, shear_mod, heat)
    turned = jnp.transpose(stacked[...])
    for g in range(chunks.shape[0]):
        here, after, before = (
            turned[at % LANES : at % LANES + BS, :] for at in (g * BS, g * BS + BS, g * BS - BS)
        )
        for t in range(2):
            chunks[g, pl.ds(t * BS, BS), :] = here[:, t * LANES : (t + 1) * LANES]
        sides = [
            jnp.where(
                sub < 4,
                after[:, t * LANES : (t + 1) * LANES],
                before[:, t * LANES : (t + 1) * LANES],
            )
            for t in range(3)
        ]
        inner = jnp.where(sub < 4, pltpu.roll(sides[1], 2, 0), pltpu.roll(sides[1], 6, 0))
        chunks[g, pl.ds(2 * BS, BS), :] = jnp.where((sub < 2) | (sub > 5), sides[0], inner)
        chunks[g, pl.ds(3 * BS, BS), :] = jnp.where(
            lane[:BS] < half, here[:, 2 * LANES :], pltpu.roll(sides[2], half, 1)
        )
    copy = pltpu.make_async_copy(chunks, chunks_out, sem)
    copy.start()

    def fill(up_ref, down_ref):
        for q in range(8):
            up_ref[pl.ds(RIM_ROWS + NEAR * q, NEAR), :] = partial_out[q, pl.ds(1, NEAR), :]
        for k in range(6):
            down_ref[pl.ds(RIM_ROWS + NEAR * k, NEAR), :] = partial_out[8 + k, pl.ds(1, NEAR), :]
        for ref, count in ((up_ref, 8), (down_ref, 6)):
            rest = EDGE_ALL - RIM_ROWS - NEAR * count
            ref[pl.ds(EDGE_ALL - rest, rest), :] = jnp.zeros((rest, LANES), jnp.float32)
        even_out[pl.ds(0, RIM_ROWS), :] = rim_twin[...]
        odd_out[pl.ds(0, RIM_ROWS), :] = rim[...]

    @pl.when(even)
    def _():
        fill(even_out, odd_out)

    @pl.when(jnp.logical_not(even))
    def _():
        fill(odd_out, even_out)

    copy.wait()


NEAR = BS + 1
EDGE_ALL = RIM_ROWS + 8 * NEAR + BS


def corrected(planes, sign):
    rows = PLANE
    total, change, press = [], [], []
    for plane in planes:
        aside = pltpu.roll(plane, 1, 1)
        total.append(plane + aside)
        change.append(plane - aside)
        press.append(sign * (plane + aside))
    forces = []
    for kx, kp, ks in FORCE_TERMS:
        both = press[kp] + change[ks]
        forces.append(
            total[kx] - pltpu.roll(total[kx], 1, 0) + both + pltpu.roll(both, 1, 0)
        )
    return forces


FORCE_TERMS = ((0, 3, 5), (3, 1, 4), (5, 4, 2))


def gather_kernel(chunks, heats_out):
    groups = lax.axis_size("gz")
    rows = PLANE
    lane = iota((rows, LANES), 1)
    group = lane // rows
    sub = iota((BS, LANES), 0)

    sources = [[], [], []]
    for g in range(groups):
        tiles = [chunks[g, pl.ds(t * BS, BS), :] for t in range(4)]
        inner = jnp.where(sub < 4, pltpu.roll(tiles[2], 6, 0), pltpu.roll(tiles[2], 2, 0))
        outer = pltpu.roll(tiles[3], LANES // 2, 1)
        for t, pair in enumerate(((tiles[0], tiles[2]), (tiles[1], inner), (tiles[3], outer))):
            sources[t].append(jnp.concatenate(pair, axis=0))

    heats = []
    for t, count in ((0, 8), (1, 4)):
        turned = []
        for k in range(groups):
            mixed = sources[t][k]
            for b in range(1, count):
                mixed = jnp.where(group == b, sources[t][(b + k) % groups], mixed)
            turned.append(pltpu.roll(mixed, k * rows, 1) if k else mixed)
        for b in range(count):
            heat = turned[(0 - b) % groups]
            for g in range(1, groups):
                heat = jnp.where(group == g, turned[(g - b) % groups], heat)
            heats.append(heat)

    def spread(position, width, first):
        tile, at = divmod(position, LANES)
        plane = jnp.zeros((rows, LANES), jnp.float32)
        for g in range(first, groups):
            to = (g - first) * rows
            inside = (lane >= to) & (lane < to + width)
            plane = jnp.where(inside, pltpu.roll(sources[tile][g], (to - at) % LANES, 1), plane)
        return plane

    place_in = lane % rows
    trial = [spread(place(k), RING, 0) for k in range(6)]
    yield_eff = spread(place(6), RING, 0)
    shear_mod = jnp.zeros((rows, LANES), jnp.float32)
    for a in range(RING):
        turned = pltpu.roll(heats[a], (a - rows + 1) % LANES, 1)
        shear_mod = jnp.where(place_in == a, turned, shear_mod)
    gx, gp, gs = [], [], []
    for c in range(VELS):
        here = spread(NODES + (RING + 1) * c, RING + 1, 1)
        aside = pltpu.roll(here, rows - 1, 0)
        total, change = here + aside, aside - here
        nxt = pltpu.roll(total, LANES - 1, 1)
        gx.append(nxt - total)
        gp.append(nxt + total)
        gs.append(change + pltpu.roll(change, LANES - 1, 1))
    terms = stress_terms(shear_mod)
    seam = returned(strained(trial, six(gx, gp, gs), terms), yield_eff, terms)[1]
    for a in range(RING):
        heats_out[a] = jnp.where(
            place_in == rows - 1, pltpu.roll(seam, rows - 1 - a, 1), heats[a]
        )


def force_kernel(ext, shears, vel, mass, stress_hbm, base_out, updated_out, low, sem):
    rows = PLANE
    row = iota((rows, LANES), 0)
    for a, updated, _ in layers(ext, [shears[block] for block in range(3)], 1, 10):
        for k in range(6):
            updated_out[k, a - 1] = updated[k]
            if a > 1:
                low[k, a - 2] = updated[k][:BS, : LANES // 2]
    copy = pltpu.make_async_copy(low, stress_hbm.at[:, :, pl.ds(0, BS), :], sem)
    copy.start()

    def element_terms(j):
        terms = []
        for k in range(6):
            here = jnp.where(row == rows - 1, 0.0, updated_out[k, j])
            prev = pltpu.roll(here, 1, 0)
            total, change = here + prev, here - prev
            aside = pltpu.roll(total, 1, 1)
            terms.append((total + aside, total - aside, change + pltpu.roll(change, 1, 1)))
        return terms

    before = element_terms(0)
    for x in range(BS):
        after = element_terms(x + 1)
        weights = 0.25 * TIME_STEP / mass[x]
        for c, (kx, kp, ks) in enumerate(FORCE_TERMS):
            force = (
                (after[kx][0] - before[kx][0])
                + (after[kp][2] + before[kp][2])
                + (after[ks][1] + before[ks][1])
            )
            base_out[c, x] = vel[c, x] + force[:, : LANES // 2] * weights
        before = after
    copy.wait()


def finish_kernel(
    heats, base, updated, partial, mass, warmth, capacity, face, odd_in, even_in, _,
    vel_hbm, stress_hbm, out_hbm,
    vel_out, stress_out, out, top, low_force, high_force, sems,
):
    upper_x = lax.axis_index("gx") == 1
    at_z = lax.axis_index("gz")
    even = lax.rem(at_z, 2) == 0
    groups = lax.axis_size("gz")
    rows = PLANE
    half = LANES // 2
    at_flat = lax.axis_index("gy") * groups + at_z
    last = lax.axis_size("gy") * groups - 1
    has_above = at_z < groups - 1
    has_below = at_z > 0
    lane = iota((rows, LANES), 1)
    row = iota((rows, LANES), 0)
    sub = iota((BS, LANES), 0)

    def below_plane(q):
        at = pl.ds(RIM_ROWS + NEAR * q - 1, rows)
        return jnp.where(has_below, jnp.where(even, odd_in[at, :], even_in[at, :]), 0.0)

    def above_plane(k):
        at = pl.ds(RIM_ROWS + NEAR * k - 1, rows)
        return jnp.where(has_above, jnp.where(even, even_in[at, :], odd_in[at, :]), 0.0)

    terms = stress_terms(partial[7])
    trial = strained([partial[k] for k in range(6)], [above_plane(k) for k in range(6)], terms)
    uppermost = returned(trial, partial[6], terms)[0]
    for k, plane in enumerate(uppermost):
        top[k] = plane
    copies = [
        pltpu.make_async_copy(*pair, sems.at[n])
        for n, pair in enumerate((
                (vel_out, vel_hbm),
                (stress_out, stress_hbm.at[:, :, pl.ds(BS, BS), :]),
                (out.at[pl.ds(0, BS // 2)], out_hbm.at[pl.ds(0, BS // 2)]),
                (out.at[pl.ds(BS // 2, BS // 2)], out_hbm.at[pl.ds(BS // 2, BS // 2)]),
            ))
    ]
    for x in range(BS):
        for k in range(6):
            plane = jnp.where(sub == BS - 1, top[k, pl.ds(x + 2, 1), :], updated[k, x + 1][BS:])
            stress_out[k, x] = plane[:, :half]
    copies[1].start()
    for c, plane in enumerate(corrected(uppermost, 1.0)):
        high_force[c] = plane
    terms = stress_terms(below_plane(7))
    trial = strained([below_plane(k) for k in range(6)], [partial[8 + k] for k in range(6)], terms)
    for c, plane in enumerate(corrected(returned(trial, below_plane(6), terms)[0], -1.0)):
        low_force[c] = plane
    for x in range(BS):
        at = pl.ds(x + 2, 1)
        weights = 0.25 * TIME_STEP / mass[x]
        for c in range(VELS):
            force = jnp.where(
                row == 0, low_force[c, at, :], jnp.where(row == rows - 1, high_force[c, at, :], 0.0)
            )
            vel_out[c, x] = base[c, x] + force[:, :half] * weights
    copies[0].start()

    above, below = at_flat < last, at_flat > 0
    u_rows = (row < BS) | ((row < BS + 3) & above) | ((row >= rows - 3) & below)
    d_rows = (row < BS) | ((row < BS + 2) & above) | ((row >= rows - 2) & below)
    us, caps = [], []
    for j in range(14):
        at = pl.ds(min(max(j - 1, 0), RING - 1) // 2 * BS, BS)
        low = jnp.where(even, odd_in[at, :], even_in[at, :])
        high = jnp.where(even, even_in[at, :], odd_in[at, :])
        if j % 2:
            low = pltpu.roll(low, 4, 0)
        else:
            high = pltpu.roll(high, 4, 0)
        side = jnp.where(sub < 4, high, low)
        u = jnp.concatenate([warmth_plane(j, warmth, face), side], axis=0)
        us.append(jnp.where(u_rows, u, 0.0))
        side = jnp.where(sub < 4, pltpu.roll(high, 5, 0), pltpu.roll(low, 3, 0))
        caps.append(6.0 + jnp.concatenate([capacity_plane(j, capacity, face), side], axis=0))

    def around(fields, a):
        here = fields[a]
        total = fields[a - 1] + fields[a + 1]
        total = total + pltpu.roll(here, 1, 0) + pltpu.roll(here, rows - 1, 0)
        total = total + jnp.where(lane == 0, 0.0, pltpu.roll(here, 1, 1))
        return total + jnp.where(lane == LANES - 1, 0.0, pltpu.roll(here, LANES - 1, 1))

    def inside(a):
        if a < 2:
            return d_rows & upper_x
        if a >= 10:
            return d_rows & jnp.logical_not(upper_x)
        return d_rows

    theta = 0.5 * (UPPER_BOUND + LOWER_BOUND)
    half_width = 0.5 * (UPPER_BOUND - LOWER_BOUND)
    sig = theta / half_width
    weight_now = 1.0 / sig
    misfit, step, total = {}, {}, {}
    for a in range(RING):
        misfit[a] = heats[a] - 6.0 * us[a + 1] + around(us, a + 1)
        step[a] = jnp.where(inside(a), misfit[a] * (1.0 / theta), 0.0)
        total[a] = us[a + 1] + step[a]
    for sweep in range(1, SWEEPS):
        weight_next = 1.0 / (2.0 * sig - weight_now)
        new_misfit, new_step = {}, {}
        for a in range(sweep, RING - sweep):
            new_misfit[a] = misfit[a] - caps[a + 1] * step[a] + around(step, a)
            moved = (weight_next * weight_now) * step[a] + (
                2.0 * weight_next / half_width
            ) * new_misfit[a]
            new_step[a] = jnp.where(inside(a), moved, 0.0)
            total[a] = total[a] + new_step[a]
        misfit, step, weight_now = new_misfit, new_step, weight_next
    for x in range(BS):
        out[x] = total[x + 2][:BS]
        if x == BS // 2 - 1:
            copies[2].start()
    copies[3].start()
    for copy in copies:
        copy.wait()


def f32(*shape):
    return jax.ShapeDtypeStruct(shape, jnp.float32)


def call(kernel, out_shape, *args, scratch=(), far_in=False, far_out=0, onto=None):
    moved = 4 * sum(a.size for a in args) + 4 * sum(o.size for o in jax.tree.leaves(out_shape))
    hbm, vmem = (pl.BlockSpec(memory_space=space) for space in (pltpu.HBM, pltpu.VMEM))
    return pl.pallas_call(
        kernel,
        out_shape=out_shape,
        in_specs=[hbm if far_in or n == onto else vmem for n in range(len(args))],
        input_output_aliases={} if onto is None else {onto: 1},
        out_specs=tuple(hbm if n < far_out else vmem for n in range(len(out_shape))),
        scratch_shapes=scratch,
        compiler_params=pltpu.CompilerParams(vmem_limit_bytes=VMEM_BYTES),
        cost_estimate=pl.CostEstimate(flops=0, bytes_accessed=moved, transcendentals=0),
    )(*args)


def room(*shape):
    return pltpu.VMEM(shape, jnp.float32)


def paired(count, first):
    pairs = []
    for i in range(first, count - 1, 2):
        pairs += [(i, i + 1), (i + 1, i)]
    return pairs


def two_round_body(
    corner_speed_prior,
    brick_stress_tensor_now,
    compact_onset_strength,
    corner_weights_diagonal,
    substance_labels,
    brick_warmth_prior,
    caloric_capacity_per_timestep,
):
    rows = PLANE
    groups = lax.axis_size("gz")
    chain = groups * lax.axis_size("gy")
    labels = jnp.transpose(substance_labels, (0, 2, 1))
    raw = (
        labels,
        corner_speed_prior,
        brick_stress_tensor_now,
        compact_onset_strength,
        brick_warmth_prior,
        caloric_capacity_per_timestep,
    )
    raw = [pltpu.with_memory_space_constraint(array, pltpu.HBM) for array in raw]
    second = compact_onset_strength.shape[-1]
    wide, shear, face, columns, corner, warmth, capacity = call(
        pack_kernel,
        (
            f32(10 * BS * rows, LANES),
            f32(rows, LANES),
            f32(FACE_TILES + 4, BS, LANES),
            f32(BS, rows, LANES),
            f32(3, rows, LANES),
            f32(*brick_warmth_prior.shape),
            f32(*brick_warmth_prior.shape),
        ),
        *raw,
        far_in=True,
        scratch=(
            room(10, BS, rows, second),
            pltpu.VMEM(labels.shape, jnp.int32),
            pltpu.SemaphoreType.DMA((len(raw) + 2,)),
        ),
    )
    face = lax.ppermute(face, "gx", [(0, 1), (1, 0)])
    columns = lax.ppermute(columns, "gy", [(0, 1), (1, 0)])
    corner = lax.ppermute(corner, ("gx", "gy"), [(0, 3), (3, 0), (1, 2), (2, 1)])
    rim, twin = call(
        rim_kernel, (f32(RIM_ROWS, LANES), f32(RIM_ROWS, LANES)), warmth, capacity, face
    )
    chunks, even, odd, ext, shears, partial = call(
        heat_kernel,
        (
            f32(groups, 4 * BS, LANES),
            f32(EDGE_ALL, LANES),
            f32(EDGE_ALL, LANES),
            f32((10 * LAYERS + 3) * rows, LANES),
            f32(3, rows, LANES),
            f32(PLANES, rows, LANES),
        ),
        wide,
        shear,
        rim,
        twin,
        face,
        columns,
        corner,
        scratch=(
            room(3 * LANES, LANES),
            room(groups, 4 * BS, LANES),
            pltpu.SemaphoreType.DMA,
        ),
        far_out=1,
    )
    chunks = lax.all_to_all(chunks, "gz", split_axis=0, concat_axis=0, tiled=True)
    odd = lax.ppermute(odd, ("gy", "gz"), paired(chain, 1))
    even = lax.ppermute(even, "gz", paired(groups, 0))
    stress, base, updated = call(
        force_kernel,
        (f32(*brick_stress_tensor_now.shape), f32(*corner_speed_prior.shape), f32(6, BS + 1, rows, LANES)),
        ext,
        shears,
        corner_speed_prior,
        corner_weights_diagonal,
        scratch=(room(6, BS, BS, second), pltpu.SemaphoreType.DMA),
        far_out=1,
    )
    (heats,) = call(gather_kernel, (f32(RING, rows, LANES),), chunks)
    odd, even, heats, base = lax.optimization_barrier((odd, even, heats, base))
    results = (corner_speed_prior.shape, brick_stress_tensor_now.shape, brick_warmth_prior.shape)
    return call(
        finish_kernel,
        tuple(f32(*shape) for shape in results),
        heats,
        base,
        updated,
        partial,
        corner_weights_diagonal,
        warmth,
        capacity,
        face,
        odd,
        even,
        stress,
        onto=10,
        scratch=(
            room(*results[0]),
            room(6, BS, BS, second),
            room(*results[2]),
            room(6, rows, LANES),
            room(VELS, rows, LANES),
            room(VELS, rows, LANES),
            pltpu.SemaphoreType.DMA((4,)),
        ),
        far_out=3,
    )


def solution(mesh):
    placed = (
        P(None, "gx", "gz", "gy"),
        P(None, "gx", "gz", "gy"),
        P("gx", "gz", "gy"),
        P("gx", "gz", "gy"),
        P("gx", None, "gy"),
        P("gx", ("gy", "gz"), None),
        P("gx", ("gy", "gz"), None),
    )
    return jax.shard_map(
        by_shape if two_rounds_fit(mesh) else body,
        mesh=mesh,
        in_specs=placed,
        out_specs=(
            P(None, "gx", "gz", "gy"),
            P(None, "gx", "gz", "gy"),
            P("gx", ("gy", "gz"), None),
        ),
        check_vma=False,
    )
```
